512 devices in a mesh: outer: 16 (over x_lo, z), inner: 32 (over y, x_hi, core).
Axes of the slice: x: 4 (x_hi: 2, x_lo: 2; x = x_hi * 2 + x_lo), y: 8, z: 8, core: 2. Of those that a mesh axis runs over, the one named last changes fastest.
Arguments:
- query_rot: bfloat16 [16, 4096, 896], P('outer', 'inner'), may hold values from -6 to 6
- key_rot: bfloat16 [16, 4096, 128], P('outer', 'inner'), may hold values from -6 to 6
- value_rows: bfloat16 [16, 4096, 128], P('outer', 'inner'), may hold values from -6 to 6
- attention_out: bfloat16 [16, 4096, 896], P('outer', 'inner'), may hold values from -6 to 6
- grad_out: bfloat16 [16, 4096, 896], P('outer', 'inner'), may hold values from -12 to 12
- log_norm: float32 [16, 7, 4096], P('outer', None, 'inner'), may hold values from 7.5 to 9
- segments: int32 [4, 4096], P(None, 'inner'), may hold values from 0 to 2, as said below
- block_table: int32 [4, 32, 32], P(None, 'inner'), may hold values from 0 to 1, as said below
Outputs:
- grad_query: bfloat16 [16, 4096, 896], P('outer', 'inner')
- grad_key: bfloat16 [16, 4096, 128], P('outer', 'inner')
- grad_value: bfloat16 [16, 4096, 128], P('outer', 'inner')
- grad_bias: float32 [4608], replicated
The draws below stay inside these ranges and needn't reach their ends.
Inputs may be any that keep to these rules, and one draw needn't show every extreme that they name: `segments`: in every example the tokens of segment 0 come first, then those of segment 1, then those of segment 2; each segment is present. block_table[e,a,b] is 1 exactly when some token of block a (tokens a * 128 to a * 128 + 127) and some token of block b of example e have segments s_q and s_k with s_k == 0 or s_k == s_q, else 0.
All inputs are finite; a program needn't handle non-finite values.
Results may differ from the reference program's by a relative error of at most 0.0056.
Values may be sent and summed in bfloat16 or wider, within the bound.
No kernel may reach another device: no remote copies, remote signals or barrier semaphores. Data moves between devices by JAX's collectives and lax.ppermute only.
A program may use at most 64 MiB of HBM per device.

```python
import math
import jax
import jax.numpy as jnp
from jax import lax

TOK_DEV = 128
HEADS = 28
KV_HEADS = 4
HEAD_DIM = 128
GROUP = 7
SEQ = 4096
BLOCKS = 32
PAIRS = 16
EXAMPLES = 4


def layout_helper(key):
    base = jax.random.fold_in(key, 7)
    example_keys = jax.random.split(base, EXAMPLES)

    def one_layout(example_key):
        first_key, second_key = jax.random.split(example_key)
        shortest = SEQ // 16
        longest = SEQ // 4 + 1
        chosen = jax.random.randint(first_key, (), shortest, longest)
        rejected = jax.random.randint(second_key, (), shortest, longest)
        positions = jnp.arange(SEQ)
        prompt = SEQ - chosen - rejected
        return jnp.where(positions < prompt, 0, jnp.where(positions < prompt + chosen, 1, 2)).astype(jnp.int32)
    return jax.vmap(one_layout)(example_keys)


def draw_segments(key, part):
    return layout_helper(key)


def draw_block_table(key, part):
    layout = layout_helper(key).reshape(EXAMPLES, BLOCKS, TOK_DEV)
    present = jnp.stack([jnp.any(layout == 0, axis=-1), jnp.any(layout == 1, axis=-1), jnp.any(layout == 2, axis=-1)], axis=-1)
    query_side = present[:, :, None, :]
    key_side = present[:, None, :, :]
    any_query = jnp.any(query_side, axis=-1)
    allowed = key_side[..., 0] & any_query | query_side[..., 1] & key_side[..., 1] | query_side[..., 2] & key_side[..., 2]
    return allowed.astype(jnp.int32)


def block_scale(stream_key, extent, cuts, smallest, high):
    def one(axis_at, shards_of):
        steps = jax.random.uniform(jax.random.fold_in(jax.random.fold_in(stream_key, 6), axis_at), (shards_of,), jnp.float32, smallest / len(cuts), high / len(cuts))
        return jnp.repeat(jnp.exp(steps), extent[axis_at] // shards_of).reshape((-1,) + (1,) * (len(extent) - axis_at - 1))

    level = one(*cuts[0])
    for cut in cuts[1:]:
        level = level * one(*cut)
    return level


def scatter_about(stream_key, shape, spread, limit, cuts=(), held_as=jnp.bfloat16):
    drawn = jax.random.normal(stream_key, shape, jnp.float32) * spread
    if len(cuts) > 0:
        drawn = block_scale(stream_key, shape, cuts, -0.22, 0.18) * drawn
    return jnp.clip(drawn, min=-limit, max=limit).astype(held_as)


def setup_inputs(seed: int = 0) -> dict:
    arg_keys = jax.random.split(jax.random.key(seed), 9)
    query_rot = scatter_about(arg_keys[0], (PAIRS, SEQ, GROUP * HEAD_DIM), 1.0, 6.0, ((0, 16), (1, 32)))
    key_rot = scatter_about(arg_keys[1], (PAIRS, SEQ, HEAD_DIM), 1.0, 6.0, ((0, 16), (1, 32)))
    value_rows = scatter_about(arg_keys[2], (PAIRS, SEQ, HEAD_DIM), 1.0, 6.0, ((0, 16), (1, 32)))
    attention_out = scatter_about(arg_keys[3], (PAIRS, SEQ, GROUP * HEAD_DIM), 1.0, 6.0, ((0, 16), (1, 32)))
    grad_out = jnp.clip(jax.random.uniform(arg_keys[4], (PAIRS, SEQ, GROUP * HEAD_DIM), jnp.float32, -12.0, 12.0) * block_scale(arg_keys[4], (PAIRS, SEQ, GROUP * HEAD_DIM), ((0, 16), (1, 32)), -0.4, 0.0), -12.0, 12.0).astype(jnp.bfloat16)
    log_norm = jnp.clip(7.5 + 1.5 * jax.random.uniform(arg_keys[5], (PAIRS, GROUP, SEQ), jnp.float32) ** block_scale(arg_keys[5], (PAIRS, GROUP, SEQ), ((0, 16), (2, 32)), -0.2, 0.2), 7.5, 9.0)
    segments = draw_segments(jax.random.fold_in(arg_keys[8], 71), 0)
    block_table = draw_block_table(jax.random.fold_in(arg_keys[8], 71), 0)
    return {"query_rot": query_rot, "key_rot": key_rot, "value_rows": value_rows, "attention_out": attention_out, "grad_out": grad_out, "log_norm": log_norm, "segments": segments, "block_table": block_table}


ROPE_BASE = 1000000.0


def unrotate(gradient, positions, heads):
    rows_here = gradient.shape[0]
    halfway = HEAD_DIM // 2
    per_head = gradient.reshape(rows_here, heads, HEAD_DIM)
    frequency = jnp.exp(jnp.arange(halfway, dtype=jnp.float32) * (-2.0 * math.log(ROPE_BASE) / HEAD_DIM))
    angles = positions[:, None] * frequency[None, :]
    cosine = jnp.cos(angles)[:, None, :]
    sine_term = jnp.sin(angles)[:, None, :]
    first_half = per_head[..., :halfway]
    second_half = per_head[..., halfway:]
    joined = jnp.concatenate([first_half * cosine + second_half * sine_term, second_half * cosine - first_half * sine_term], axis=-1)
    return joined.reshape(rows_here, heads * HEAD_DIM)


def one_pair(inputs):
    query_rot, key_rot, value_rows, attention_out, grad_out, log_norm, segments, block_table = inputs
    group_size = HEADS // KV_HEADS
    scaling = HEAD_DIM ** -0.5
    highest = lax.Precision.HIGHEST
    queries = query_rot.astype(jnp.float32).reshape(SEQ, group_size, HEAD_DIM)
    grads_out = grad_out.astype(jnp.float32).reshape(SEQ, group_size, HEAD_DIM)
    outputs = attention_out.astype(jnp.float32).reshape(SEQ, group_size, HEAD_DIM)
    keys_all = key_rot.astype(jnp.float32)
    values_all = value_rows.astype(jnp.float32)
    deltas = jnp.transpose(jnp.sum(grads_out * outputs, axis=-1), (1, 0))

    def one_block(carry, block_index):
        key_grads, value_grads = carry
        start = (block_index * TOK_DEV).astype(jnp.int32)
        block_queries = lax.dynamic_slice_in_dim(queries, start, TOK_DEV, 0)
        block_grads = lax.dynamic_slice_in_dim(grads_out, start, TOK_DEV, 0)
        seg_query = lax.dynamic_slice_in_dim(segments, start, TOK_DEV, 0)
        block_norms = lax.dynamic_slice_in_dim(log_norm, start, TOK_DEV, 1)
        block_deltas = lax.dynamic_slice_in_dim(deltas, start, TOK_DEV, 1)
        table_row = jnp.repeat(lax.dynamic_index_in_dim(block_table, block_index.astype(jnp.int32), 0, keepdims=False), TOK_DEV)
        allowed = (table_row[None, :] == 1) & ((segments[None, :] == 0) | (segments[None, :] == seg_query[:, None]))
        scores = jnp.einsum("tgd,ud->gtu", block_queries, keys_all, precision=highest) * scaling
        probs = jnp.where(allowed[None], jnp.exp(scores - block_norms[..., None]), 0.0)
        probs_low = lax.optimization_barrier(probs.astype(jnp.bfloat16)).astype(jnp.float32)
        grad_probs = jnp.einsum("tgd,ud->gtu", block_grads, values_all, precision=highest)
        grad_scores = probs * (grad_probs - block_deltas[..., None])
        scores_low = lax.optimization_barrier(grad_scores.astype(jnp.bfloat16)).astype(jnp.float32)
        value_grads = value_grads + jnp.einsum("gtu,tgd->ud", probs_low, block_grads, precision=highest)
        key_grads = key_grads + jnp.einsum("gtu,tgd->ud", scores_low, block_queries, precision=highest)
        query_part = jnp.einsum("gtu,ud->tgd", scores_low, keys_all, precision=highest)
        return (key_grads, value_grads), query_part

    empty = jnp.zeros((SEQ, HEAD_DIM), jnp.float32)
    (key_grads, value_grads), query_blocks = lax.scan(one_block, (empty, empty), jnp.arange(BLOCKS, dtype=jnp.int32))
    positions = jnp.arange(SEQ, dtype=jnp.float32)
    query_full = unrotate(query_blocks.reshape(SEQ, group_size * HEAD_DIM) * scaling, positions, group_size)
    key_full = unrotate(key_grads * scaling, positions, 1)
    value_full = value_grads
    return (query_full.astype(jnp.bfloat16), key_full.astype(jnp.bfloat16), value_full.astype(jnp.bfloat16), jnp.sum(query_full, axis=0), jnp.sum(key_full, axis=0), jnp.sum(value_full, axis=0))


def reference(query_rot, key_rot, value_rows, attention_out, grad_out, log_norm, segments, block_table):
    seg_pairs = jnp.repeat(segments, KV_HEADS, axis=0)
    table_pairs = jnp.repeat(block_table, KV_HEADS, axis=0)
    results = lax.map(one_pair, (query_rot, key_rot, value_rows, attention_out, grad_out, log_norm, seg_pairs, table_pairs))
    query_bias = jnp.sum(results[3].reshape(EXAMPLES, HEADS * HEAD_DIM), axis=0)
    key_bias = jnp.sum(results[4].reshape(EXAMPLES, KV_HEADS * HEAD_DIM), axis=0)
    value_bias = jnp.sum(results[5].reshape(EXAMPLES, KV_HEADS * HEAD_DIM), axis=0)
    return (results[0], results[1], results[2], jnp.concatenate([query_bias, key_bias, value_bias]))
```

```python
import math

import jax
import jax.numpy as jnp
from jax import lax
from jax.experimental import pallas as pl
from jax.experimental.pallas import tpu as pltpu
from jax.sharding import PartitionSpec as P

HEADS = 28
KV_HEADS = 4
HEAD_DIM = 128
GROUP = HEADS // KV_HEADS
SEQ = 4096
ROPE_BASE = 1000000.0
HALF = HEAD_DIM // 2
SCALE = HEAD_DIM ** (-0.5)
LOG2E = math.log2(math.e)
META = 16
BPC = 2
ROWS = HEADS + 2 * KV_HEADS


def frequencies():
    return jnp.exp(jnp.arange(HALF, dtype=jnp.float32) * (-2.0 * math.log(ROPE_BASE) / HEAD_DIM))


def attention_kernel(
    head_ref, meta_ref, kv_ref, q_ref, go_ref, ao_ref, norm_ref, seg_ref,
    cosq_ref, sinq_ref, cosr_ref, sinr_ref, cosc_ref, sinc_ref,
    dkv_ref, dq_ref, bias_ref,
    q_rows, go_rows, q_cols, go_cols, delta, norm2, low, high, dq_acc, sums, bounds,
):
    step = pl.program_id(0)
    steps = pl.num_programs(0)
    tokens = q_ref.shape[0]
    chunk = BPC * tokens
    start = step * chunk
    f32 = jnp.float32

    @pl.when(step == 0)
    def _():
        meta = jnp.sum(meta_ref[...].astype(f32), axis=0)
        row = lax.broadcasted_iota(jnp.int32, meta.shape, 0)
        first = jnp.sum(jnp.where(row == 0, meta, 0.0)).astype(jnp.int32)
        second = jnp.sum(jnp.where(row == 1, meta, 0.0)).astype(jnp.int32)
        seg = seg_ref[...]
        bounds[0] = first
        bounds[1] = second
        bounds[2] = jnp.min(seg)
        bounds[3] = jnp.max(seg)
        bounds[4] = jnp.max(jnp.where(seg == 1, 1, 0))
        lo = jnp.where(seg == 1, first, jnp.where(seg == 2, second, 0))
        hi = jnp.where(seg == 1, second, jnp.where(seg == 2, SEQ, 0))
        for g in range(GROUP):
            here = slice(g * HEAD_DIM, (g + 1) * HEAD_DIM)
            there = slice(g * tokens, (g + 1) * tokens)
            q = q_ref[:, here]
            go = go_ref[:, here]
            q_rows[there, :] = q
            go_rows[there, :] = go
            q_cols[:, there] = q.T
            go_cols[:, there] = go.T
            product = go.astype(f32) * ao_ref[:, here].astype(f32)
            delta[:, there] = jnp.sum(product.T, axis=0, keepdims=True)
            norm2[:, there] = norm_ref[g : g + 1, :] * LOG2E
            low[:, there] = lo
            high[:, there] = hi
        dq_acc[...] = jnp.zeros_like(dq_acc)
        sums[...] = jnp.zeros_like(sums)

    first = bounds[0]
    second = bounds[1]
    end = start + chunk
    has1 = bounds[4] > 0
    has2 = bounds[3] == 2
    whole = (
        (end <= first)
        | ((bounds[2] == 1) & (bounds[3] == 1) & (start >= first) & (end <= second))
        | ((bounds[2] == 2) & (start >= second))
    )
    some = (start < first) | (has1 & (end > first) & (start < second)) | (has2 & (end > second))

    def compute(masked):
        keys = kv_ref[:, :tokens, :HEAD_DIM].reshape(chunk, HEAD_DIM)
        values = kv_ref[:, :tokens, HEAD_DIM:].reshape(chunk, HEAD_DIM)
        scores = jnp.dot(keys, q_cols[...], preferred_element_type=f32)
        probs = jnp.exp2(scores * (SCALE * LOG2E) - norm2[...])
        if masked:
            at = start + lax.broadcasted_iota(jnp.int32, probs.shape, 0)
            probs = jnp.where((at < first) | ((at >= low[...]) & (at < high[...])), probs, 0.0)
        grad_probs = jnp.dot(values, go_cols[...], preferred_element_type=f32)
        scores_low = (probs * (grad_probs - delta[...])).astype(jnp.bfloat16)
        dv = jnp.dot(probs.astype(jnp.bfloat16), go_rows[...], preferred_element_type=f32)
        dk = jnp.dot(scores_low, q_rows[...], preferred_element_type=f32)
        dq_acc[...] += jnp.dot(keys.T, scores_low, preferred_element_type=f32)
        dkv_ref[:, :HEAD_DIM] = dk
        dkv_ref[:, HEAD_DIM:] = dv
        u = jnp.sum(dk * cosr_ref[...], axis=0, keepdims=True)
        w = jnp.sum(dk * sinr_ref[...], axis=0, keepdims=True)
        c = cosc_ref[pl.ds(step, 1), :]
        s = sinc_ref[pl.ds(step, 1), :]
        sums[0:1, :] += u * c - w * s
        sums[1:2, :] += u * s + w * c
        sums[2:3, :] += jnp.sum(dv, axis=0, keepdims=True)

    @pl.when(whole)
    def _():
        compute(False)

    @pl.when(some & jnp.logical_not(whole))
    def _():
        compute(True)

    @pl.when(jnp.logical_not(some))
    def _():
        dkv_ref[...] = jnp.zeros_like(dkv_ref)

    @pl.when(step == steps - 1)
    def _():
        head = head_ref[0]
        bias_ref[...] = jnp.zeros_like(bias_ref)
        cosine = cosq_ref[...]
        sine = sinq_ref[...]
        for g in range(GROUP):
            there = slice(g * tokens, (g + 1) * tokens)
            a = dq_acc[:HALF, there] * SCALE
            b = dq_acc[HALF:, there] * SCALE
            turned = jnp.concatenate([a * cosine + b * sine, b * cosine - a * sine], axis=0).T
            dq_ref[:, g * HEAD_DIM : (g + 1) * HEAD_DIM] = turned.astype(jnp.bfloat16)
            bias_ref[pl.ds(head * GROUP + g, 1), :] = jnp.sum(turned, axis=0, keepdims=True)
        u = sums[0:1, :] * SCALE
        w = sums[1:2, :] * SCALE
        swapped = jnp.concatenate([w[:, HALF:], -w[:, :HALF]], axis=1)
        bias_ref[pl.ds(HEADS + head, 1), :] = u + swapped
        bias_ref[pl.ds(HEADS + KV_HEADS + head, 1), :] = sums[2:3, :]


def local(query_rot, key_rot, value_rows, attention_out, grad_out, log_norm, segments, block_table):
    tokens = query_rot.shape[1]
    members = lax.axis_size("inner")
    mine = lax.axis_index("inner")
    outer = lax.axis_index("outer")
    example = outer // KV_HEADS
    head = outer % KV_HEADS
    seg = lax.dynamic_index_in_dim(segments, example, 0, keepdims=True)
    prompt = jnp.sum((seg == 0).astype(jnp.float32))
    chosen = jnp.sum((seg <= 1).astype(jnp.float32))
    row = lax.broadcasted_iota(jnp.int32, (META, 2 * HEAD_DIM), 0)
    lane = lax.broadcasted_iota(jnp.int32, (META, 2 * HEAD_DIM), 1)
    meta = jnp.where(row == 0, prompt, jnp.where(row == 1, chosen, 0.0))
    meta = jnp.where(lane == 0, meta, 0.0).astype(jnp.bfloat16)
    packed = jnp.concatenate(
        [jnp.concatenate([key_rot[0], value_rows[0]], axis=1), meta], axis=0
    )
    everything = lax.all_gather(packed, "inner", axis=0, tiled=False)

    frequency = frequencies()
    positions = (mine * tokens + jnp.arange(tokens, dtype=jnp.int32)).astype(jnp.float32)
    angles = frequency[:, None] * positions[None, :]
    cosq, sinq = jnp.cos(angles), jnp.sin(angles)
    chunk = BPC * tokens
    steps = members // BPC
    doubled = jnp.concatenate([frequency, frequency])[None, :]
    inside = jnp.arange(chunk, dtype=jnp.float32)[:, None] * doubled
    across = (jnp.arange(steps, dtype=jnp.float32) * chunk)[:, None] * doubled

    width = GROUP * HEAD_DIM
    lanes = GROUP * tokens
    whole = lambda *shape: pl.BlockSpec(shape, lambda i: (0,) * len(shape))
    dkv, dq, bias = pl.pallas_call(
        attention_kernel,
        grid=(steps,),
        in_specs=[
            pl.BlockSpec(memory_space=pltpu.SMEM),
            pl.BlockSpec((members, META, 2 * HEAD_DIM), lambda i: (0, tokens // META, 0)),
            pl.BlockSpec((BPC, tokens + META, 2 * HEAD_DIM), lambda i: (i, 0, 0)),
            whole(tokens, width),
            whole(tokens, width),
            whole(tokens, width),
            whole(GROUP, tokens),
            whole(1, tokens),
            whole(HALF, tokens),
            whole(HALF, tokens),
            whole(chunk, HEAD_DIM),
            whole(chunk, HEAD_DIM),
            whole(steps, HEAD_DIM),
            whole(steps, HEAD_DIM),
        ],
        out_specs=[
            pl.BlockSpec((chunk, 2 * HEAD_DIM), lambda i: (i, 0)),
            whole(tokens, width),
            whole(ROWS, HEAD_DIM),
        ],
        out_shape=[
            jax.ShapeDtypeStruct((members * tokens, 2 * HEAD_DIM), jnp.float32),
            jax.ShapeDtypeStruct((tokens, width), jnp.bfloat16),
            jax.ShapeDtypeStruct((ROWS, HEAD_DIM), jnp.float32),
        ],
        scratch_shapes=[
            pltpu.VMEM((lanes, HEAD_DIM), jnp.bfloat16),
            pltpu.VMEM((lanes, HEAD_DIM), jnp.bfloat16),
            pltpu.VMEM((HEAD_DIM, lanes), jnp.bfloat16),
            pltpu.VMEM((HEAD_DIM, lanes), jnp.bfloat16),
            pltpu.VMEM((1, lanes), jnp.float32),
            pltpu.VMEM((1, lanes), jnp.float32),
            pltpu.VMEM((1, lanes), jnp.int32),
            pltpu.VMEM((1, lanes), jnp.int32),
            pltpu.VMEM((HEAD_DIM, lanes), jnp.float32),
            pltpu.VMEM((8, HEAD_DIM), jnp.float32),
            pltpu.SMEM((8,), jnp.int32),
        ],
        compiler_params=pltpu.CompilerParams(vmem_limit_bytes=40 << 20),
    )(
        head[None].astype(jnp.int32), everything, everything, query_rot[0], grad_out[0],
        attention_out[0], log_norm[0], seg, cosq, sinq,
        jnp.cos(inside), jnp.sin(inside), jnp.cos(across), jnp.sin(across),
    )

    home = lax.psum_scatter(dkv, "inner", scatter_dimension=0, tiled=True)
    grad_bias = lax.psum(bias, ("outer", "inner")).reshape(-1)
    key_sum = home[:, :HEAD_DIM] * SCALE
    value_sum = home[:, HEAD_DIM:]
    cosk, sink = cosq.T, sinq.T
    a, b = key_sum[:, :HALF], key_sum[:, HALF:]
    key_full = jnp.concatenate([a * cosk + b * sink, b * cosk - a * sink], axis=1)
    return (
        dq[None],
        key_full.astype(jnp.bfloat16)[None],
        value_sum.astype(jnp.bfloat16)[None],
        grad_bias,
    )


def solution(mesh):
    placed = (
        P("outer", "inner", None),
        P("outer", "inner", None),
        P("outer", "inner", None),
        P("outer", "inner", None),
        P("outer", "inner", None),
        P("outer", None, "inner"),
        P(None, "inner"),
        P(None, "inner", None),
    )
    return jax.shard_map(
        local,
        mesh=mesh,
        in_specs=placed,
        out_specs=(
            P("outer", "inner", None),
            P("outer", "inner", None),
            P("outer", "inner", None),
            P(),
        ),
        check_vma=False,
    )
```

```python
import math

import jax
import jax.numpy as jnp
from jax import lax
from jax.experimental import pallas as pl
from jax.experimental.pallas import tpu as pltpu
from jax.sharding import Mesh, PartitionSpec as P

HEADS = 28
KV_HEADS = 4
HEAD_DIM = 128
GROUP = HEADS // KV_HEADS
TOK = 128
ROPE_BASE = 1000000.0
HALF = HEAD_DIM // 2
SCALE = HEAD_DIM ** (-0.5)
LOG2E = math.log2(math.e)

RINGS = 8
NEAR = 4
BPC = 2
META = 16
LANES = GROUP * TOK
WIDTH = GROUP * HEAD_DIM
PACK = 2 * LANES + 48
BIAS_ROWS = GROUP + 2

F32 = jnp.float32
BF16 = jnp.bfloat16


def split(value, terms):
    parts = []
    for _ in range(terms):
        part = value.astype(BF16)
        parts.append(part)
        value = value - part.astype(F32)
    return parts


def pack_kernel(q_ref, go_ref, ao_ref, norm_ref, seg_ref, k_ref, v_ref, pack_ref, kv_ref):
    seg = seg_ref[...]
    deltas = []
    for g in range(GROUP):
        here = slice(g * HEAD_DIM, (g + 1) * HEAD_DIM)
        go = go_ref[:, here]
        pack_ref[g * TOK : (g + 1) * TOK, :] = q_ref[:, here]
        pack_ref[LANES + g * TOK : LANES + (g + 1) * TOK, :] = go
        product = go.astype(F32) * ao_ref[:, here].astype(F32)
        deltas.append(jnp.sum(product.T, axis=0, keepdims=True))
    zero = jnp.zeros((1, TOK), F32)
    eight = lambda rows: jnp.concatenate(rows + [zero] * (8 - len(rows)), axis=0)
    norms = norm_ref[...] * LOG2E
    parts = split(eight([norms[g : g + 1, :] for g in range(GROUP)] + [seg.astype(F32)]), 3)
    parts += split(eight(deltas), 3)
    rows = jnp.concatenate([part.astype(F32) for part in parts], axis=0)
    pack_ref[2 * LANES :, :] = rows.astype(BF16)

    row = lax.broadcasted_iota(jnp.int32, (META, 2 * HEAD_DIM), 0)
    prompt = jnp.sum(jnp.where(seg == 0, 1.0, 0.0))
    chosen = jnp.sum(jnp.where(seg <= 1, 1.0, 0.0))
    meta = jnp.where(row == 0, prompt, jnp.where(row == 1, chosen, 0.0)).astype(BF16)
    keys = k_ref[...]
    values = v_ref[...]
    for y in range(RINGS):
        kv_ref[y, :TOK, :HEAD_DIM] = keys
        kv_ref[y, :TOK, HEAD_DIM:] = values
        kv_ref[y, TOK:, :] = meta


def attention_kernel(
    meta_ref, kv_ref, pack0, pack1, pack2, pack3, cosq_ref, sinq_ref, cosr_ref, sinr_ref, cosc_ref, sinc_ref,
    dkv_ref, dq0, dq1, dq2, dq3,
    q_rows, go_rows, q_cols, go_cols, delta, norm2, seg_q, dq_acc, kv_acc, turned_sum, sums, kinds, counts,
):
    kp = pl.program_id(0)
    qi = pl.program_id(1)
    last = pl.num_programs(0) - 1
    chunk = BPC * TOK

    @pl.when((kp == 0) & (qi == 0))
    def _():
        for y in range(RINGS):
            meta = meta_ref[y].astype(F32)
            counts[0, y] = jnp.max(meta[0:1, :]).astype(jnp.int32)
            counts[1, y] = jnp.max(meta[1:2, :]).astype(jnp.int32)
        dq_acc[...] = jnp.zeros_like(dq_acc)
        turned_sum[...] = jnp.zeros_like(turned_sum)
        sums[...] = jnp.zeros_like(sums)

    for c, pack in enumerate((pack0, pack1, pack2, pack3)):

        @pl.when((kp == 0) & (qi == c))
        def _(c=c, pack=pack):
            extra = pack[2 * LANES :, :].astype(F32)
            norms = extra[0:8] + extra[8:16] + extra[16:24]
            deltas = extra[24:32] + extra[32:40] + extra[40:48]
            seg = norms[GROUP : GROUP + 1, :].astype(jnp.int32)
            kinds[0, c] = jnp.min(seg)
            kinds[1, c] = jnp.max(seg)
            kinds[2, c] = jnp.max(jnp.where(seg == 1, 1, 0))
            q_rows[c] = pack[:LANES, :]
            go_rows[c] = pack[LANES : 2 * LANES, :]
            for g in range(GROUP):
                there = slice(g * TOK, (g + 1) * TOK)
                q_cols[c, :, there] = pack[g * TOK : (g + 1) * TOK, :].T
                go_cols[c, :, there] = pack[LANES + g * TOK : LANES + (g + 1) * TOK, :].T
                delta[c, :, there] = deltas[g : g + 1, :]
                norm2[c, :, there] = norms[g : g + 1, :]
                seg_q[c, :, there] = seg

    @pl.when(qi == 0)
    def _():
        kv_acc[...] = jnp.zeros_like(kv_acc)

    least, most, has1 = kinds[0, qi], kinds[1, qi], kinds[2, qi] > 0
    whole = True
    some = False
    for b in range(BPC):
        c0, c1 = counts[0, kp * BPC + b], counts[1, kp * BPC + b]
        entire = (
            (c0 == TOK)
            | ((least == 1) & (most == 1) & (c0 == 0) & (c1 == TOK))
            | ((least == 2) & (c1 == 0))
        )
        part = (c0 > 0) | (has1 & (c1 > c0)) | ((most == 2) & (c1 < TOK))
        whole = entire & whole
        some = part | some

    def compute(masked):
        keys = kv_ref[:, :TOK, :HEAD_DIM].reshape(chunk, HEAD_DIM)
        values = kv_ref[:, :TOK, HEAD_DIM:].reshape(chunk, HEAD_DIM)
        scores = jnp.dot(keys, q_cols[qi], preferred_element_type=F32)
        probs = jnp.exp2(scores * (SCALE * LOG2E) - norm2[qi])
        if masked:
            at = lax.broadcasted_iota(jnp.int32, (TOK, LANES), 0)
            seg = seg_q[qi]
            pieces = []
            for b in range(BPC):
                c0, c1 = counts[0, kp * BPC + b], counts[1, kp * BPC + b]
                low = jnp.where(seg == 1, c0, jnp.where(seg == 2, c1, 0))
                high = jnp.where(seg == 1, c1, jnp.where(seg == 2, TOK, 0))
                allowed = (at < c0) | ((at >= low) & (at < high))
                pieces.append(jnp.where(allowed, probs[b * TOK : (b + 1) * TOK, :], 0.0))
            probs = jnp.concatenate(pieces, axis=0)
        grad_probs = jnp.dot(values, go_cols[qi], preferred_element_type=F32)
        scores_low = (probs * (grad_probs - delta[qi])).astype(BF16)
        dv = jnp.dot(probs.astype(BF16), go_rows[qi], preferred_element_type=F32)
        dk = jnp.dot(scores_low, q_rows[qi], preferred_element_type=F32)
        dq_acc[qi] += jnp.dot(keys.T, scores_low, preferred_element_type=F32)
        kv_acc[:, :HEAD_DIM] += dk
        kv_acc[:, HEAD_DIM:] += dv

    @pl.when(whole)
    def _():
        compute(False)

    @pl.when(some & jnp.logical_not(whole))
    def _():
        compute(True)

    @pl.when(qi == NEAR - 1)
    def _():
        total = kv_acc[...]
        low = total.astype(BF16)
        for b in range(BPC):
            dkv_ref[kp * BPC + b, :TOK, :] = low[b * TOK : (b + 1) * TOK, :]
            dk = total[b * TOK : (b + 1) * TOK, :HEAD_DIM]
            u = jnp.sum(dk * cosr_ref[...], axis=0, keepdims=True)
            w = jnp.sum(dk * sinr_ref[...], axis=0, keepdims=True)
            c = cosc_ref[pl.ds(kp * BPC + b, 1), :]
            s = sinc_ref[pl.ds(kp * BPC + b, 1), :]
            sums[0:1, :] += u * c - w * s
            sums[1:2, :] += u * s + w * c
        sums[2:3, :] += jnp.sum(total[:, HEAD_DIM:], axis=0, keepdims=True)

    for c, out in enumerate((dq0, dq1, dq2, dq3)):

        @pl.when((kp == last) & (qi == c))
        def _(c=c, out=out):
            cosine = cosq_ref[c]
            sine = sinq_ref[c]
            for g in range(GROUP):
                there = slice(g * TOK, (g + 1) * TOK)
                a = dq_acc[c, :HALF, there] * SCALE
                b = dq_acc[c, HALF:, there] * SCALE
                turned = jnp.concatenate([a * cosine + b * sine, b * cosine - a * sine], axis=0)
                out[:, there] = turned.astype(out.dtype)
                turned_sum[:, there] += turned

    @pl.when((kp == last) & (qi == NEAR - 1))
    def _():
        rows = []
        for g in range(GROUP):
            rows.append(jnp.sum(turned_sum[:, g * TOK : (g + 1) * TOK].T, axis=0, keepdims=True))
        u = sums[0:1, :] * SCALE
        w = sums[1:2, :] * SCALE
        rows.append(u + jnp.concatenate([w[:, HALF:], -w[:, :HALF]], axis=1))
        rows.append(sums[2:3, :])
        rows.append(jnp.zeros((META - BIAS_ROWS, HEAD_DIM), F32))
        both = jnp.concatenate(split(jnp.concatenate(rows, axis=0), 2), axis=1)
        for y in range(RINGS):
            dkv_ref[y, TOK:, :] = both


def bias_kernel(got_ref, out_ref):
    total = jnp.sum(got_ref[...].astype(F32), axis=0)
    total = total[:, :HEAD_DIM] + total[:, HEAD_DIM:]
    for r in range(BIAS_ROWS):
        row = total[r : r + 1, :]
        out_ref[:, :, r * HEAD_DIM : (r + 1) * HEAD_DIM] = jnp.broadcast_to(
            row[None], (out_ref.shape[0], 1, HEAD_DIM)
        )


def finish_kernel(got_ref, dq0, dq1, dq2, dq3, cosk_ref, sink_ref, dq_ref, dk_ref, dv_ref):
    total = jnp.sum(got_ref[:, :TOK, :].astype(F32), axis=0)
    dv_ref[...] = total[:, HEAD_DIM:].astype(BF16)
    a = total[:, :HALF] * SCALE
    b = total[:, HALF:HEAD_DIM] * SCALE
    cosine = cosk_ref[...]
    sine = sink_ref[...]
    dk_ref[...] = jnp.concatenate([a * cosine + b * sine, b * cosine - a * sine], axis=1).astype(BF16)
    for g in range(GROUP):
        there = slice(g * TOK, (g + 1) * TOK)
        value = dq0[:, there] + dq1[:, there].astype(F32)
        value = value + (dq2[:, there].astype(F32) + dq3[:, there].astype(F32))
        dq_ref[:, g * HEAD_DIM : (g + 1) * HEAD_DIM] = value.T.astype(BF16)


def local(query_rot, key_rot, value_rows, attention_out, grad_out, log_norm, segments, block_table):
    near_axes = ("xh", "core")
    y = lax.axis_index("y")
    near = lax.axis_index(near_axes)
    outer = lax.axis_index("outer")
    example = outer // KV_HEADS
    seg = lax.dynamic_index_in_dim(segments, example, 0, keepdims=True)
    params = pltpu.CompilerParams(vmem_limit_bytes=48 << 20)

    pack, kv_copies = pl.pallas_call(
        pack_kernel,
        out_shape=[
            jax.ShapeDtypeStruct((PACK, TOK), BF16),
            jax.ShapeDtypeStruct((RINGS, TOK + META, 2 * HEAD_DIM), BF16),
        ],
        compiler_params=params,
    )(query_rot[0], grad_out[0], attention_out[0], log_norm[0], seg, key_rot[0], value_rows[0])

    def swap(value, bits):
        return lax.ppermute(value, near_axes, [(i, i ^ bits) for i in range(NEAR)])

    packs = [pack, swap(pack, 1), swap(pack, 2), swap(pack, 3)]
    kv = lax.all_to_all(kv_copies, "y", split_axis=0, concat_axis=0, tiled=True)

    frequency = jnp.exp(
        jnp.arange(HALF, dtype=F32) * (-2.0 * math.log(ROPE_BASE) / HEAD_DIM)
    )
    inside = jnp.arange(TOK, dtype=jnp.int32)
    blocks = y * NEAR + jnp.bitwise_xor(near, jnp.arange(NEAR, dtype=jnp.int32))
    positions = (blocks[:, None] * TOK + inside[None, :]).astype(F32)
    angles = frequency[None, :, None] * positions[:, None, :]
    cosq, sinq = jnp.cos(angles), jnp.sin(angles)
    doubled = jnp.concatenate([frequency, frequency])[None, :]
    within = inside.astype(F32)[:, None] * doubled
    starts = ((jnp.arange(RINGS, dtype=jnp.int32) * NEAR + near) * TOK).astype(F32)
    across = starts[:, None] * doubled
    mine = positions[0][:, None] * frequency[None, :]
    cosk, sink = jnp.cos(mine), jnp.sin(mine)

    whole = lambda *shape: pl.BlockSpec(shape, lambda i, j: (0,) * len(shape))
    dq_shape = lambda kind: jax.ShapeDtypeStruct((HEAD_DIM, LANES), kind)
    dkv, *parts = pl.pallas_call(
        attention_kernel,
        grid=(RINGS // BPC, NEAR),
        in_specs=[
            pl.BlockSpec((RINGS, META, 2 * HEAD_DIM), lambda i, j: (0, TOK // META, 0)),
            pl.BlockSpec((BPC, TOK + META, 2 * HEAD_DIM), lambda i, j: (i, 0, 0)),
            whole(PACK, TOK),
            whole(PACK, TOK),
            whole(PACK, TOK),
            whole(PACK, TOK),
            whole(NEAR, HALF, TOK),
            whole(NEAR, HALF, TOK),
            whole(TOK, HEAD_DIM),
            whole(TOK, HEAD_DIM),
            whole(RINGS, HEAD_DIM),
            whole(RINGS, HEAD_DIM),
        ],
        out_specs=[
            whole(RINGS, TOK + META, 2 * HEAD_DIM),
            whole(HEAD_DIM, LANES),
            whole(HEAD_DIM, LANES),
            whole(HEAD_DIM, LANES),
            whole(HEAD_DIM, LANES),
        ],
        out_shape=[
            jax.ShapeDtypeStruct((RINGS, TOK + META, 2 * HEAD_DIM), BF16),
            dq_shape(F32),
            dq_shape(F32),
            dq_shape(BF16),
            dq_shape(BF16),
        ],
        scratch_shapes=[
            pltpu.VMEM((NEAR, LANES, HEAD_DIM), BF16),
            pltpu.VMEM((NEAR, LANES, HEAD_DIM), BF16),
            pltpu.VMEM((NEAR, HEAD_DIM, LANES), BF16),
            pltpu.VMEM((NEAR, HEAD_DIM, LANES), BF16),
            pltpu.VMEM((NEAR, 1, LANES), F32),
            pltpu.VMEM((NEAR, 1, LANES), F32),
            pltpu.VMEM((NEAR, 1, LANES), jnp.int32),
            pltpu.VMEM((NEAR, HEAD_DIM, LANES), F32),
            pltpu.VMEM((BPC * TOK, 2 * HEAD_DIM), F32),
            pltpu.VMEM((HEAD_DIM, LANES), F32),
            pltpu.VMEM((8, HEAD_DIM), F32),
            pltpu.SMEM((3, NEAR), jnp.int32),
            pltpu.SMEM((2, RINGS), jnp.int32),
        ],
        compiler_params=params,
    )(
        kv, kv, *packs, cosq, sinq,
        jnp.cos(within), jnp.sin(within), jnp.cos(across), jnp.sin(across),
    )

    home = [parts[0], swap(parts[1], 1), swap(parts[2], 2), swap(parts[3], 3)]
    got = lax.all_to_all(dkv, "y", split_axis=0, concat_axis=0, tiled=True)

    team = lax.axis_size("outer") * NEAR
    bias_copies = pl.pallas_call(
        bias_kernel,
        grid=(1,),
        in_specs=[pl.BlockSpec((RINGS, META, 2 * HEAD_DIM), lambda i: (0, TOK // META, 0))],
        out_specs=pl.BlockSpec((team, 1, BIAS_ROWS * HEAD_DIM), lambda i: (0, 0, 0)),
        out_shape=jax.ShapeDtypeStruct((team, 1, BIAS_ROWS * HEAD_DIM), F32),
        compiler_params=params,
    )(got)
    biases = lax.all_to_all(
        bias_copies, ("outer",) + near_axes, split_axis=0, concat_axis=0, tiled=True
    )

    dq, dk, dv = pl.pallas_call(
        finish_kernel,
        out_shape=[
            jax.ShapeDtypeStruct((TOK, WIDTH), BF16),
            jax.ShapeDtypeStruct((TOK, HEAD_DIM), BF16),
            jax.ShapeDtypeStruct((TOK, HEAD_DIM), BF16),
        ],
        compiler_params=params,
    )(got, *home, cosk, sink)

    examples = team // (KV_HEADS * NEAR)
    summed = biases.reshape(examples, KV_HEADS, NEAR, BIAS_ROWS * HEAD_DIM).sum(axis=(0, 2))
    grad_bias = jnp.concatenate(
        [
            summed[:, :WIDTH].reshape(-1),
            summed[:, WIDTH : WIDTH + HEAD_DIM].reshape(-1),
            summed[:, WIDTH + HEAD_DIM :].reshape(-1),
        ]
    )
    return dq[None], dk[None], dv[None], grad_bias


def solution(mesh):
    fine = Mesh(mesh.devices.reshape(-1, RINGS, 2, 2), ("outer", "y", "xh", "core"))
    inner = ("y", "xh", "core")
    rows = P("outer", inner, None)
    placed = (
        rows,
        rows,
        rows,
        rows,
        rows,
        P("outer", None, inner),
        P(None, inner),
        P(None, inner, None),
    )
    return jax.shard_map(
        local, mesh=fine, in_specs=placed, out_specs=(rows, rows, rows, P()), check_vma=False
    )
```

```python
import math

import jax
import jax.numpy as jnp
from jax import lax
from jax.experimental import pallas as pl
from jax.experimental.pallas import tpu as pltpu
from jax.sharding import Mesh, PartitionSpec as P

HEADS = 28
KV_HEADS = 4
HEAD_DIM = 128
GROUP = HEADS // KV_HEADS
TOK = 128
ROPE_BASE = 1000000.0
HALF = HEAD_DIM // 2
SCALE = HEAD_DIM ** (-0.5)
LOG2E = math.log2(math.e)

RINGS = 8
NEAR = 4
BPC = 2
META = 16
LANES = GROUP * TOK
WIDTH = GROUP * HEAD_DIM
PACK = 2 * LANES + 48
BIAS_ROWS = GROUP + 2

F32 = jnp.float32
BF16 = jnp.bfloat16


def split(value, terms):
    parts = []
    for _ in range(terms):
        part = value.astype(BF16)
        parts.append(part)
        value = value - part.astype(F32)
    return parts


def pack_keys_kernel(seg_ref, k_ref, v_ref, kv_ref):
    seg = seg_ref[...]
    row = lax.broadcasted_iota(jnp.int32, (META, 2 * HEAD_DIM), 0)
    prompt = jnp.sum(jnp.where(seg == 0, 1.0, 0.0))
    chosen = jnp.sum(jnp.where(seg <= 1, 1.0, 0.0))
    meta = jnp.where(row == 0, prompt, jnp.where(row == 1, chosen, 0.0)).astype(BF16)
    keys = k_ref[...]
    values = v_ref[...]
    for y in range(RINGS):
        kv_ref[y, :TOK, :HEAD_DIM] = keys
        kv_ref[y, :TOK, HEAD_DIM:] = values
        kv_ref[y, TOK:, :] = meta


def pack_queries_kernel(q_ref, go_ref, ao_ref, norm_ref, seg_ref, unused_ref, pack_ref, ao_own, sems):
    copies = []
    for g in range(GROUP):
        here = slice(g * HEAD_DIM, (g + 1) * HEAD_DIM)
        rows = pl.ds(g * TOK, TOK)
        far_rows = pl.ds(LANES + g * TOK, TOK)
        trio = [
            pltpu.make_async_copy(go_ref.at[:, here], pack_ref.at[far_rows, :], sems.at[0, g]),
            pltpu.make_async_copy(ao_ref.at[:, here], ao_own.at[rows, :], sems.at[1, g]),
            pltpu.make_async_copy(q_ref.at[:, here], pack_ref.at[rows, :], sems.at[2, g]),
        ]
        for copy in trio:
            copy.start()
        copies.append(trio)
    seg = seg_ref[...]
    zero = jnp.zeros((1, TOK), F32)
    eight = lambda rows: jnp.concatenate(rows + [zero] * (8 - len(rows)), axis=0)
    norms = norm_ref[...] * LOG2E
    parts = split(eight([norms[g : g + 1, :] for g in range(GROUP)] + [seg.astype(F32)]), 3)
    deltas = []
    for g in range(GROUP):
        copies[g][0].wait()
        copies[g][1].wait()
        go = pack_ref[LANES + g * TOK : LANES + (g + 1) * TOK, :]
        product = go.astype(F32) * ao_own[g * TOK : (g + 1) * TOK, :].astype(F32)
        deltas.append(jnp.sum(product.T, axis=0, keepdims=True))
    parts += split(eight(deltas), 3)
    rows = jnp.concatenate([part.astype(F32) for part in parts], axis=0)
    pack_ref[2 * LANES :, :] = rows.astype(BF16)
    for g in range(GROUP):
        copies[g][2].wait()


def attention_kernel(
    meta_ref, kv_ref, pack0, pack1, pack2, pack3, cosq_ref, sinq_ref, cosr_ref, sinr_ref, cosc_ref, sinc_ref,
    dkv_ref, dq0, dq1, dq_far,
    q_rows, go_rows, q_cols, go_cols, delta, norm2, seg_q, dq_acc, kv_acc, turned_sum, sums, kinds, counts,
):
    kp = pl.program_id(0)
    qi = pl.program_id(1)
    last = pl.num_programs(0) - 1
    chunk = BPC * TOK

    @pl.when((kp == 0) & (qi == 0))
    def _():
        for y in range(RINGS):
            meta = meta_ref[y].astype(F32)
            counts[0, y] = jnp.max(meta[0:1, :]).astype(jnp.int32)
            counts[1, y] = jnp.max(meta[1:2, :]).astype(jnp.int32)
        dq_acc[...] = jnp.zeros_like(dq_acc)
        turned_sum[...] = jnp.zeros_like(turned_sum)
        sums[...] = jnp.zeros_like(sums)

    for c, pack in enumerate((pack0, pack1, pack2, pack3)):

        @pl.when((kp == 0) & (qi == c))
        def _(c=c, pack=pack):
            extra = pack[2 * LANES :, :].astype(F32)
            norms = extra[0:8] + extra[8:16] + extra[16:24]
            deltas = extra[24:32] + extra[32:40] + extra[40:48]
            seg = norms[GROUP : GROUP + 1, :].astype(jnp.int32)
            kinds[0, c] = jnp.min(seg)
            kinds[1, c] = jnp.max(seg)
            kinds[2, c] = jnp.max(jnp.where(seg == 1, 1, 0))
            q_rows[c] = pack[:LANES, :]
            go_rows[c] = pack[LANES : 2 * LANES, :]
            for g in range(GROUP):
                there = slice(g * TOK, (g + 1) * TOK)
                q_cols[c, :, there] = pack[g * TOK : (g + 1) * TOK, :].T
                go_cols[c, :, there] = pack[LANES + g * TOK : LANES + (g + 1) * TOK, :].T
                delta[c, :, there] = deltas[g : g + 1, :]
                norm2[c, :, there] = norms[g : g + 1, :]
                seg_q[c, :, there] = seg

    @pl.when(qi == 0)
    def _():
        kv_acc[...] = jnp.zeros_like(kv_acc)

    least, most, has1 = kinds[0, qi], kinds[1, qi], kinds[2, qi] > 0
    whole = True
    some = False
    for b in range(BPC):
        c0, c1 = counts[0, kp * BPC + b], counts[1, kp * BPC + b]
        entire = (
            (c0 == TOK)
            | ((least == 1) & (most == 1) & (c0 == 0) & (c1 == TOK))
            | ((least == 2) & (c1 == 0))
        )
        part = (c0 > 0) | (has1 & (c1 > c0)) | ((most == 2) & (c1 < TOK))
        whole = entire & whole
        some = part | some

    def compute(masked):
        keys = kv_ref[:, :TOK, :HEAD_DIM].reshape(chunk, HEAD_DIM)
        values = kv_ref[:, :TOK, HEAD_DIM:].reshape(chunk, HEAD_DIM)
        scores = jnp.dot(keys, q_cols[qi], preferred_element_type=F32)
        probs = jnp.exp2(scores * (SCALE * LOG2E) - norm2[qi])
        if masked:
            at = lax.broadcasted_iota(jnp.int32, (TOK, LANES), 0)
            seg = seg_q[qi]
            pieces = []
            for b in range(BPC):
                c0, c1 = counts[0, kp * BPC + b], counts[1, kp * BPC + b]
                low = jnp.where(seg == 1, c0, jnp.where(seg == 2, c1, 0))
                high = jnp.where(seg == 1, c1, jnp.where(seg == 2, TOK, 0))
                allowed = (at < c0) | ((at >= low) & (at < high))
                pieces.append(jnp.where(allowed, probs[b * TOK : (b + 1) * TOK, :], 0.0))
            probs = jnp.concatenate(pieces, axis=0)
        grad_probs = jnp.dot(values, go_cols[qi], preferred_element_type=F32)
        scores_low = (probs * (grad_probs - delta[qi])).astype(BF16)
        dv = jnp.dot(probs.astype(BF16), go_rows[qi], preferred_element_type=F32)
        dk = jnp.dot(scores_low, q_rows[qi], preferred_element_type=F32)
        dq_acc[qi] += jnp.dot(keys.T, scores_low, preferred_element_type=F32)
        kv_acc[:, :HEAD_DIM] += dk
        kv_acc[:, HEAD_DIM:] += dv

    @pl.when(whole)
    def _():
        compute(False)

    @pl.when(some & jnp.logical_not(whole))
    def _():
        compute(True)

    @pl.when(qi == NEAR - 1)
    def _():
        total = kv_acc[...]
        low = total.astype(BF16)
        for b in range(BPC):
            dkv_ref[kp * BPC + b, :TOK, :] = low[b * TOK : (b + 1) * TOK, :]
            dk = total[b * TOK : (b + 1) * TOK, :HEAD_DIM]
            u = jnp.sum(dk * cosr_ref[...], axis=0, keepdims=True)
            w = jnp.sum(dk * sinr_ref[...], axis=0, keepdims=True)
            c = cosc_ref[pl.ds(kp * BPC + b, 1), :]
            s = sinc_ref[pl.ds(kp * BPC + b, 1), :]
            sums[0:1, :] += u * c - w * s
            sums[1:2, :] += u * s + w * c
        sums[2:3, :] += jnp.sum(total[:, HEAD_DIM:], axis=0, keepdims=True)

    for c, out in enumerate((dq0, dq1, dq_far.at[0], dq_far.at[1])):

        @pl.when((kp == last) & (qi == c))
        def _(c=c, out=out):
            cosine = cosq_ref[c]
            sine = sinq_ref[c]
            for g in range(GROUP):
                there = slice(g * TOK, (g + 1) * TOK)
                a = dq_acc[c, :HALF, there] * SCALE
                b = dq_acc[c, HALF:, there] * SCALE
                turned = jnp.concatenate([a * cosine + b * sine, b * cosine - a * sine], axis=0)
                out[:, there] = turned.astype(out.dtype)
                turned_sum[:, there] += turned

    @pl.when((kp == last) & (qi == NEAR - 1))
    def _():
        rows = []
        for g in range(GROUP):
            rows.append(jnp.sum(turned_sum[:, g * TOK : (g + 1) * TOK].T, axis=0, keepdims=True))
        u = sums[0:1, :] * SCALE
        w = sums[1:2, :] * SCALE
        rows.append(u + jnp.concatenate([w[:, HALF:], -w[:, :HALF]], axis=1))
        rows.append(sums[2:3, :])
        rows.append(jnp.zeros((META - BIAS_ROWS, HEAD_DIM), F32))
        both = jnp.concatenate(split(jnp.concatenate(rows, axis=0), 2), axis=1)
        for y in range(RINGS):
            dkv_ref[y, TOK:, :] = both


def bias_kernel(got_ref, unused_ref, out_ref):
    total = jnp.sum(got_ref[...].astype(F32), axis=0)
    total = total[:, :HEAD_DIM] + total[:, HEAD_DIM:]
    for r in range(BIAS_ROWS):
        row = total[r : r + 1, :]
        out_ref[:, :, r * HEAD_DIM : (r + 1) * HEAD_DIM] = jnp.broadcast_to(
            row[None], (out_ref.shape[0], 1, HEAD_DIM)
        )


def add_kernel(own_ref, far_ref, out_ref):
    out_ref[...] = own_ref[...] + far_ref[1].astype(F32)


def finish_kernel(got_ref, dq_own, dq_far, dq_near, cosk_ref, sink_ref, dq_ref, dk_ref, dv_ref):
    total = jnp.sum(got_ref[:, :TOK, :].astype(F32), axis=0)
    dv_ref[...] = total[:, HEAD_DIM:].astype(BF16)
    a = total[:, :HALF] * SCALE
    b = total[:, HALF:HEAD_DIM] * SCALE
    cosine = cosk_ref[...]
    sine = sink_ref[...]
    dk_ref[...] = jnp.concatenate([a * cosine + b * sine, b * cosine - a * sine], axis=1).astype(BF16)
    for g in range(GROUP):
        there = slice(g * TOK, (g + 1) * TOK)
        value = dq_own[:, there] + (dq_far[0, :, there].astype(F32) + dq_near[:, there])
        dq_ref[:, g * HEAD_DIM : (g + 1) * HEAD_DIM] = value.T.astype(BF16)


def local(query_rot, key_rot, value_rows, attention_out, grad_out, log_norm, segments, block_table):
    near_axes = ("xh", "core")
    y = lax.axis_index("y")
    near = lax.axis_index(near_axes)
    outer = lax.axis_index("outer")
    example = outer // KV_HEADS
    seg = lax.dynamic_index_in_dim(segments, example, 0, keepdims=True)
    params = pltpu.CompilerParams(vmem_limit_bytes=48 << 20)

    kv_copies = pl.pallas_call(
        pack_keys_kernel,
        out_shape=jax.ShapeDtypeStruct((RINGS, TOK + META, 2 * HEAD_DIM), BF16),
        compiler_params=params,
    )(seg, key_rot[0], value_rows[0])
    kv = lax.all_to_all(kv_copies, "y", split_axis=0, concat_axis=0, tiled=True)
    vmem = pl.BlockSpec(memory_space=pltpu.VMEM)
    hbm = pl.BlockSpec(memory_space=pltpu.HBM)
    anywhere = pl.BlockSpec(memory_space=pl.ANY)
    pack = pl.pallas_call(
        pack_queries_kernel,
        in_specs=[hbm, hbm, hbm, vmem, vmem, anywhere],
        out_shape=jax.ShapeDtypeStruct((PACK, TOK), BF16),
        scratch_shapes=[pltpu.VMEM((LANES, TOK), BF16), pltpu.SemaphoreType.DMA((3, GROUP))],
        compiler_params=params,
    )(query_rot[0], grad_out[0], attention_out[0], log_norm[0], seg, kv_copies)

    def swap(value, bits):
        return lax.ppermute(value, near_axes, [(i, i ^ bits) for i in range(NEAR)])

    far = swap(pack, 2)
    packs = [pack, swap(pack, 1), far, swap(far, 1)]

    frequency = jnp.exp(
        jnp.arange(HALF, dtype=F32) * (-2.0 * math.log(ROPE_BASE) / HEAD_DIM)
    )
    inside = jnp.arange(TOK, dtype=jnp.int32)
    blocks = y * NEAR + jnp.bitwise_xor(near, jnp.arange(NEAR, dtype=jnp.int32))
    positions = (blocks[:, None] * TOK + inside[None, :]).astype(F32)
    angles = frequency[None, :, None] * positions[:, None, :]
    cosq, sinq = jnp.cos(angles), jnp.sin(angles)
    doubled = jnp.concatenate([frequency, frequency])[None, :]
    within = inside.astype(F32)[:, None] * doubled
    starts = ((jnp.arange(RINGS, dtype=jnp.int32) * NEAR + near) * TOK).astype(F32)
    across = starts[:, None] * doubled
    mine = positions[0][:, None] * frequency[None, :]
    cosk, sink = jnp.cos(mine), jnp.sin(mine)

    whole = lambda *shape: pl.BlockSpec(shape, lambda i, j: (0,) * len(shape))
    dkv, dq_own, dq_near, dq_far = pl.pallas_call(
        attention_kernel,
        grid=(RINGS // BPC, NEAR),
        in_specs=[
            pl.BlockSpec((RINGS, META, 2 * HEAD_DIM), lambda i, j: (0, TOK // META, 0)),
            pl.BlockSpec((BPC, TOK + META, 2 * HEAD_DIM), lambda i, j: (i, 0, 0)),
            whole(PACK, TOK),
            whole(PACK, TOK),
            whole(PACK, TOK),
            whole(PACK, TOK),
            whole(NEAR, HALF, TOK),
            whole(NEAR, HALF, TOK),
            whole(TOK, HEAD_DIM),
            whole(TOK, HEAD_DIM),
            whole(RINGS, HEAD_DIM),
            whole(RINGS, HEAD_DIM),
        ],
        out_specs=[
            whole(RINGS, TOK + META, 2 * HEAD_DIM),
            whole(HEAD_DIM, LANES),
            whole(HEAD_DIM, LANES),
            whole(2, HEAD_DIM, LANES),
        ],
        out_shape=[
            jax.ShapeDtypeStruct((RINGS, TOK + META, 2 * HEAD_DIM), BF16),
            jax.ShapeDtypeStruct((HEAD_DIM, LANES), F32),
            jax.ShapeDtypeStruct((HEAD_DIM, LANES), F32),
            jax.ShapeDtypeStruct((2, HEAD_DIM, LANES), BF16),
        ],
        scratch_shapes=[
            pltpu.VMEM((NEAR, LANES, HEAD_DIM), BF16),
            pltpu.VMEM((NEAR, LANES, HEAD_DIM), BF16),
            pltpu.VMEM((NEAR, HEAD_DIM, LANES), BF16),
            pltpu.VMEM((NEAR, HEAD_DIM, LANES), BF16),
            pltpu.VMEM((NEAR, 1, LANES), F32),
            pltpu.VMEM((NEAR, 1, LANES), F32),
            pltpu.VMEM((NEAR, 1, LANES), jnp.int32),
            pltpu.VMEM((NEAR, HEAD_DIM, LANES), F32),
            pltpu.VMEM((BPC * TOK, 2 * HEAD_DIM), F32),
            pltpu.VMEM((HEAD_DIM, LANES), F32),
            pltpu.VMEM((8, HEAD_DIM), F32),
            pltpu.SMEM((3, NEAR), jnp.int32),
            pltpu.SMEM((2, RINGS), jnp.int32),
        ],
        compiler_params=params,
    )(
        kv, kv, *packs, cosq, sinq,
        jnp.cos(within), jnp.sin(within), jnp.cos(across), jnp.sin(across),
    )

    got = lax.all_to_all(dkv, "y", split_axis=0, concat_axis=0, tiled=True)
    far_back = swap(dq_far, 2)
    near_sum = pl.pallas_call(
        add_kernel,
        out_shape=jax.ShapeDtypeStruct((HEAD_DIM, LANES), F32),
        compiler_params=params,
    )(dq_near, far_back)
    near_back = swap(near_sum, 1)

    team = lax.axis_size("outer") * NEAR
    bias_copies = pl.pallas_call(
        bias_kernel,
        grid=(1,),
        in_specs=[
            pl.BlockSpec((RINGS, META, 2 * HEAD_DIM), lambda i: (0, TOK // META, 0)),
            anywhere,
        ],
        out_specs=pl.BlockSpec((team, 1, BIAS_ROWS * HEAD_DIM), lambda i: (0, 0, 0)),
        out_shape=jax.ShapeDtypeStruct((team, 1, BIAS_ROWS * HEAD_DIM), F32),
        compiler_params=params,
    )(got, near_back)
    biases = lax.all_to_all(
        bias_copies, ("outer",) + near_axes, split_axis=0, concat_axis=0, tiled=True
    )

    dq, dk, dv = pl.pallas_call(
        finish_kernel,
        out_shape=[
            jax.ShapeDtypeStruct((TOK, WIDTH), BF16),
            jax.ShapeDtypeStruct((TOK, HEAD_DIM), BF16),
            jax.ShapeDtypeStruct((TOK, HEAD_DIM), BF16),
        ],
        compiler_params=params,
    )(got, dq_own, far_back, near_back, cosk, sink)

    examples = team // (KV_HEADS * NEAR)
    summed = biases.reshape(examples, KV_HEADS, NEAR, BIAS_ROWS * HEAD_DIM).sum(axis=(0, 2))
    grad_bias = jnp.concatenate(
        [
            summed[:, :WIDTH].reshape(-1),
            summed[:, WIDTH : WIDTH + HEAD_DIM].reshape(-1),
            summed[:, WIDTH + HEAD_DIM :].reshape(-1),
        ]
    )
    return dq[None], dk[None], dv[None], grad_bias


def solution(mesh):
    fine = Mesh(mesh.devices.reshape(-1, RINGS, 2, 2), ("outer", "y", "xh", "core"))
    inner = ("y", "xh", "core")
    rows = P("outer", inner, None)
    placed = (
        rows,
        rows,
        rows,
        rows,
        rows,
        P("outer", None, inner),
        P(None, inner),
        P(None, inner, None),
    )
    return jax.shard_map(
        local, mesh=fine, in_specs=placed, out_specs=(rows, rows, rows, P()), check_vma=False
    )
```

```python
import math

import jax
import jax.numpy as jnp
from jax import lax
from jax.experimental import pallas as pl
from jax.experimental.pallas import tpu as pltpu
from jax.sharding import Mesh, PartitionSpec as P

HEADS = 28
KV_HEADS = 4
HEAD_DIM = 128
GROUP = HEADS // KV_HEADS
TOK = 128
ROPE_BASE = 1000000.0
HALF = HEAD_DIM // 2
SCALE = HEAD_DIM ** (-0.5)
LOG2E = math.log2(math.e)

RINGS = 8
NEAR = 4
BPC = 8
META = 16
LANES = GROUP * TOK
WIDTH = GROUP * HEAD_DIM
HEADSETS = [(0, 2), (2, 4), (4, 6), (6, 7)]
PACK = 2 * LANES + 48
BIAS_ROWS = GROUP + 2

F32 = jnp.float32
BF16 = jnp.bfloat16


def split(value, terms):
    parts = []
    for _ in range(terms):
        part = value.astype(BF16)
        parts.append(part)
        value = value - part.astype(F32)
    return parts


def pack_keys_kernel(seg_ref, k_ref, v_ref, kv_ref):
    seg = seg_ref[...]
    row = lax.broadcasted_iota(jnp.int32, (META, 2 * HEAD_DIM), 0)
    prompt = jnp.sum(jnp.where(seg == 0, 1.0, 0.0))
    chosen = jnp.sum(jnp.where(seg <= 1, 1.0, 0.0))
    meta = jnp.where(row == 0, prompt, jnp.where(row == 1, chosen, 0.0)).astype(BF16)
    keys = k_ref[...]
    values = v_ref[...]
    for y in range(RINGS):
        kv_ref[y, :TOK, :HEAD_DIM] = keys
        kv_ref[y, :TOK, HEAD_DIM:] = values
        kv_ref[y, TOK:, :] = meta


def pack_queries_kernel(q_ref, go_ref, ao_ref, norm_ref, seg_ref, unused_ref, pack_ref, ao_own, sems):
    copies = []
    for g in range(GROUP):
        here = slice(g * HEAD_DIM, (g + 1) * HEAD_DIM)
        rows = pl.ds(g * TOK, TOK)
        far_rows = pl.ds(LANES + g * TOK, TOK)
        trio = [
            pltpu.make_async_copy(go_ref.at[:, here], pack_ref.at[far_rows, :], sems.at[0, g]),
            pltpu.make_async_copy(ao_ref.at[:, here], ao_own.at[rows, :], sems.at[1, g]),
            pltpu.make_async_copy(q_ref.at[:, here], pack_ref.at[rows, :], sems.at[2, g]),
        ]
        for copy in trio:
            copy.start()
        copies.append(trio)
    seg = seg_ref[...]
    zero = jnp.zeros((1, TOK), F32)
    eight = lambda rows: jnp.concatenate(rows + [zero] * (8 - len(rows)), axis=0)
    norms = norm_ref[...] * LOG2E
    parts = split(eight([norms[g : g + 1, :] for g in range(GROUP)] + [seg.astype(F32)]), 3)
    deltas = []
    for g in range(GROUP):
        copies[g][0].wait()
        copies[g][1].wait()
        go = pack_ref[LANES + g * TOK : LANES + (g + 1) * TOK, :]
        product = go.astype(F32) * ao_own[g * TOK : (g + 1) * TOK, :].astype(F32)
        deltas.append(jnp.sum(product.T, axis=0, keepdims=True))
    parts += split(eight(deltas), 3)
    rows = jnp.concatenate([part.astype(F32) for part in parts], axis=0)
    pack_ref[2 * LANES :, :] = rows.astype(BF16)
    for g in range(GROUP):
        copies[g][2].wait()


def attention_kernel(
    kv_ref, pack0, pack1, pack2, pack3, cosq_ref, sinq_ref, cosr_ref, sinr_ref, cosc_ref, sinc_ref,
    dkv_ref, dq0, dq1, dq_far,
    pack, kv_acc, turned_sum, counts,
):
    part = pl.program_id(0)
    rows_in = BPC * TOK
    contract = (((1,), (1,)), ((), ()))

    @pl.when(part == 0)
    def _():
        for y in range(RINGS):
            meta = kv_ref[y, TOK:, :].astype(F32)
            counts[0, y] = jnp.max(meta[0:1, :]).astype(jnp.int32)
            counts[1, y] = jnp.max(meta[1:2, :]).astype(jnp.int32)
        turned_sum[...] = jnp.zeros_like(turned_sum)
        kv_acc[...] = jnp.zeros_like(kv_acc)

    for c, source in enumerate((pack0, pack1, pack2, pack3)):

        @pl.when(part == c)
        def _(source=source):
            pack[...] = source[...]

    extra = pack[2 * LANES :, :].astype(F32)
    norms = extra[0:8] + extra[8:16] + extra[16:24]
    deltas = extra[24:32] + extra[32:40] + extra[40:48]
    seg = norms[GROUP : GROUP + 1, :].astype(jnp.int32)
    across = lambda rows, g0, g1: jnp.concatenate([rows[g : g + 1, :] for g in range(g0, g1)], axis=1)
    at = lax.broadcasted_iota(jnp.int32, (TOK, TOK), 0)
    dq = jnp.zeros((HEAD_DIM, LANES), F32)
    for k in range(RINGS // BPC):
        blocks = pl.ds(k * BPC, BPC)
        keys = kv_ref[blocks, :TOK, :HEAD_DIM].reshape(rows_in, HEAD_DIM)
        values = kv_ref[blocks, :TOK, HEAD_DIM:].reshape(rows_in, HEAD_DIM)
        allowed = []
        for b in range(k * BPC, (k + 1) * BPC):
            c0, c1 = counts[0, b], counts[1, b]
            below = jnp.where(seg == 1, c1, c0)
            above = jnp.where(seg == 2, c1, TOK)
            allowed.append((at < below) | (at >= above))
        allowed = jnp.concatenate(allowed, axis=0)
        probs_low = []
        scores_low = []
        for g0, g1 in HEADSETS:
            there = slice(g0 * TOK, g1 * TOK)
            near = slice(LANES + g0 * TOK, LANES + g1 * TOK)
            scores = lax.dot_general(keys, pack[there, :], contract, preferred_element_type=F32)
            probs = jnp.exp2(scores * (SCALE * LOG2E) - across(norms, g0, g1))
            probs = jnp.where(jnp.concatenate([allowed] * (g1 - g0), axis=1), probs, 0.0)
            grad_probs = lax.dot_general(values, pack[near, :], contract, preferred_element_type=F32)
            scores_low.append((probs * (grad_probs - across(deltas, g0, g1))).astype(BF16))
            probs_low.append(probs.astype(BF16))
        scores_low = jnp.concatenate(scores_low, axis=1)
        probs_low = jnp.concatenate(probs_low, axis=1)
        dv = jnp.dot(probs_low, pack[LANES : 2 * LANES, :], preferred_element_type=F32)
        dk = jnp.dot(scores_low, pack[:LANES, :], preferred_element_type=F32)
        kv_acc[k * rows_in : (k + 1) * rows_in, :HEAD_DIM] += dk
        kv_acc[k * rows_in : (k + 1) * rows_in, HEAD_DIM:] += dv
        dq += jnp.dot(keys.T, scores_low, preferred_element_type=F32)

    cosine = jnp.concatenate([cosq_ref[part]] * GROUP, axis=1) * SCALE
    sine = jnp.concatenate([sinq_ref[part]] * GROUP, axis=1) * SCALE
    upper, lower = dq[:HALF], dq[HALF:]
    turned = jnp.concatenate(
        [upper * cosine + lower * sine, lower * cosine - upper * sine], axis=0
    )
    turned_sum[...] += turned
    for c, out in enumerate((dq0, dq1, dq_far.at[0], dq_far.at[1])):

        @pl.when(part == c)
        def _(out=out):
            out[...] = turned.astype(out.dtype)

    @pl.when(part == NEAR - 1)
    def _():
        u_all = jnp.zeros((1, HEAD_DIM), F32)
        w_all = jnp.zeros((1, HEAD_DIM), F32)
        v_all = jnp.zeros((1, HEAD_DIM), F32)
        for b in range(RINGS):
            total = kv_acc[b * TOK : (b + 1) * TOK, :]
            dkv_ref[b, :TOK, :] = total.astype(BF16)
            dk = total[:, :HEAD_DIM]
            u = jnp.sum(dk * cosr_ref[...], axis=0, keepdims=True)
            w = jnp.sum(dk * sinr_ref[...], axis=0, keepdims=True)
            c = cosc_ref[b : b + 1, :]
            s = sinc_ref[b : b + 1, :]
            u_all += u * c - w * s
            w_all += u * s + w * c
            v_all += jnp.sum(total[:, HEAD_DIM:], axis=0, keepdims=True)
        rows = []
        for g in range(GROUP):
            rows.append(jnp.sum(turned_sum[:, g * TOK : (g + 1) * TOK].T, axis=0, keepdims=True))
        u = u_all * SCALE
        w = w_all * SCALE
        rows.append(u + jnp.concatenate([w[:, HALF:], -w[:, :HALF]], axis=1))
        rows.append(v_all)
        rows.append(jnp.zeros((META - BIAS_ROWS, HEAD_DIM), F32))
        both = jnp.concatenate(split(jnp.concatenate(rows, axis=0), 2), axis=1)
        for y in range(RINGS):
            dkv_ref[y, TOK:, :] = both


def attend(kv, packs, cosq, sinq, cosr, sinr, cosc, sinc):
    vmem = pl.BlockSpec(memory_space=pltpu.VMEM)
    return pl.pallas_call(
        attention_kernel,
        grid=(NEAR,),
        in_specs=[vmem] * 11,
        out_specs=[vmem] * 4,
        out_shape=[
            jax.ShapeDtypeStruct((RINGS, TOK + META, 2 * HEAD_DIM), BF16),
            jax.ShapeDtypeStruct((HEAD_DIM, LANES), F32),
            jax.ShapeDtypeStruct((HEAD_DIM, LANES), F32),
            jax.ShapeDtypeStruct((2, HEAD_DIM, LANES), BF16),
        ],
        scratch_shapes=[
            pltpu.VMEM((PACK, TOK), BF16),
            pltpu.VMEM((RINGS * TOK, 2 * HEAD_DIM), F32),
            pltpu.VMEM((HEAD_DIM, LANES), F32),
            pltpu.SMEM((2, RINGS), jnp.int32),
        ],
        compiler_params=pltpu.CompilerParams(vmem_limit_bytes=24 << 20),
    )(kv, *packs, cosq, sinq, cosr, sinr, cosc, sinc)


def bias_kernel(got_ref, unused_ref, out_ref):
    total = jnp.sum(got_ref[...].astype(F32), axis=0)
    total = total[:, :HEAD_DIM] + total[:, HEAD_DIM:]
    for r in range(BIAS_ROWS):
        row = total[r : r + 1, :]
        out_ref[:, :, r * HEAD_DIM : (r + 1) * HEAD_DIM] = jnp.broadcast_to(
            row[None], (out_ref.shape[0], 1, HEAD_DIM)
        )


def add_kernel(own_ref, far_ref, out_ref):
    out_ref[...] = own_ref[...] + far_ref[1].astype(F32)


def finish_kernel(got_ref, dq_own, dq_far, dq_near, cosk_ref, sink_ref, dq_ref, dk_ref, dv_ref):
    total = jnp.sum(got_ref[:, :TOK, :].astype(F32), axis=0)
    dv_ref[...] = total[:, HEAD_DIM:].astype(BF16)
    a = total[:, :HALF] * SCALE
    b = total[:, HALF:HEAD_DIM] * SCALE
    cosine = cosk_ref[...]
    sine = sink_ref[...]
    dk_ref[...] = jnp.concatenate([a * cosine + b * sine, b * cosine - a * sine], axis=1).astype(BF16)
    for g in range(GROUP):
        there = slice(g * TOK, (g + 1) * TOK)
        value = dq_own[:, there] + (dq_far[0, :, there].astype(F32) + dq_near[:, there])
        dq_ref[:, g * HEAD_DIM : (g + 1) * HEAD_DIM] = value.T.astype(BF16)


def local(query_rot, key_rot, value_rows, attention_out, grad_out, log_norm, segments, block_table):
    near_axes = ("xh", "core")
    y = lax.axis_index("y")
    near = lax.axis_index(near_axes)
    outer = lax.axis_index("outer")
    example = outer // KV_HEADS
    seg = lax.dynamic_index_in_dim(segments, example, 0, keepdims=True)
    params = pltpu.CompilerParams(vmem_limit_bytes=8 << 20)

    kv_copies = pl.pallas_call(
        pack_keys_kernel,
        out_shape=jax.ShapeDtypeStruct((RINGS, TOK + META, 2 * HEAD_DIM), BF16),
        compiler_params=params,
    )(seg, key_rot[0], value_rows[0])
    kv = lax.all_to_all(kv_copies, "y", split_axis=0, concat_axis=0, tiled=True)
    vmem = pl.BlockSpec(memory_space=pltpu.VMEM)
    hbm = pl.BlockSpec(memory_space=pltpu.HBM)
    anywhere = pl.BlockSpec(memory_space=pl.ANY)
    pack = pl.pallas_call(
        pack_queries_kernel,
        in_specs=[hbm, hbm, hbm, vmem, vmem, anywhere],
        out_shape=jax.ShapeDtypeStruct((PACK, TOK), BF16),
        scratch_shapes=[pltpu.VMEM((LANES, TOK), BF16), pltpu.SemaphoreType.DMA((3, GROUP))],
        compiler_params=params,
    )(query_rot[0], grad_out[0], attention_out[0], log_norm[0], seg, kv_copies)

    def swap(value, bits):
        return lax.ppermute(value, near_axes, [(i, i ^ bits) for i in range(NEAR)])

    far = swap(pack, 2)
    pack, far = lax.optimization_barrier((pack, far))
    packs = [pack, swap(pack, 1), far, swap(far, 1)]

    frequency = jnp.exp(
        jnp.arange(HALF, dtype=F32) * (-2.0 * math.log(ROPE_BASE) / HEAD_DIM)
    )
    inside = jnp.arange(TOK, dtype=jnp.int32)
    blocks = y * NEAR + jnp.bitwise_xor(near, jnp.arange(NEAR, dtype=jnp.int32))
    positions = (blocks[:, None] * TOK + inside[None, :]).astype(F32)
    angles = frequency[None, :, None] * positions[:, None, :]
    cosq, sinq = jnp.cos(angles), jnp.sin(angles)
    doubled = jnp.concatenate([frequency, frequency])[None, :]
    within = inside.astype(F32)[:, None] * doubled
    starts = ((jnp.arange(RINGS, dtype=jnp.int32) * NEAR + near) * TOK).astype(F32)
    across = starts[:, None] * doubled
    mine = positions[0][:, None] * frequency[None, :]
    cosk, sink = jnp.cos(mine), jnp.sin(mine)

    dkv, dq_own, dq_near, dq_far = attend(
        kv, packs, cosq, sinq, jnp.cos(within), jnp.sin(within), jnp.cos(across), jnp.sin(across)
    )

    got = lax.all_to_all(dkv, "y", split_axis=0, concat_axis=0, tiled=True)
    far_back = swap(dq_far, 2)
    near_sum = pl.pallas_call(
        add_kernel,
        out_shape=jax.ShapeDtypeStruct((HEAD_DIM, LANES), F32),
        compiler_params=params,
    )(dq_near, far_back)
    near_back = swap(near_sum, 1)

    team = lax.axis_size("outer") * NEAR
    bias_copies = pl.pallas_call(
        bias_kernel,
        grid=(1,),
        in_specs=[
            pl.BlockSpec((RINGS, META, 2 * HEAD_DIM), lambda i: (0, TOK // META, 0)),
            anywhere,
        ],
        out_specs=pl.BlockSpec((team, 1, BIAS_ROWS * HEAD_DIM), lambda i: (0, 0, 0)),
        out_shape=jax.ShapeDtypeStruct((team, 1, BIAS_ROWS * HEAD_DIM), F32),
        compiler_params=params,
    )(got, far_back)
    biases = lax.all_to_all(
        bias_copies, ("outer",) + near_axes, split_axis=0, concat_axis=0, tiled=True
    )

    dq, dk, dv = pl.pallas_call(
        finish_kernel,
        out_shape=[
            jax.ShapeDtypeStruct((TOK, WIDTH), BF16),
            jax.ShapeDtypeStruct((TOK, HEAD_DIM), BF16),
            jax.ShapeDtypeStruct((TOK, HEAD_DIM), BF16),
        ],
        compiler_params=params,
    )(got, dq_own, far_back, near_back, cosk, sink)

    examples = team // (KV_HEADS * NEAR)
    summed = biases.reshape(examples, KV_HEADS, NEAR, BIAS_ROWS * HEAD_DIM).sum(axis=(0, 2))
    grad_bias = jnp.concatenate(
        [
            summed[:, :WIDTH].reshape(-1),
            summed[:, WIDTH : WIDTH + HEAD_DIM].reshape(-1),
            summed[:, WIDTH + HEAD_DIM :].reshape(-1),
        ]
    )
    return dq[None], dk[None], dv[None], grad_bias


def solution(mesh):
    fine = Mesh(mesh.devices.reshape(-1, RINGS, 2, 2), ("outer", "y", "xh", "core"))
    inner = ("y", "xh", "core")
    rows = P("outer", inner, None)
    placed = (
        rows,
        rows,
        rows,
        rows,
        rows,
        P("outer", None, inner),
        P(None, inner),
        P(None, inner, None),
    )
    return jax.shard_map(
        local, mesh=fine, in_specs=placed, out_specs=(rows, rows, rows, P()), check_vma=False
    )
```

```python
import math

import jax
import jax.numpy as jnp
from jax import lax
from jax.experimental import pallas as pl
from jax.experimental.pallas import tpu as pltpu
from jax.sharding import Mesh, PartitionSpec as P

HEADS = 28
KV_HEADS = 4
HEAD_DIM = 128
GROUP = HEADS // KV_HEADS
TOK = 128
ROPE_BASE = 1000000.0
HALF = HEAD_DIM // 2
SCALE = HEAD_DIM ** (-0.5)
LOG2E = math.log2(math.e)

RINGS = 8
NEAR = 4
BPC = 8
META = 16
LANES = GROUP * TOK
WIDTH = GROUP * HEAD_DIM
HEADSETS = [(0, 2), (2, 4), (4, 6), (6, 7)]
PACK = 2 * LANES + 48
BIAS_ROWS = GROUP + 2
ALL_ROWS = HEADS + 2 * KV_HEADS
TAIL = 48
TEAM = 64

F32 = jnp.float32
BF16 = jnp.bfloat16


def split(value, terms):
    parts = []
    for _ in range(terms):
        part = value.astype(BF16)
        parts.append(part)
        value = value - part.astype(F32)
    return parts


def pack_keys_kernel(seg_ref, k_ref, v_ref, kv_ref):
    seg = seg_ref[...]
    row = lax.broadcasted_iota(jnp.int32, (META, 2 * HEAD_DIM), 0)
    prompt = jnp.sum(jnp.where(seg == 0, 1.0, 0.0))
    chosen = jnp.sum(jnp.where(seg <= 1, 1.0, 0.0))
    meta = jnp.where(row == 0, prompt, jnp.where(row == 1, chosen, 0.0)).astype(BF16)
    keys = k_ref[...]
    values = v_ref[...]
    for y in range(RINGS):
        kv_ref[y, :TOK, :HEAD_DIM] = keys
        kv_ref[y, :TOK, HEAD_DIM:] = values
        kv_ref[y, TOK:, :] = meta


def pack_queries_kernel(q_ref, go_ref, ao_ref, norm_ref, seg_ref, unused_ref, pack_ref, ao_own, sems):
    copies = []
    for g in range(GROUP):
        here = slice(g * HEAD_DIM, (g + 1) * HEAD_DIM)
        rows = pl.ds(g * TOK, TOK)
        far_rows = pl.ds(LANES + g * TOK, TOK)
        trio = [
            pltpu.make_async_copy(go_ref.at[:, here], pack_ref.at[far_rows, :], sems.at[0, g]),
            pltpu.make_async_copy(ao_ref.at[:, here], ao_own.at[rows, :], sems.at[1, g]),
            pltpu.make_async_copy(q_ref.at[:, here], pack_ref.at[rows, :], sems.at[2, g]),
        ]
        for copy in trio:
            copy.start()
        copies.append(trio)
    seg = seg_ref[...]
    zero = jnp.zeros((1, TOK), F32)
    eight = lambda rows: jnp.concatenate(rows + [zero] * (8 - len(rows)), axis=0)
    norms = norm_ref[...] * LOG2E
    parts = split(eight([norms[g : g + 1, :] for g in range(GROUP)] + [seg.astype(F32)]), 3)
    deltas = []
    for g in range(GROUP):
        copies[g][0].wait()
        copies[g][1].wait()
        go = pack_ref[LANES + g * TOK : LANES + (g + 1) * TOK, :]
        product = go.astype(F32) * ao_own[g * TOK : (g + 1) * TOK, :].astype(F32)
        deltas.append(jnp.sum(product.T, axis=0, keepdims=True))
    parts += split(eight(deltas), 3)
    rows = jnp.concatenate([part.astype(F32) for part in parts], axis=0)
    pack_ref[2 * LANES :, :] = rows.astype(BF16)
    for g in range(GROUP):
        copies[g][2].wait()


def attention_kernel(
    kv_ref, pack0, pack1, pack2, pack3, cosq_ref, sinq_ref, cosr_ref, sinr_ref, cosc_ref, sinc_ref,
    dkv_ref, dq0, dq1, dq_far, bias_ref,
    pack, kv_acc, turned_sum, counts,
):
    part = pl.program_id(0)
    rows_in = BPC * TOK
    contract = (((1,), (1,)), ((), ()))

    @pl.when(part == 0)
    def _():
        for y in range(RINGS):
            meta = kv_ref[y, TOK:, :].astype(F32)
            counts[0, y] = jnp.max(meta[0:1, :]).astype(jnp.int32)
            counts[1, y] = jnp.max(meta[1:2, :]).astype(jnp.int32)
        turned_sum[...] = jnp.zeros_like(turned_sum)
        kv_acc[...] = jnp.zeros_like(kv_acc)

    for c, source in enumerate((pack0, pack1, pack2, pack3)):

        @pl.when(part == c)
        def _(source=source):
            pack[...] = source[...]

    extra = pack[2 * LANES :, :].astype(F32)
    norms = extra[0:8] + extra[8:16] + extra[16:24]
    deltas = extra[24:32] + extra[32:40] + extra[40:48]
    seg = norms[GROUP : GROUP + 1, :].astype(jnp.int32)
    across = lambda rows, g0, g1: jnp.concatenate([rows[g : g + 1, :] for g in range(g0, g1)], axis=1)
    at = lax.broadcasted_iota(jnp.int32, (TOK, TOK), 0)
    dq = jnp.zeros((HEAD_DIM, LANES), F32)
    for k in range(RINGS // BPC):
        blocks = pl.ds(k * BPC, BPC)
        keys = kv_ref[blocks, :TOK, :HEAD_DIM].reshape(rows_in, HEAD_DIM)
        values = kv_ref[blocks, :TOK, HEAD_DIM:].reshape(rows_in, HEAD_DIM)
        allowed = []
        for b in range(k * BPC, (k + 1) * BPC):
            c0, c1 = counts[0, b], counts[1, b]
            below = jnp.where(seg == 1, c1, c0)
            above = jnp.where(seg == 2, c1, TOK)
            allowed.append((at < below) | (at >= above))
        allowed = jnp.concatenate(allowed, axis=0)
        probs_low = []
        scores_low = []
        for g0, g1 in HEADSETS:
            there = slice(g0 * TOK, g1 * TOK)
            near = slice(LANES + g0 * TOK, LANES + g1 * TOK)
            scores = lax.dot_general(keys, pack[there, :], contract, preferred_element_type=F32)
            probs = jnp.exp2(scores * (SCALE * LOG2E) - across(norms, g0, g1))
            probs = jnp.where(jnp.concatenate([allowed] * (g1 - g0), axis=1), probs, 0.0)
            grad_probs = lax.dot_general(values, pack[near, :], contract, preferred_element_type=F32)
            scores_low.append((probs * (grad_probs - across(deltas, g0, g1))).astype(BF16))
            probs_low.append(probs.astype(BF16))
        scores_low = jnp.concatenate(scores_low, axis=1)
        probs_low = jnp.concatenate(probs_low, axis=1)
        dv = jnp.dot(probs_low, pack[LANES : 2 * LANES, :], preferred_element_type=F32)
        dk = jnp.dot(scores_low, pack[:LANES, :], preferred_element_type=F32)
        kv_acc[k * rows_in : (k + 1) * rows_in, :HEAD_DIM] += dk
        kv_acc[k * rows_in : (k + 1) * rows_in, HEAD_DIM:] += dv
        dq += jnp.dot(keys.T, scores_low, preferred_element_type=F32)

    cosine = jnp.concatenate([cosq_ref[part]] * GROUP, axis=1) * SCALE
    sine = jnp.concatenate([sinq_ref[part]] * GROUP, axis=1) * SCALE
    upper, lower = dq[:HALF], dq[HALF:]
    turned = jnp.concatenate(
        [upper * cosine + lower * sine, lower * cosine - upper * sine], axis=0
    )
    turned_sum[...] += turned
    for c, out in enumerate((dq0, dq1, dq_far.at[0], dq_far.at[1])):

        @pl.when(part == c)
        def _(out=out):
            out[...] = turned.astype(out.dtype)

    @pl.when(part == NEAR - 1)
    def _():
        u_all = jnp.zeros((1, HEAD_DIM), F32)
        w_all = jnp.zeros((1, HEAD_DIM), F32)
        v_all = jnp.zeros((1, HEAD_DIM), F32)
        for b in range(RINGS):
            total = kv_acc[b * TOK : (b + 1) * TOK, :]
            dkv_ref[b, :TOK, :] = total.astype(BF16)
            dk = total[:, :HEAD_DIM]
            u = jnp.sum(dk * cosr_ref[...], axis=0, keepdims=True)
            w = jnp.sum(dk * sinr_ref[...], axis=0, keepdims=True)
            c = cosc_ref[b : b + 1, :]
            s = sinc_ref[b : b + 1, :]
            u_all += u * c - w * s
            w_all += u * s + w * c
            v_all += jnp.sum(total[:, HEAD_DIM:], axis=0, keepdims=True)
        rows = []
        for g in range(GROUP):
            rows.append(jnp.sum(turned_sum[:, g * TOK : (g + 1) * TOK].T, axis=0, keepdims=True))
        u = u_all * SCALE
        w = w_all * SCALE
        rows.append(u + jnp.concatenate([w[:, HALF:], -w[:, :HALF]], axis=1))
        rows.append(v_all)
        for r, row in enumerate(rows):
            bias_ref[:, :, r * HEAD_DIM : (r + 1) * HEAD_DIM] = jnp.broadcast_to(
                row[None], (TEAM, 1, HEAD_DIM)
            )


def attend(kv, packs, cosq, sinq, cosr, sinr, cosc, sinc):
    vmem = pl.BlockSpec(memory_space=pltpu.VMEM)
    return pl.pallas_call(
        attention_kernel,
        grid=(NEAR,),
        in_specs=[vmem] * 11,
        out_specs=[vmem]
        + [pl.BlockSpec((HEAD_DIM, LANES), lambda i: (0, 0))] * 2
        + [vmem] * 2,
        out_shape=[
            jax.ShapeDtypeStruct((RINGS, TOK + TAIL, 2 * HEAD_DIM), BF16),
            pltpu.HBM((HEAD_DIM, LANES), F32),
            pltpu.HBM((HEAD_DIM, LANES), F32),
            jax.ShapeDtypeStruct((2, HEAD_DIM, LANES), BF16),
            jax.ShapeDtypeStruct((TEAM, 1, BIAS_ROWS * HEAD_DIM), F32),
        ],
        scratch_shapes=[
            pltpu.VMEM((PACK, TOK), BF16),
            pltpu.VMEM((RINGS * TOK, 2 * HEAD_DIM), F32),
            pltpu.VMEM((HEAD_DIM, LANES), F32),
            pltpu.SMEM((2, RINGS), jnp.int32),
        ],
        compiler_params=pltpu.CompilerParams(vmem_limit_bytes=24 << 20),
    )(kv, *packs, cosq, sinq, cosr, sinr, cosc, sinc)


def merge_kernel(bias_ref, dkv_ref, unused_ref, out_ref, tail, sems):
    per_pair = jnp.sum(bias_ref[...].reshape(TEAM // NEAR, NEAR, BIAS_ROWS * HEAD_DIM), axis=1)
    groups = TEAM // (NEAR * KV_HEADS)
    heads = []
    for c in range(KV_HEADS):
        total = per_pair[c : c + 1, :]
        for e in range(1, groups):
            row = e * KV_HEADS + c
            total = total + per_pair[row : row + 1, :]
        heads.append(total)
    piece = lambda c, r: heads[c][:, r * HEAD_DIM : (r + 1) * HEAD_DIM]
    rows = [piece(c, g) for c in range(KV_HEADS) for g in range(GROUP)]
    rows += [piece(c, GROUP) for c in range(KV_HEADS)]
    rows += [piece(c, GROUP + 1) for c in range(KV_HEADS)]
    rows.append(jnp.zeros((TAIL - ALL_ROWS, HEAD_DIM), F32))
    tail[...] = jnp.concatenate(split(jnp.concatenate(rows, axis=0), 2), axis=1)
    copies = []
    for y in range(RINGS):
        copy = pltpu.make_async_copy(tail, out_ref.at[y, pl.ds(TOK, TAIL), :], sems.at[y])
        copy.start()
        copies.append(copy)
    for copy in copies:
        copy.wait()


def add_kernel(own_ref, far_ref, out_ref):
    out_ref[...] = own_ref[...] + far_ref[1].astype(F32)


def finish_kernel(got_ref, dq_own, dq_far, dq_near, cosk_ref, sink_ref, dq_ref, dk_ref, dv_ref, bias_ref):
    tail = jnp.sum(got_ref[:, TOK:, :].astype(F32), axis=0)
    bias_ref[...] = (tail[:, :HEAD_DIM] + tail[:, HEAD_DIM:])[:ALL_ROWS]
    total = jnp.sum(got_ref[:, :TOK, :].astype(F32), axis=0)
    dv_ref[...] = total[:, HEAD_DIM:].astype(BF16)
    a = total[:, :HALF] * SCALE
    b = total[:, HALF:HEAD_DIM] * SCALE
    cosine = cosk_ref[...]
    sine = sink_ref[...]
    dk_ref[...] = jnp.concatenate([a * cosine + b * sine, b * cosine - a * sine], axis=1).astype(BF16)
    for g in range(GROUP):
        there = slice(g * TOK, (g + 1) * TOK)
        value = dq_own[:, there] + (dq_far[0, :, there].astype(F32) + dq_near[:, there])
        dq_ref[:, g * HEAD_DIM : (g + 1) * HEAD_DIM] = value.T.astype(BF16)


def local(query_rot, key_rot, value_rows, attention_out, grad_out, log_norm, segments, block_table):
    near_axes = ("xh", "core")
    y = lax.axis_index("y")
    near = lax.axis_index(near_axes)
    outer = lax.axis_index("outer")
    example = outer // KV_HEADS
    seg = lax.dynamic_index_in_dim(segments, example, 0, keepdims=True)
    params = pltpu.CompilerParams(vmem_limit_bytes=8 << 20)

    kv_copies = pl.pallas_call(
        pack_keys_kernel,
        out_shape=jax.ShapeDtypeStruct((RINGS, TOK + META, 2 * HEAD_DIM), BF16),
        compiler_params=params,
    )(seg, key_rot[0], value_rows[0])
    kv = lax.all_to_all(kv_copies, "y", split_axis=0, concat_axis=0, tiled=True)
    vmem = pl.BlockSpec(memory_space=pltpu.VMEM)
    hbm = pl.BlockSpec(memory_space=pltpu.HBM)
    anywhere = pl.BlockSpec(memory_space=pl.ANY)
    pack = pl.pallas_call(
        pack_queries_kernel,
        in_specs=[hbm, hbm, hbm, vmem, vmem, anywhere],
        out_shape=jax.ShapeDtypeStruct((PACK, TOK), BF16),
        scratch_shapes=[pltpu.VMEM((LANES, TOK), BF16), pltpu.SemaphoreType.DMA((3, GROUP))],
        compiler_params=params,
    )(query_rot[0], grad_out[0], attention_out[0], log_norm[0], seg, kv_copies)

    def swap(value, bits):
        return lax.ppermute(value, near_axes, [(i, i ^ bits) for i in range(NEAR)])

    far = swap(pack, 2)
    pack, far = lax.optimization_barrier((pack, far))
    packs = [pack, swap(pack, 1), far, swap(far, 1)]

    frequency = jnp.exp(
        jnp.arange(HALF, dtype=F32) * (-2.0 * math.log(ROPE_BASE) / HEAD_DIM)
    )
    inside = jnp.arange(TOK, dtype=jnp.int32)
    blocks = y * NEAR + jnp.bitwise_xor(near, jnp.arange(NEAR, dtype=jnp.int32))
    positions = (blocks[:, None] * TOK + inside[None, :]).astype(F32)
    angles = frequency[None, :, None] * positions[:, None, :]
    cosq, sinq = jnp.cos(angles), jnp.sin(angles)
    doubled = jnp.concatenate([frequency, frequency])[None, :]
    within = inside.astype(F32)[:, None] * doubled
    starts = ((jnp.arange(RINGS, dtype=jnp.int32) * NEAR + near) * TOK).astype(F32)
    across = starts[:, None] * doubled
    mine = positions[0][:, None] * frequency[None, :]
    cosk, sink = jnp.cos(mine), jnp.sin(mine)

    dkv, dq_own, dq_near, dq_far, bias = attend(
        kv, packs, cosq, sinq, jnp.cos(within), jnp.sin(within), jnp.cos(across), jnp.sin(across)
    )

    far_back = swap(dq_far, 2)
    biases = lax.all_to_all(
        bias, ("outer",) + near_axes, split_axis=0, concat_axis=0, tiled=True
    )
    dkv = pl.pallas_call(
        merge_kernel,
        in_specs=[vmem, anywhere, anywhere],
        out_specs=anywhere,
        out_shape=jax.ShapeDtypeStruct(dkv.shape, BF16),
        scratch_shapes=[pltpu.VMEM((TAIL, 2 * HEAD_DIM), BF16), pltpu.SemaphoreType.DMA((RINGS,))],
        input_output_aliases={1: 0},
        compiler_params=params,
    )(biases, dkv, far_back)
    got = lax.all_to_all(dkv, "y", split_axis=0, concat_axis=0, tiled=True)
    near_sum = pl.pallas_call(
        add_kernel,
        out_shape=jax.ShapeDtypeStruct((HEAD_DIM, LANES), F32),
        compiler_params=params,
    )(dq_near, far_back)
    near_back = swap(near_sum, 1)

    dq, dk, dv, grad_bias = pl.pallas_call(
        finish_kernel,
        out_shape=[
            jax.ShapeDtypeStruct((TOK, WIDTH), BF16),
            jax.ShapeDtypeStruct((TOK, HEAD_DIM), BF16),
            jax.ShapeDtypeStruct((TOK, HEAD_DIM), BF16),
            jax.ShapeDtypeStruct((ALL_ROWS, HEAD_DIM), F32),
        ],
        compiler_params=params,
    )(got, dq_own, far_back, near_back, cosk, sink)
    return dq[None], dk[None], dv[None], grad_bias.reshape(-1)


def solution(mesh):
    fine = Mesh(mesh.devices.reshape(-1, RINGS, 2, 2), ("outer", "y", "xh", "core"))
    inner = ("y", "xh", "core")
    rows = P("outer", inner, None)
    placed = (
        rows,
        rows,
        rows,
        rows,
        rows,
        P("outer", None, inner),
        P(None, inner),
        P(None, inner, None),
    )
    return jax.shard_map(
        local, mesh=fine, in_specs=placed, out_specs=(rows, rows, rows, P()), check_vma=False
    )
```

```python
import math

import jax
import jax.numpy as jnp
from jax import lax
from jax.experimental import pallas as pl
from jax.experimental.pallas import tpu as pltpu
from jax.sharding import Mesh, PartitionSpec as P

HEADS = 28
KV_HEADS = 4
HEAD_DIM = 128
GROUP = HEADS // KV_HEADS
TOK = 128
ROPE_BASE = 1000000.0
HALF = HEAD_DIM // 2
SCALE = HEAD_DIM ** (-0.5)
LOG2E = math.log2(math.e)

RINGS = 8
NEAR = 4
BPC = 8
META = 16
LANES = GROUP * TOK
WIDTH = GROUP * HEAD_DIM
HEADSETS = [(0, 2), (2, 4), (4, 6), (6, 7)]
PACK = 2 * LANES + 48
BIAS_ROWS = GROUP + 2

F32 = jnp.float32
BF16 = jnp.bfloat16


def split(value, terms):
    parts = []
    for _ in range(terms):
        part = value.astype(BF16)
        parts.append(part)
        value = value - part.astype(F32)
    return parts


def pack_keys_kernel(seg_ref, k_ref, v_ref, kv_ref, meta, sems):
    copies = []
    for y in range(RINGS):
        for i, source in enumerate((k_ref, v_ref)):
            there = kv_ref.at[y, pl.ds(0, TOK), pl.ds(i * HEAD_DIM, HEAD_DIM)]
            copies.append(pltpu.make_async_copy(source, there, sems.at[i, y]))
            copies[-1].start()
    seg = seg_ref[...]
    row = lax.broadcasted_iota(jnp.int32, (META, 2 * HEAD_DIM), 0)
    prompt = jnp.sum(jnp.where(seg == 0, 1.0, 0.0))
    chosen = jnp.sum(jnp.where(seg <= 1, 1.0, 0.0))
    meta[...] = jnp.where(row == 0, prompt, jnp.where(row == 1, chosen, 0.0)).astype(BF16)
    for y in range(RINGS):
        copies.append(pltpu.make_async_copy(meta, kv_ref.at[y, pl.ds(TOK, META), :], sems.at[2, y]))
        copies[-1].start()
    for copy in copies:
        copy.wait()


def pack_queries_kernel(q_ref, go_ref, ao_ref, norm_ref, seg_ref, unused_ref, pack_ref, ao_own, sems):
    copies = []
    for g in range(GROUP):
        here = slice(g * HEAD_DIM, (g + 1) * HEAD_DIM)
        rows = pl.ds(g * TOK, TOK)
        far_rows = pl.ds(LANES + g * TOK, TOK)
        trio = [
            pltpu.make_async_copy(go_ref.at[:, here], pack_ref.at[far_rows, :], sems.at[0, g]),
            pltpu.make_async_copy(ao_ref.at[:, here], ao_own.at[rows, :], sems.at[1, g]),
            pltpu.make_async_copy(q_ref.at[:, here], pack_ref.at[rows, :], sems.at[2, g]),
        ]
        for copy in trio:
            copy.start()
        copies.append(trio)
    seg = seg_ref[...]
    zero = jnp.zeros((1, TOK), F32)
    eight = lambda rows: jnp.concatenate(rows + [zero] * (8 - len(rows)), axis=0)
    norms = norm_ref[...] * LOG2E
    parts = split(eight([norms[g : g + 1, :] for g in range(GROUP)] + [seg.astype(F32)]), 3)
    deltas = []
    for g in range(GROUP):
        copies[g][0].wait()
        copies[g][1].wait()
        go = pack_ref[LANES + g * TOK : LANES + (g + 1) * TOK, :]
        product = go.astype(F32) * ao_own[g * TOK : (g + 1) * TOK, :].astype(F32)
        deltas.append(jnp.sum(product.T, axis=0, keepdims=True))
    parts += split(eight(deltas), 3)
    rows = jnp.concatenate([part.astype(F32) for part in parts], axis=0)
    pack_ref[2 * LANES :, :] = rows.astype(BF16)
    for g in range(GROUP):
        copies[g][2].wait()


def attention_kernel(
    kv_ref, pack0, pack1, pack2, pack3, cosq_ref, sinq_ref, cosr_ref, sinr_ref, cosc_ref, sinc_ref,
    dkv_ref, dq0, dq1, dq_far,
    pack, kv_acc, turned_sum, counts,
):
    part = pl.program_id(0)
    rows_in = BPC * TOK
    contract = (((1,), (1,)), ((), ()))

    @pl.when(part == 0)
    def _():
        for y in range(RINGS):
            meta = kv_ref[y, TOK:, :].astype(F32)
            counts[0, y] = jnp.max(meta[0:1, :]).astype(jnp.int32)
            counts[1, y] = jnp.max(meta[1:2, :]).astype(jnp.int32)
        turned_sum[...] = jnp.zeros_like(turned_sum)
        kv_acc[...] = jnp.zeros_like(kv_acc)

    for c, source in enumerate((pack0, pack1, pack2, pack3)):

        @pl.when(part == c)
        def _(source=source):
            pack[...] = source[...]

    extra = pack[2 * LANES :, :].astype(F32)
    norms = extra[0:8] + extra[8:16] + extra[16:24]
    deltas = extra[24:32] + extra[32:40] + extra[40:48]
    seg = norms[GROUP : GROUP + 1, :].astype(jnp.int32)
    across = lambda rows, g0, g1: jnp.concatenate([rows[g : g + 1, :] for g in range(g0, g1)], axis=1)
    at = lax.broadcasted_iota(jnp.int32, (TOK, TOK), 0)
    dq = jnp.zeros((HEAD_DIM, LANES), F32)
    for k in range(RINGS // BPC):
        blocks = pl.ds(k * BPC, BPC)
        keys = kv_ref[blocks, :TOK, :HEAD_DIM].reshape(rows_in, HEAD_DIM)
        values = kv_ref[blocks, :TOK, HEAD_DIM:].reshape(rows_in, HEAD_DIM)
        allowed = []
        for b in range(k * BPC, (k + 1) * BPC):
            c0, c1 = counts[0, b], counts[1, b]
            below = jnp.where(seg == 1, c1, c0)
            above = jnp.where(seg == 2, c1, TOK)
            allowed.append((at < below) | (at >= above))
        allowed = jnp.concatenate(allowed, axis=0)
        probs_low = []
        scores_low = []
        for g0, g1 in HEADSETS:
            there = slice(g0 * TOK, g1 * TOK)
            near = slice(LANES + g0 * TOK, LANES + g1 * TOK)
            scores = lax.dot_general(keys, pack[there, :], contract, preferred_element_type=F32)
            probs = jnp.exp2(scores * (SCALE * LOG2E) - across(norms, g0, g1))
            probs = jnp.where(jnp.concatenate([allowed] * (g1 - g0), axis=1), probs, 0.0)
            grad_probs = lax.dot_general(values, pack[near, :], contract, preferred_element_type=F32)
            scores_low.append((probs * (grad_probs - across(deltas, g0, g1))).astype(BF16))
            probs_low.append(probs.astype(BF16))
        scores_low = jnp.concatenate(scores_low, axis=1)
        probs_low = jnp.concatenate(probs_low, axis=1)
        dv = jnp.dot(probs_low, pack[LANES : 2 * LANES, :], preferred_element_type=F32)
        dk = jnp.dot(scores_low, pack[:LANES, :], preferred_element_type=F32)
        kv_acc[k * rows_in : (k + 1) * rows_in, :HEAD_DIM] += dk
        kv_acc[k * rows_in : (k + 1) * rows_in, HEAD_DIM:] += dv
        dq += jnp.dot(keys.T, scores_low, preferred_element_type=F32)

    cosine = jnp.concatenate([cosq_ref[part]] * GROUP, axis=1) * SCALE
    sine = jnp.concatenate([sinq_ref[part]] * GROUP, axis=1) * SCALE
    upper, lower = dq[:HALF], dq[HALF:]
    turned = jnp.concatenate(
        [upper * cosine + lower * sine, lower * cosine - upper * sine], axis=0
    )
    turned_sum[...] += turned
    for c, out in enumerate((dq0, dq1, dq_far.at[0], dq_far.at[1])):

        @pl.when(part == c)
        def _(out=out):
            out[...] = turned.astype(out.dtype)

    @pl.when(part == NEAR - 1)
    def _():
        u_all = jnp.zeros((1, HEAD_DIM), F32)
        w_all = jnp.zeros((1, HEAD_DIM), F32)
        v_all = jnp.zeros((1, HEAD_DIM), F32)
        for b in range(RINGS):
            total = kv_acc[b * TOK : (b + 1) * TOK, :]
            dkv_ref[b, :TOK, :] = total.astype(BF16)
            dk = total[:, :HEAD_DIM]
            u = jnp.sum(dk * cosr_ref[...], axis=0, keepdims=True)
            w = jnp.sum(dk * sinr_ref[...], axis=0, keepdims=True)
            c = cosc_ref[b : b + 1, :]
            s = sinc_ref[b : b + 1, :]
            u_all += u * c - w * s
            w_all += u * s + w * c
            v_all += jnp.sum(total[:, HEAD_DIM:], axis=0, keepdims=True)
        rows = []
        for g in range(GROUP):
            rows.append(jnp.sum(turned_sum[:, g * TOK : (g + 1) * TOK].T, axis=0, keepdims=True))
        u = u_all * SCALE
        w = w_all * SCALE
        rows.append(u + jnp.concatenate([w[:, HALF:], -w[:, :HALF]], axis=1))
        rows.append(v_all)
        rows.append(jnp.zeros((META - BIAS_ROWS, HEAD_DIM), F32))
        both = jnp.concatenate(split(jnp.concatenate(rows, axis=0), 2), axis=1)
        for y in range(RINGS):
            dkv_ref[y, TOK:, :] = both


def attend(kv, packs, cosq, sinq, cosr, sinr, cosc, sinc):
    vmem = pl.BlockSpec(memory_space=pltpu.VMEM)
    return pl.pallas_call(
        attention_kernel,
        grid=(NEAR,),
        in_specs=[vmem] * 11,
        out_specs=[vmem] + [pl.BlockSpec((HEAD_DIM, LANES), lambda i: (0, 0))] * 2 + [vmem],
        out_shape=[
            jax.ShapeDtypeStruct((RINGS, TOK + META, 2 * HEAD_DIM), BF16),
            pltpu.HBM((HEAD_DIM, LANES), F32),
            pltpu.HBM((HEAD_DIM, LANES), F32),
            jax.ShapeDtypeStruct((2, HEAD_DIM, LANES), BF16),
        ],
        scratch_shapes=[
            pltpu.VMEM((PACK, TOK), BF16),
            pltpu.VMEM((RINGS * TOK, 2 * HEAD_DIM), F32),
            pltpu.VMEM((HEAD_DIM, LANES), F32),
            pltpu.SMEM((2, RINGS), jnp.int32),
        ],
        compiler_params=pltpu.CompilerParams(vmem_limit_bytes=24 << 20),
    )(kv, *packs, cosq, sinq, cosr, sinr, cosc, sinc)


def bias_kernel(got_ref, unused_ref, out_ref):
    total = jnp.sum(got_ref[...].astype(F32), axis=0)
    total = total[:, :HEAD_DIM] + total[:, HEAD_DIM:]
    for r in range(BIAS_ROWS):
        row = total[r : r + 1, :]
        out_ref[:, :, r * HEAD_DIM : (r + 1) * HEAD_DIM] = jnp.broadcast_to(
            row[None], (out_ref.shape[0], 1, HEAD_DIM)
        )


def bias_sum_kernel(got_ref, out_ref):
    pairs = got_ref.shape[0] // NEAR
    per_pair = jnp.sum(got_ref[...].reshape(pairs, NEAR, BIAS_ROWS * HEAD_DIM), axis=1)
    for c in range(KV_HEADS):
        total = per_pair[c : c + 1, :]
        for row in range(c + KV_HEADS, pairs, KV_HEADS):
            total = total + per_pair[row : row + 1, :]
        for r in range(BIAS_ROWS):
            at = c * GROUP + r if r < GROUP else HEADS + (r - GROUP) * KV_HEADS + c
            out_ref[at : at + 1, :] = total[:, r * HEAD_DIM : (r + 1) * HEAD_DIM]


def add_kernel(own_ref, far_ref, out_ref):
    out_ref[...] = own_ref[...] + far_ref[1].astype(F32)


def finish_kernel(got_ref, dq_own, dq_far, dq_near, cosk_ref, sink_ref, dq_ref, dk_ref, dv_ref):
    total = jnp.sum(got_ref[:, :TOK, :].astype(F32), axis=0)
    dv_ref[...] = total[:, HEAD_DIM:].astype(BF16)
    a = total[:, :HALF] * SCALE
    b = total[:, HALF:HEAD_DIM] * SCALE
    cosine = cosk_ref[...]
    sine = sink_ref[...]
    dk_ref[...] = jnp.concatenate([a * cosine + b * sine, b * cosine - a * sine], axis=1).astype(BF16)
    for g in range(GROUP):
        there = slice(g * TOK, (g + 1) * TOK)
        value = dq_own[:, there] + (dq_far[0, :, there].astype(F32) + dq_near[:, there])
        dq_ref[:, g * HEAD_DIM : (g + 1) * HEAD_DIM] = value.T.astype(BF16)


def local(query_rot, key_rot, value_rows, attention_out, grad_out, log_norm, segments, block_table):
    near_axes = ("xh", "core")
    y = lax.axis_index("y")
    near = lax.axis_index(near_axes)
    outer = lax.axis_index("outer")
    example = outer // KV_HEADS
    seg = lax.dynamic_index_in_dim(segments, example, 0, keepdims=True)
    params = pltpu.CompilerParams(vmem_limit_bytes=8 << 20)

    vmem = pl.BlockSpec(memory_space=pltpu.VMEM)
    hbm = pl.BlockSpec(memory_space=pltpu.HBM)
    anywhere = pl.BlockSpec(memory_space=pl.ANY)
    kv_copies = pl.pallas_call(
        pack_keys_kernel,
        in_specs=[vmem, hbm, hbm],
        out_specs=hbm,
        out_shape=pltpu.HBM((RINGS, TOK + META, 2 * HEAD_DIM), BF16),
        scratch_shapes=[
            pltpu.VMEM((META, 2 * HEAD_DIM), BF16),
            pltpu.SemaphoreType.DMA((3, RINGS)),
        ],
        compiler_params=params,
    )(
        seg,
        pltpu.with_memory_space_constraint(key_rot[0], pltpu.HBM),
        pltpu.with_memory_space_constraint(value_rows[0], pltpu.HBM),
    )
    kv = lax.all_to_all(kv_copies, "y", split_axis=0, concat_axis=0, tiled=True)
    pack = pl.pallas_call(
        pack_queries_kernel,
        in_specs=[hbm, hbm, hbm, vmem, vmem, anywhere],
        out_shape=jax.ShapeDtypeStruct((PACK, TOK), BF16),
        scratch_shapes=[pltpu.VMEM((LANES, TOK), BF16), pltpu.SemaphoreType.DMA((3, GROUP))],
        compiler_params=params,
    )(query_rot[0], grad_out[0], attention_out[0], log_norm[0], seg, pltpu.with_memory_space_constraint(kv_copies, pltpu.HBM))

    def swap(value, bits):
        return lax.ppermute(value, near_axes, [(i, i ^ bits) for i in range(NEAR)])

    frequency = jnp.exp(
        jnp.arange(HALF, dtype=F32) * (-2.0 * math.log(ROPE_BASE) / HEAD_DIM)
    )
    inside = jnp.arange(TOK, dtype=jnp.int32)
    blocks = y * NEAR + jnp.bitwise_xor(near, jnp.arange(NEAR, dtype=jnp.int32))
    positions = (blocks[:, None] * TOK + inside[None, :]).astype(F32)
    angles = frequency[None, :, None] * positions[:, None, :]
    cosq, sinq = jnp.cos(angles), jnp.sin(angles)
    doubled = jnp.concatenate([frequency, frequency])[None, :]
    within = inside.astype(F32)[:, None] * doubled
    starts = ((jnp.arange(RINGS, dtype=jnp.int32) * NEAR + near) * TOK).astype(F32)
    across = starts[:, None] * doubled
    mine = positions[0][:, None] * frequency[None, :]
    cosk, sink = jnp.cos(mine), jnp.sin(mine)

    far = swap(pack, 2)
    pack_later, cosq = lax.optimization_barrier((pack, cosq))
    packs = [pack, swap(pack_later, 1), far, swap(far, 1)]

    dkv, dq_own, dq_near, dq_far = attend(
        kv, packs, cosq, sinq, jnp.cos(within), jnp.sin(within), jnp.cos(across), jnp.sin(across)
    )

    got = lax.all_to_all(dkv, "y", split_axis=0, concat_axis=0, tiled=True)
    far_back = swap(dq_far, 2)
    near_sum = pl.pallas_call(
        add_kernel,
        out_shape=jax.ShapeDtypeStruct((HEAD_DIM, LANES), F32),
        compiler_params=params,
    )(dq_near, far_back)
    near_back = swap(near_sum, 1)

    team = lax.axis_size("outer") * NEAR
    bias_copies = pl.pallas_call(
        bias_kernel,
        grid=(1,),
        in_specs=[
            pl.BlockSpec((RINGS, META, 2 * HEAD_DIM), lambda i: (0, TOK // META, 0)),
            anywhere,
        ],
        out_specs=pl.BlockSpec((team, 1, BIAS_ROWS * HEAD_DIM), lambda i: (0, 0, 0)),
        out_shape=jax.ShapeDtypeStruct((team, 1, BIAS_ROWS * HEAD_DIM), F32),
        compiler_params=params,
    )(got, far_back)
    biases = lax.all_to_all(
        bias_copies, ("outer",) + near_axes, split_axis=0, concat_axis=0, tiled=True
    )

    dq, dk, dv = pl.pallas_call(
        finish_kernel,
        out_shape=[
            jax.ShapeDtypeStruct((TOK, WIDTH), BF16),
            jax.ShapeDtypeStruct((TOK, HEAD_DIM), BF16),
            jax.ShapeDtypeStruct((TOK, HEAD_DIM), BF16),
        ],
        compiler_params=params,
    )(got, dq_own, far_back, near_back, cosk, sink)

    grad_bias = pl.pallas_call(
        bias_sum_kernel,
        out_shape=jax.ShapeDtypeStruct((HEADS + 2 * KV_HEADS, HEAD_DIM), F32),
        compiler_params=params,
    )(biases).reshape(-1)
    return dq[None], dk[None], dv[None], grad_bias


def solution(mesh):
    fine = Mesh(mesh.devices.reshape(-1, RINGS, 2, 2), ("outer", "y", "xh", "core"))
    inner = ("y", "xh", "core")
    rows = P("outer", inner, None)
    placed = (
        rows,
        rows,
        rows,
        rows,
        rows,
        P("outer", None, inner),
        P(None, inner),
        P(None, inner, None),
    )
    return jax.shard_map(
        local, mesh=fine, in_specs=placed, out_specs=(rows, rows, rows, P()), check_vma=False
    )
```

```python
import math

import jax
import jax.numpy as jnp
from jax import lax
from jax.experimental import pallas as pl
from jax.experimental.pallas import tpu as pltpu
from jax.sharding import Mesh, PartitionSpec as P

HEADS = 28
KV_HEADS = 4
HEAD_DIM = 128
GROUP = HEADS // KV_HEADS
TOK = 128
ROPE_BASE = 1000000.0
HALF = HEAD_DIM // 2
SCALE = HEAD_DIM ** (-0.5)
LOG2E = math.log2(math.e)

RINGS = 8
NEAR = 4
BPC = 8
META = 16
LANES = GROUP * TOK
WIDTH = GROUP * HEAD_DIM
HEADSETS = [(0, 2), (2, 4), (4, 6), (6, 7)]
PACK = 2 * LANES + 48
BIAS_ROWS = GROUP + 2

F32 = jnp.float32
BF16 = jnp.bfloat16


def split(value, terms):
    parts = []
    for _ in range(terms):
        part = value.astype(BF16)
        parts.append(part)
        value = value - part.astype(F32)
    return parts


def pack_keys_kernel(seg_ref, k_ref, v_ref, kv_ref, own, sems):
    loads = [
        pltpu.make_async_copy(k_ref, own.at[pl.ds(0, TOK), pl.ds(0, HEAD_DIM)], sems.at[0]),
        pltpu.make_async_copy(v_ref, own.at[pl.ds(0, TOK), pl.ds(HEAD_DIM, HEAD_DIM)], sems.at[1]),
    ]
    for copy in loads:
        copy.start()
    seg = seg_ref[...]
    row = lax.broadcasted_iota(jnp.int32, (META, 2 * HEAD_DIM), 0)
    prompt = jnp.sum(jnp.where(seg == 0, 1.0, 0.0))
    chosen = jnp.sum(jnp.where(seg <= 1, 1.0, 0.0))
    own[TOK:, :] = jnp.where(row == 0, prompt, jnp.where(row == 1, chosen, 0.0)).astype(BF16)
    for copy in loads:
        copy.wait()
    stores = [pltpu.make_async_copy(own, kv_ref.at[y], sems.at[2 + y]) for y in range(RINGS)]
    for copy in stores:
        copy.start()
    for copy in stores:
        copy.wait()


def pack_queries_kernel(q_ref, go_ref, ao_ref, norm_ref, seg_ref, unused_ref, pack_ref, ao_own, sems):
    copies = []
    for g in range(GROUP):
        here = slice(g * HEAD_DIM, (g + 1) * HEAD_DIM)
        rows = pl.ds(g * TOK, TOK)
        far_rows = pl.ds(LANES + g * TOK, TOK)
        trio = [
            pltpu.make_async_copy(go_ref.at[:, here], pack_ref.at[far_rows, :], sems.at[0, g]),
            pltpu.make_async_copy(ao_ref.at[:, here], ao_own.at[rows, :], sems.at[1, g]),
            pltpu.make_async_copy(q_ref.at[:, here], pack_ref.at[rows, :], sems.at[2, g]),
        ]
        for copy in trio:
            copy.start()
        copies.append(trio)
    seg = seg_ref[...]
    zero = jnp.zeros((1, TOK), F32)
    eight = lambda rows: jnp.concatenate(rows + [zero] * (8 - len(rows)), axis=0)
    norms = norm_ref[...] * LOG2E
    parts = split(eight([norms[g : g + 1, :] for g in range(GROUP)] + [seg.astype(F32)]), 3)
    deltas = []
    for g in range(GROUP):
        copies[g][0].wait()
        copies[g][1].wait()
        go = pack_ref[LANES + g * TOK : LANES + (g + 1) * TOK, :]
        product = go.astype(F32) * ao_own[g * TOK : (g + 1) * TOK, :].astype(F32)
        deltas.append(jnp.sum(product.T, axis=0, keepdims=True))
    parts += split(eight(deltas), 3)
    rows = jnp.concatenate([part.astype(F32) for part in parts], axis=0)
    pack_ref[2 * LANES :, :] = rows.astype(BF16)
    for g in range(GROUP):
        copies[g][2].wait()


def attention_kernel(
    kv_ref, pack0, pack1, pack2, pack3, cosq_ref, sinq_ref, cosr_ref, sinr_ref, cosc_ref, sinc_ref,
    dkv_ref, dq0, dq1, dq_far,
    pack, kv_acc, turned_sum, counts,
):
    part = pl.program_id(0)
    rows_in = BPC * TOK
    contract = (((1,), (1,)), ((), ()))

    @pl.when(part == 0)
    def _():
        for y in range(RINGS):
            meta = kv_ref[y, TOK:, :].astype(F32)
            counts[0, y] = jnp.max(meta[0:1, :]).astype(jnp.int32)
            counts[1, y] = jnp.max(meta[1:2, :]).astype(jnp.int32)
        turned_sum[...] = jnp.zeros_like(turned_sum)
        kv_acc[...] = jnp.zeros_like(kv_acc)

    for c, source in enumerate((pack0, pack1, pack2, pack3)):

        @pl.when(part == c)
        def _(source=source):
            pack[...] = source[...]

    extra = pack[2 * LANES :, :].astype(F32)
    norms = extra[0:8] + extra[8:16] + extra[16:24]
    deltas = extra[24:32] + extra[32:40] + extra[40:48]
    seg = norms[GROUP : GROUP + 1, :].astype(jnp.int32)
    across = lambda rows, g0, g1: jnp.concatenate([rows[g : g + 1, :] for g in range(g0, g1)], axis=1)
    at = lax.broadcasted_iota(jnp.int32, (TOK, TOK), 0)
    dq = jnp.zeros((HEAD_DIM, LANES), F32)
    for k in range(RINGS // BPC):
        blocks = pl.ds(k * BPC, BPC)
        keys = kv_ref[blocks, :TOK, :HEAD_DIM].reshape(rows_in, HEAD_DIM)
        values = kv_ref[blocks, :TOK, HEAD_DIM:].reshape(rows_in, HEAD_DIM)
        allowed = []
        for b in range(k * BPC, (k + 1) * BPC):
            c0, c1 = counts[0, b], counts[1, b]
            below = jnp.where(seg == 1, c1, c0)
            above = jnp.where(seg == 2, c1, TOK)
            allowed.append((at < below) | (at >= above))
        allowed = jnp.concatenate(allowed, axis=0)
        probs_low = []
        scores_low = []
        for g0, g1 in HEADSETS:
            there = slice(g0 * TOK, g1 * TOK)
            near = slice(LANES + g0 * TOK, LANES + g1 * TOK)
            scores = lax.dot_general(keys, pack[there, :], contract, preferred_element_type=F32)
            probs = jnp.exp2(scores * (SCALE * LOG2E) - across(norms, g0, g1))
            probs = jnp.where(jnp.concatenate([allowed] * (g1 - g0), axis=1), probs, 0.0)
            grad_probs = lax.dot_general(values, pack[near, :], contract, preferred_element_type=F32)
            scores_low.append((probs * (grad_probs - across(deltas, g0, g1))).astype(BF16))
            probs_low.append(probs.astype(BF16))
        scores_low = jnp.concatenate(scores_low, axis=1)
        probs_low = jnp.concatenate(probs_low, axis=1)
        dv = jnp.dot(probs_low, pack[LANES : 2 * LANES, :], preferred_element_type=F32)
        dk = jnp.dot(scores_low, pack[:LANES, :], preferred_element_type=F32)
        kv_acc[k * rows_in : (k + 1) * rows_in, :HEAD_DIM] += dk
        kv_acc[k * rows_in : (k + 1) * rows_in, HEAD_DIM:] += dv
        dq += jnp.dot(keys.T, scores_low, preferred_element_type=F32)

    cosine = jnp.concatenate([cosq_ref[part]] * GROUP, axis=1) * SCALE
    sine = jnp.concatenate([sinq_ref[part]] * GROUP, axis=1) * SCALE
    upper, lower = dq[:HALF], dq[HALF:]
    turned = jnp.concatenate(
        [upper * cosine + lower * sine, lower * cosine - upper * sine], axis=0
    )
    turned_sum[...] += turned
    for c, out in enumerate((dq0, dq1, dq_far.at[0], dq_far.at[1])):

        @pl.when(part == c)
        def _(out=out):
            out[...] = turned.astype(out.dtype)

    @pl.when(part == NEAR - 1)
    def _():
        u_all = jnp.zeros((1, HEAD_DIM), F32)
        w_all = jnp.zeros((1, HEAD_DIM), F32)
        v_all = jnp.zeros((1, HEAD_DIM), F32)
        for b in range(RINGS):
            total = kv_acc[b * TOK : (b + 1) * TOK, :]
            dkv_ref[b, :TOK, :] = total.astype(BF16)
            dk = total[:, :HEAD_DIM]
            u = jnp.sum(dk * cosr_ref[...], axis=0, keepdims=True)
            w = jnp.sum(dk * sinr_ref[...], axis=0, keepdims=True)
            c = cosc_ref[b : b + 1, :]
            s = sinc_ref[b : b + 1, :]
            u_all += u * c - w * s
            w_all += u * s + w * c
            v_all += jnp.sum(total[:, HEAD_DIM:], axis=0, keepdims=True)
        rows = []
        for g in range(GROUP):
            rows.append(jnp.sum(turned_sum[:, g * TOK : (g + 1) * TOK].T, axis=0, keepdims=True))
        u = u_all * SCALE
        w = w_all * SCALE
        rows.append(u + jnp.concatenate([w[:, HALF:], -w[:, :HALF]], axis=1))
        rows.append(v_all)
        rows.append(jnp.zeros((META - BIAS_ROWS, HEAD_DIM), F32))
        both = jnp.concatenate(split(jnp.concatenate(rows, axis=0), 2), axis=1)
        for y in range(RINGS):
            dkv_ref[y, TOK:, :] = both


def attend(kv, packs, cosq, sinq, cosr, sinr, cosc, sinc):
    vmem = pl.BlockSpec(memory_space=pltpu.VMEM)
    return pl.pallas_call(
        attention_kernel,
        grid=(NEAR,),
        in_specs=[vmem] * 11,
        out_specs=[vmem] + [pl.BlockSpec((HEAD_DIM, LANES), lambda i: (0, 0))] * 2 + [vmem],
        out_shape=[
            jax.ShapeDtypeStruct((RINGS, TOK + META, 2 * HEAD_DIM), BF16),
            pltpu.HBM((HEAD_DIM, LANES), F32),
            pltpu.HBM((HEAD_DIM, LANES), F32),
            jax.ShapeDtypeStruct((2, HEAD_DIM, LANES), BF16),
        ],
        scratch_shapes=[
            pltpu.VMEM((PACK, TOK), BF16),
            pltpu.VMEM((RINGS * TOK, 2 * HEAD_DIM), F32),
            pltpu.VMEM((HEAD_DIM, LANES), F32),
            pltpu.SMEM((2, RINGS), jnp.int32),
        ],
        compiler_params=pltpu.CompilerParams(vmem_limit_bytes=24 << 20),
    )(kv, *packs, cosq, sinq, cosr, sinr, cosc, sinc)


def bias_kernel(got_ref, unused_ref, out_ref):
    total = jnp.sum(got_ref[...].astype(F32), axis=0)
    total = total[:, :HEAD_DIM] + total[:, HEAD_DIM:]
    for r in range(BIAS_ROWS):
        row = total[r : r + 1, :]
        out_ref[:, :, r * HEAD_DIM : (r + 1) * HEAD_DIM] = jnp.broadcast_to(
            row[None], (out_ref.shape[0], 1, HEAD_DIM)
        )


def bias_sum_kernel(got_ref, out_ref):
    pairs = got_ref.shape[0] // NEAR
    per_pair = jnp.sum(got_ref[...].reshape(pairs, NEAR, BIAS_ROWS * HEAD_DIM), axis=1)
    for c in range(KV_HEADS):
        total = per_pair[c : c + 1, :]
        for row in range(c + KV_HEADS, pairs, KV_HEADS):
            total = total + per_pair[row : row + 1, :]
        for r in range(BIAS_ROWS):
            at = c * GROUP + r if r < GROUP else HEADS + (r - GROUP) * KV_HEADS + c
            out_ref[at : at + 1, :] = total[:, r * HEAD_DIM : (r + 1) * HEAD_DIM]


def add_kernel(own_ref, far_ref, out_ref):
    out_ref[...] = own_ref[...] + far_ref[1].astype(F32)


def finish_kernel(got_ref, dq_own, dq_far, dq_near, cosk_ref, sink_ref, dq_ref, dk_ref, dv_ref):
    total = jnp.sum(got_ref[:, :TOK, :].astype(F32), axis=0)
    dv_ref[...] = total[:, HEAD_DIM:].astype(BF16)
    a = total[:, :HALF] * SCALE
    b = total[:, HALF:HEAD_DIM] * SCALE
    cosine = cosk_ref[...]
    sine = sink_ref[...]
    dk_ref[...] = jnp.concatenate([a * cosine + b * sine, b * cosine - a * sine], axis=1).astype(BF16)
    for g in range(GROUP):
        there = slice(g * TOK, (g + 1) * TOK)
        value = dq_own[:, there] + (dq_far[0, :, there].astype(F32) + dq_near[:, there])
        dq_ref[:, g * HEAD_DIM : (g + 1) * HEAD_DIM] = value.T.astype(BF16)


def local(query_rot, key_rot, value_rows, attention_out, grad_out, log_norm, segments, block_table):
    near_axes = ("xh", "core")
    y = lax.axis_index("y")
    near = lax.axis_index(near_axes)
    outer = lax.axis_index("outer")
    example = outer // KV_HEADS
    seg = lax.dynamic_index_in_dim(segments, example, 0, keepdims=True)
    params = pltpu.CompilerParams(vmem_limit_bytes=8 << 20)

    vmem = pl.BlockSpec(memory_space=pltpu.VMEM)
    hbm = pl.BlockSpec(memory_space=pltpu.HBM)
    anywhere = pl.BlockSpec(memory_space=pl.ANY)
    kv_copies = pl.pallas_call(
        pack_keys_kernel,
        in_specs=[vmem, hbm, hbm],
        out_specs=hbm,
        out_shape=pltpu.HBM((RINGS, TOK + META, 2 * HEAD_DIM), BF16),
        scratch_shapes=[
            pltpu.VMEM((TOK + META, 2 * HEAD_DIM), BF16),
            pltpu.SemaphoreType.DMA((2 + RINGS,)),
        ],
        compiler_params=params,
    )(
        seg,
        pltpu.with_memory_space_constraint(key_rot[0], pltpu.HBM),
        pltpu.with_memory_space_constraint(value_rows[0], pltpu.HBM),
    )
    kv = lax.all_to_all(kv_copies, "y", split_axis=0, concat_axis=0, tiled=True)
    pack = pl.pallas_call(
        pack_queries_kernel,
        in_specs=[hbm, hbm, hbm, vmem, vmem, anywhere],
        out_shape=jax.ShapeDtypeStruct((PACK, TOK), BF16),
        scratch_shapes=[pltpu.VMEM((LANES, TOK), BF16), pltpu.SemaphoreType.DMA((3, GROUP))],
        compiler_params=params,
    )(query_rot[0], grad_out[0], attention_out[0], log_norm[0], seg, pltpu.with_memory_space_constraint(kv_copies, pltpu.HBM))

    def swap(value, bits):
        return lax.ppermute(value, near_axes, [(i, i ^ bits) for i in range(NEAR)])

    frequency = jnp.exp(
        jnp.arange(HALF, dtype=F32) * (-2.0 * math.log(ROPE_BASE) / HEAD_DIM)
    )
    inside = jnp.arange(TOK, dtype=jnp.int32)
    blocks = y * NEAR + jnp.bitwise_xor(near, jnp.arange(NEAR, dtype=jnp.int32))
    positions = (blocks[:, None] * TOK + inside[None, :]).astype(F32)
    angles = frequency[None, :, None] * positions[:, None, :]
    cosq, sinq = jnp.cos(angles), jnp.sin(angles)
    doubled = jnp.concatenate([frequency, frequency])[None, :]
    within = inside.astype(F32)[:, None] * doubled
    starts = ((jnp.arange(RINGS, dtype=jnp.int32) * NEAR + near) * TOK).astype(F32)
    across = starts[:, None] * doubled
    mine = positions[0][:, None] * frequency[None, :]
    cosk, sink = jnp.cos(mine), jnp.sin(mine)

    far = swap(pack, 2)
    pack_later, cosq = lax.optimization_barrier((pack, cosq))
    packs = [pack, swap(pack_later, 1), far, swap(far, 1)]

    dkv, dq_own, dq_near, dq_far = attend(
        kv, packs, cosq, sinq, jnp.cos(within), jnp.sin(within), jnp.cos(across), jnp.sin(across)
    )

    got = lax.all_to_all(dkv, "y", split_axis=0, concat_axis=0, tiled=True)
    far_back = swap(dq_far, 2)
    near_sum = pl.pallas_call(
        add_kernel,
        out_shape=jax.ShapeDtypeStruct((HEAD_DIM, LANES), F32),
        compiler_params=params,
    )(dq_near, far_back)
    near_back = swap(near_sum, 1)

    team = lax.axis_size("outer") * NEAR
    bias_copies = pl.pallas_call(
        bias_kernel,
        grid=(1,),
        in_specs=[
            pl.BlockSpec((RINGS, META, 2 * HEAD_DIM), lambda i: (0, TOK // META, 0)),
            anywhere,
        ],
        out_specs=pl.BlockSpec((team, 1, BIAS_ROWS * HEAD_DIM), lambda i: (0, 0, 0)),
        out_shape=jax.ShapeDtypeStruct((team, 1, BIAS_ROWS * HEAD_DIM), F32),
        compiler_params=params,
    )(got, far_back)
    biases = lax.all_to_all(
        bias_copies, ("outer",) + near_axes, split_axis=0, concat_axis=0, tiled=True
    )

    dq, dk, dv = pl.pallas_call(
        finish_kernel,
        out_shape=[
            jax.ShapeDtypeStruct((TOK, WIDTH), BF16),
            jax.ShapeDtypeStruct((TOK, HEAD_DIM), BF16),
            jax.ShapeDtypeStruct((TOK, HEAD_DIM), BF16),
        ],
        compiler_params=params,
    )(got, dq_own, far_back, near_back, cosk, sink)

    grad_bias = pl.pallas_call(
        bias_sum_kernel,
        out_shape=jax.ShapeDtypeStruct((HEADS + 2 * KV_HEADS, HEAD_DIM), F32),
        compiler_params=params,
    )(biases).reshape(-1)
    return dq[None], dk[None], dv[None], grad_bias


def solution(mesh):
    fine = Mesh(mesh.devices.reshape(-1, RINGS, 2, 2), ("outer", "y", "xh", "core"))
    inner = ("y", "xh", "core")
    rows = P("outer", inner, None)
    placed = (
        rows,
        rows,
        rows,
        rows,
        rows,
        P("outer", None, inner),
        P(None, inner),
        P(None, inner, None),
    )
    return jax.shard_map(
        local, mesh=fine, in_specs=placed, out_specs=(rows, rows, rows, P()), check_vma=False
    )
```

```python
import math

import jax
import jax.numpy as jnp
from jax import lax
from jax.experimental import pallas as pl
from jax.experimental.pallas import tpu as pltpu
from jax.sharding import Mesh, PartitionSpec as P

HEADS = 28
KV_HEADS = 4
HEAD_DIM = 128
GROUP = HEADS // KV_HEADS
TOK = 128
ROPE_BASE = 1000000.0
HALF = HEAD_DIM // 2
SCALE = HEAD_DIM ** (-0.5)
LOG2E = math.log2(math.e)

RINGS = 8
NEAR = 4
BPC = 8
META = 16
LANES = GROUP * TOK
WIDTH = GROUP * HEAD_DIM
HEADSETS = [(0, 2), (2, 4), (4, 6), (6, 7)]
PACK = 2 * LANES + 48
BIAS_ROWS = GROUP + 2
BIAS_COLS = 5

F32 = jnp.float32
BF16 = jnp.bfloat16


def split(value, terms):
    parts = []
    for _ in range(terms):
        part = value.astype(BF16)
        parts.append(part)
        value = value - part.astype(F32)
    return parts


def pack_keys_kernel(seg_ref, k_ref, v_ref, kv_ref, own, sems):
    loads = [
        pltpu.make_async_copy(k_ref, own.at[pl.ds(0, TOK), pl.ds(0, HEAD_DIM)], sems.at[0]),
        pltpu.make_async_copy(v_ref, own.at[pl.ds(0, TOK), pl.ds(HEAD_DIM, HEAD_DIM)], sems.at[1]),
    ]
    for copy in loads:
        copy.start()
    seg = seg_ref[...]
    row = lax.broadcasted_iota(jnp.int32, (META, 2 * HEAD_DIM), 0)
    prompt = jnp.sum(jnp.where(seg == 0, 1.0, 0.0))
    chosen = jnp.sum(jnp.where(seg <= 1, 1.0, 0.0))
    own[TOK:, :] = jnp.where(row == 0, prompt, jnp.where(row == 1, chosen, 0.0)).astype(BF16)
    for copy in loads:
        copy.wait()
    stores = [pltpu.make_async_copy(own, kv_ref.at[y], sems.at[2 + y]) for y in range(RINGS)]
    for copy in stores:
        copy.start()
    for copy in stores:
        copy.wait()


def pack_queries_kernel(q_ref, go_ref, ao_ref, norm_ref, seg_ref, unused_ref, pack_ref, ao_own, sems):
    copies = []
    for g in range(GROUP):
        here = slice(g * HEAD_DIM, (g + 1) * HEAD_DIM)
        rows = pl.ds(g * TOK, TOK)
        far_rows = pl.ds(LANES + g * TOK, TOK)
        trio = [
            pltpu.make_async_copy(go_ref.at[:, here], pack_ref.at[far_rows, :], sems.at[0, g]),
            pltpu.make_async_copy(ao_ref.at[:, here], ao_own.at[rows, :], sems.at[1, g]),
            pltpu.make_async_copy(q_ref.at[:, here], pack_ref.at[rows, :], sems.at[2, g]),
        ]
        for copy in trio:
            copy.start()
        copies.append(trio)
    seg = seg_ref[...]
    zero = jnp.zeros((1, TOK), F32)
    eight = lambda rows: jnp.concatenate(rows + [zero] * (8 - len(rows)), axis=0)
    norms = norm_ref[...] * LOG2E
    parts = split(eight([norms[g : g + 1, :] for g in range(GROUP)] + [seg.astype(F32)]), 3)
    deltas = []
    for g in range(GROUP):
        copies[g][0].wait()
        copies[g][1].wait()
        go = pack_ref[LANES + g * TOK : LANES + (g + 1) * TOK, :]
        product = go.astype(F32) * ao_own[g * TOK : (g + 1) * TOK, :].astype(F32)
        deltas.append(jnp.sum(product.T, axis=0, keepdims=True))
    parts += split(eight(deltas), 3)
    rows = jnp.concatenate([part.astype(F32) for part in parts], axis=0)
    pack_ref[2 * LANES :, :] = rows.astype(BF16)
    for g in range(GROUP):
        copies[g][2].wait()


def attention_kernel(
    kv_ref, pack0, pack1, pack2, pack3, cosq_ref, sinq_ref, cosr_ref, sinr_ref, cosc_ref, sinc_ref,
    dkv_ref, dq0, dq1, dq_far,
    pack, kv_acc, turned_sum, counts,
):
    part = pl.program_id(0)
    rows_in = BPC * TOK
    contract = (((1,), (1,)), ((), ()))

    @pl.when(part == 0)
    def _():
        for y in range(RINGS):
            meta = kv_ref[y, TOK:, :].astype(F32)
            counts[0, y] = jnp.max(meta[0:1, :]).astype(jnp.int32)
            counts[1, y] = jnp.max(meta[1:2, :]).astype(jnp.int32)
        turned_sum[...] = jnp.zeros_like(turned_sum)
        kv_acc[...] = jnp.zeros_like(kv_acc)

    for c, source in enumerate((pack0, pack1, pack2, pack3)):

        @pl.when(part == c)
        def _(source=source):
            pack[...] = source[...]

    extra = pack[2 * LANES :, :].astype(F32)
    norms = extra[0:8] + extra[8:16] + extra[16:24]
    deltas = extra[24:32] + extra[32:40] + extra[40:48]
    seg = norms[GROUP : GROUP + 1, :].astype(jnp.int32)
    across = lambda rows, g0, g1: jnp.concatenate([rows[g : g + 1, :] for g in range(g0, g1)], axis=1)
    at = lax.broadcasted_iota(jnp.int32, (TOK, TOK), 0)
    dq = jnp.zeros((HEAD_DIM, LANES), F32)
    for k in range(RINGS // BPC):
        blocks = pl.ds(k * BPC, BPC)
        keys = kv_ref[blocks, :TOK, :HEAD_DIM].reshape(rows_in, HEAD_DIM)
        values = kv_ref[blocks, :TOK, HEAD_DIM:].reshape(rows_in, HEAD_DIM)
        allowed = []
        for b in range(k * BPC, (k + 1) * BPC):
            c0, c1 = counts[0, b], counts[1, b]
            below = jnp.where(seg == 1, c1, c0)
            above = jnp.where(seg == 2, c1, TOK)
            allowed.append((at < below) | (at >= above))
        allowed = jnp.concatenate(allowed, axis=0)
        probs_low = []
        scores_low = []
        for g0, g1 in HEADSETS:
            there = slice(g0 * TOK, g1 * TOK)
            near = slice(LANES + g0 * TOK, LANES + g1 * TOK)
            scores = lax.dot_general(keys, pack[there, :], contract, preferred_element_type=F32)
            probs = jnp.exp2(scores * (SCALE * LOG2E) - across(norms, g0, g1))
            probs = jnp.where(jnp.concatenate([allowed] * (g1 - g0), axis=1), probs, 0.0)
            grad_probs = lax.dot_general(values, pack[near, :], contract, preferred_element_type=F32)
            scores_low.append((probs * (grad_probs - across(deltas, g0, g1))).astype(BF16))
            probs_low.append(probs.astype(BF16))
        scores_low = jnp.concatenate(scores_low, axis=1)
        probs_low = jnp.concatenate(probs_low, axis=1)
        dv = jnp.dot(probs_low, pack[LANES : 2 * LANES, :], preferred_element_type=F32)
        dk = jnp.dot(scores_low, pack[:LANES, :], preferred_element_type=F32)
        kv_acc[k * rows_in : (k + 1) * rows_in, :HEAD_DIM] += dk
        kv_acc[k * rows_in : (k + 1) * rows_in, HEAD_DIM:] += dv
        dq += jnp.dot(keys.T, scores_low, preferred_element_type=F32)

    cosine = jnp.concatenate([cosq_ref[part]] * GROUP, axis=1) * SCALE
    sine = jnp.concatenate([sinq_ref[part]] * GROUP, axis=1) * SCALE
    upper, lower = dq[:HALF], dq[HALF:]
    turned = jnp.concatenate(
        [upper * cosine + lower * sine, lower * cosine - upper * sine], axis=0
    )
    turned_sum[...] += turned
    for c, out in enumerate((dq0, dq1, dq_far.at[0], dq_far.at[1])):

        @pl.when(part == c)
        def _(out=out):
            out[...] = turned.astype(out.dtype)

    @pl.when(part == NEAR - 1)
    def _():
        u_all = jnp.zeros((1, HEAD_DIM), F32)
        w_all = jnp.zeros((1, HEAD_DIM), F32)
        v_all = jnp.zeros((1, HEAD_DIM), F32)
        for b in range(RINGS):
            total = kv_acc[b * TOK : (b + 1) * TOK, :]
            dkv_ref[b, :TOK, :] = total.astype(BF16)
            dk = total[:, :HEAD_DIM]
            u = jnp.sum(dk * cosr_ref[...], axis=0, keepdims=True)
            w = jnp.sum(dk * sinr_ref[...], axis=0, keepdims=True)
            c = cosc_ref[b : b + 1, :]
            s = sinc_ref[b : b + 1, :]
            u_all += u * c - w * s
            w_all += u * s + w * c
            v_all += jnp.sum(total[:, HEAD_DIM:], axis=0, keepdims=True)
        rows = []
        for g in range(GROUP):
            rows.append(jnp.sum(turned_sum[:, g * TOK : (g + 1) * TOK].T, axis=0, keepdims=True))
        u = u_all * SCALE
        w = w_all * SCALE
        rows.append(u + jnp.concatenate([w[:, HALF:], -w[:, :HALF]], axis=1))
        rows.append(v_all)
        rows.append(jnp.zeros((META - BIAS_ROWS, HEAD_DIM), F32))
        both = jnp.concatenate(split(jnp.concatenate(rows, axis=0), 2), axis=1)
        for y in range(RINGS):
            dkv_ref[y, TOK:, :] = both


def attend(kv, packs, cosq, sinq, cosr, sinr, cosc, sinc):
    vmem = pl.BlockSpec(memory_space=pltpu.VMEM)
    return pl.pallas_call(
        attention_kernel,
        grid=(NEAR,),
        in_specs=[vmem] * 11,
        out_specs=[vmem] + [pl.BlockSpec((HEAD_DIM, LANES), lambda i: (0, 0))] * 2 + [vmem],
        out_shape=[
            jax.ShapeDtypeStruct((RINGS, TOK + META, 2 * HEAD_DIM), BF16),
            pltpu.HBM((HEAD_DIM, LANES), F32),
            pltpu.HBM((HEAD_DIM, LANES), F32),
            jax.ShapeDtypeStruct((2, HEAD_DIM, LANES), BF16),
        ],
        scratch_shapes=[
            pltpu.VMEM((PACK, TOK), BF16),
            pltpu.VMEM((RINGS * TOK, 2 * HEAD_DIM), F32),
            pltpu.VMEM((HEAD_DIM, LANES), F32),
            pltpu.SMEM((2, RINGS), jnp.int32),
        ],
        compiler_params=pltpu.CompilerParams(vmem_limit_bytes=24 << 20),
    )(kv, *packs, cosq, sinq, cosr, sinr, cosc, sinc)


def bias_kernel(got_ref, unused_ref, out_ref):
    total = jnp.sum(got_ref[...].astype(F32), axis=0)
    total = total[:, :HEAD_DIM] + total[:, HEAD_DIM:]
    rows = [total[r : r + 1, :] for r in range(BIAS_ROWS)]
    rows.append(jnp.zeros((1, HEAD_DIM), F32))
    pair = jnp.concatenate(
        [
            jnp.concatenate(rows[:BIAS_COLS], axis=1),
            jnp.concatenate(rows[BIAS_COLS:], axis=1),
        ],
        axis=0,
    )
    out_ref[...] = jnp.broadcast_to(pair.astype(BF16)[None], out_ref.shape)


def bias_sum_kernel(got_ref, out_ref):
    pairs = got_ref.shape[0] // NEAR
    for c in range(KV_HEADS):
        total = None
        for row in range(c, pairs, KV_HEADS):
            part = jnp.sum(got_ref[row * NEAR : (row + 1) * NEAR].astype(F32), axis=0)
            total = part if total is None else total + part
        for r in range(BIAS_ROWS):
            at = c * GROUP + r if r < GROUP else HEADS + (r - GROUP) * KV_HEADS + c
            i, j = r // BIAS_COLS, r % BIAS_COLS
            out_ref[at : at + 1, :] = total[i : i + 1, j * HEAD_DIM : (j + 1) * HEAD_DIM]


def add_kernel(own_ref, far_ref, out_ref):
    out_ref[...] = own_ref[...] + far_ref[1].astype(F32)


def finish_kernel(got_ref, dq_own, dq_far, dq_near, cosk_ref, sink_ref, dq_ref, dk_ref, dv_ref):
    total = jnp.sum(got_ref[:, :TOK, :].astype(F32), axis=0)
    dv_ref[...] = total[:, HEAD_DIM:].astype(BF16)
    a = total[:, :HALF] * SCALE
    b = total[:, HALF:HEAD_DIM] * SCALE
    cosine = cosk_ref[...]
    sine = sink_ref[...]
    dk_ref[...] = jnp.concatenate([a * cosine + b * sine, b * cosine - a * sine], axis=1).astype(BF16)
    for g in range(GROUP):
        there = slice(g * TOK, (g + 1) * TOK)
        value = dq_own[:, there] + (dq_far[0, :, there].astype(F32) + dq_near[:, there])
        dq_ref[:, g * HEAD_DIM : (g + 1) * HEAD_DIM] = value.T.astype(BF16)


def local(query_rot, key_rot, value_rows, attention_out, grad_out, log_norm, segments, block_table):
    near_axes = ("xh", "core")
    y = lax.axis_index("y")
    near = lax.axis_index(near_axes)
    outer = lax.axis_index("outer")
    example = outer // KV_HEADS
    seg = lax.dynamic_index_in_dim(segments, example, 0, keepdims=True)
    params = pltpu.CompilerParams(vmem_limit_bytes=8 << 20)

    vmem = pl.BlockSpec(memory_space=pltpu.VMEM)
    hbm = pl.BlockSpec(memory_space=pltpu.HBM)
    anywhere = pl.BlockSpec(memory_space=pl.ANY)
    kv_copies = pl.pallas_call(
        pack_keys_kernel,
        in_specs=[vmem, hbm, hbm],
        out_specs=hbm,
        out_shape=pltpu.HBM((RINGS, TOK + META, 2 * HEAD_DIM), BF16),
        scratch_shapes=[
            pltpu.VMEM((TOK + META, 2 * HEAD_DIM), BF16),
            pltpu.SemaphoreType.DMA((2 + RINGS,)),
        ],
        compiler_params=params,
    )(
        seg,
        pltpu.with_memory_space_constraint(key_rot[0], pltpu.HBM),
        pltpu.with_memory_space_constraint(value_rows[0], pltpu.HBM),
    )
    kv = lax.all_to_all(kv_copies, "y", split_axis=0, concat_axis=0, tiled=True)
    pack = pl.pallas_call(
        pack_queries_kernel,
        in_specs=[hbm, hbm, hbm, vmem, vmem, anywhere],
        out_shape=jax.ShapeDtypeStruct((PACK, TOK), BF16),
        scratch_shapes=[pltpu.VMEM((LANES, TOK), BF16), pltpu.SemaphoreType.DMA((3, GROUP))],
        compiler_params=params,
    )(query_rot[0], grad_out[0], attention_out[0], log_norm[0], seg, pltpu.with_memory_space_constraint(kv_copies, pltpu.HBM))

    def swap(value, bits):
        return lax.ppermute(value, near_axes, [(i, i ^ bits) for i in range(NEAR)])

    frequency = jnp.exp(
        jnp.arange(HALF, dtype=F32) * (-2.0 * math.log(ROPE_BASE) / HEAD_DIM)
    )
    inside = jnp.arange(TOK, dtype=jnp.int32)
    blocks = y * NEAR + jnp.bitwise_xor(near, jnp.arange(NEAR, dtype=jnp.int32))
    positions = (blocks[:, None] * TOK + inside[None, :]).astype(F32)
    angles = frequency[None, :, None] * positions[:, None, :]
    cosq, sinq = jnp.cos(angles), jnp.sin(angles)
    doubled = jnp.concatenate([frequency, frequency])[None, :]
    within = inside.astype(F32)[:, None] * doubled
    starts = ((jnp.arange(RINGS, dtype=jnp.int32) * NEAR + near) * TOK).astype(F32)
    across = starts[:, None] * doubled
    mine = positions[0][:, None] * frequency[None, :]
    cosk, sink = jnp.cos(mine), jnp.sin(mine)

    far = swap(pack, 2)
    pack_later, cosq = lax.optimization_barrier((pack, cosq))
    packs = [pack, swap(pack_later, 1), far, swap(far, 1)]

    dkv, dq_own, dq_near, dq_far = attend(
        kv, packs, cosq, sinq, jnp.cos(within), jnp.sin(within), jnp.cos(across), jnp.sin(across)
    )

    got = lax.all_to_all(dkv, "y", split_axis=0, concat_axis=0, tiled=True)
    far_back = swap(dq_far, 2)
    near_sum = pl.pallas_call(
        add_kernel,
        out_shape=jax.ShapeDtypeStruct((HEAD_DIM, LANES), F32),
        compiler_params=params,
    )(dq_near, far_back)
    near_back = swap(near_sum, 1)

    team = lax.axis_size("outer") * NEAR
    bias_copies = pl.pallas_call(
        bias_kernel,
        grid=(1,),
        in_specs=[
            pl.BlockSpec((RINGS, META, 2 * HEAD_DIM), lambda i: (0, TOK // META, 0)),
            anywhere,
        ],
        out_specs=pl.BlockSpec((team, 2, BIAS_COLS * HEAD_DIM), lambda i: (0, 0, 0)),
        out_shape=jax.ShapeDtypeStruct((team, 2, BIAS_COLS * HEAD_DIM), BF16),
        compiler_params=params,
    )(got, far_back)
    biases = lax.all_to_all(
        bias_copies, ("outer",) + near_axes, split_axis=0, concat_axis=0, tiled=True
    )

    dq, dk, dv = pl.pallas_call(
        finish_kernel,
        out_shape=[
            jax.ShapeDtypeStruct((TOK, WIDTH), BF16),
            jax.ShapeDtypeStruct((TOK, HEAD_DIM), BF16),
            jax.ShapeDtypeStruct((TOK, HEAD_DIM), BF16),
        ],
        compiler_params=params,
    )(got, dq_own, far_back, near_back, cosk, sink)

    grad_bias = pl.pallas_call(
        bias_sum_kernel,
        out_shape=jax.ShapeDtypeStruct((HEADS + 2 * KV_HEADS, HEAD_DIM), F32),
        compiler_params=params,
    )(biases).reshape(-1)
    return dq[None], dk[None], dv[None], grad_bias


def solution(mesh):
    fine = Mesh(mesh.devices.reshape(-1, RINGS, 2, 2), ("outer", "y", "xh", "core"))
    inner = ("y", "xh", "core")
    rows = P("outer", inner, None)
    placed = (
        rows,
        rows,
        rows,
        rows,
        rows,
        P("outer", None, inner),
        P(None, inner),
        P(None, inner, None),
    )
    return jax.shard_map(
        local, mesh=fine, in_specs=placed, out_specs=(rows, rows, rows, P()), check_vma=False
    )
```

```python
import math

import jax
import jax.numpy as jnp
from jax import lax
from jax.experimental import pallas as pl
from jax.experimental.pallas import tpu as pltpu
from jax.sharding import Mesh, PartitionSpec as P

HEADS = 28
KV_HEADS = 4
HEAD_DIM = 128
GROUP = HEADS // KV_HEADS
TOK = 128
ROPE_BASE = 1000000.0
HALF = HEAD_DIM // 2
SCALE = HEAD_DIM ** (-0.5)
LOG2E = math.log2(math.e)

RINGS = 8
NEAR = 4
BPC = 8
META = 8
LANES = GROUP * TOK
WIDTH = GROUP * HEAD_DIM
HEADSETS = [(0, 2), (2, 4), (4, 6), (6, 7)]
PACK = 2 * LANES + 48
BIAS_ROWS = GROUP + 2
BIAS_COLS = 5

F32 = jnp.float32
BF16 = jnp.bfloat16


def split(value, terms):
    parts = []
    for _ in range(terms):
        part = value.astype(BF16)
        parts.append(part)
        value = value - part.astype(F32)
    return parts


def pack_keys_kernel(seg_ref, k_ref, v_ref, kv_ref, own, sems):
    loads = [
        pltpu.make_async_copy(k_ref, own.at[pl.ds(0, TOK), pl.ds(0, HEAD_DIM)], sems.at[0]),
        pltpu.make_async_copy(v_ref, own.at[pl.ds(0, TOK), pl.ds(HEAD_DIM, HEAD_DIM)], sems.at[1]),
    ]
    for copy in loads:
        copy.start()
    seg = seg_ref[...]
    row = lax.broadcasted_iota(jnp.int32, (META, 2 * HEAD_DIM), 0)
    prompt = jnp.sum(jnp.where(seg == 0, 1.0, 0.0))
    chosen = jnp.sum(jnp.where(seg <= 1, 1.0, 0.0))
    own[TOK:, :] = jnp.where(row == 0, prompt, jnp.where(row == 1, chosen, 0.0)).astype(BF16)
    for copy in loads:
        copy.wait()
    stores = [pltpu.make_async_copy(own, kv_ref.at[y], sems.at[2 + y]) for y in range(RINGS)]
    for copy in stores:
        copy.start()
    for copy in stores:
        copy.wait()


def pack_queries_kernel(q_ref, go_ref, ao_ref, norm_ref, seg_ref, unused_ref, pack_ref, ao_own, sems):
    copies = []
    for g in range(GROUP):
        here = slice(g * HEAD_DIM, (g + 1) * HEAD_DIM)
        rows = pl.ds(g * TOK, TOK)
        far_rows = pl.ds(LANES + g * TOK, TOK)
        trio = [
            pltpu.make_async_copy(go_ref.at[:, here], pack_ref.at[far_rows, :], sems.at[0, g]),
            pltpu.make_async_copy(ao_ref.at[:, here], ao_own.at[rows, :], sems.at[1, g]),
            pltpu.make_async_copy(q_ref.at[:, here], pack_ref.at[rows, :], sems.at[2, g]),
        ]
        for copy in trio:
            copy.start()
        copies.append(trio)
    seg = seg_ref[...]
    zero = jnp.zeros((1, TOK), F32)
    eight = lambda rows: jnp.concatenate(rows + [zero] * (8 - len(rows)), axis=0)
    norms = norm_ref[...] * LOG2E
    parts = split(eight([norms[g : g + 1, :] for g in range(GROUP)] + [seg.astype(F32)]), 3)
    deltas = []
    for g in range(GROUP):
        copies[g][0].wait()
        copies[g][1].wait()
        go = pack_ref[LANES + g * TOK : LANES + (g + 1) * TOK, :]
        product = go.astype(F32) * ao_own[g * TOK : (g + 1) * TOK, :].astype(F32)
        deltas.append(jnp.sum(product.T, axis=0, keepdims=True))
    parts += split(eight(deltas), 3)
    rows = jnp.concatenate([part.astype(F32) for part in parts], axis=0)
    pack_ref[2 * LANES :, :] = rows.astype(BF16)
    for g in range(GROUP):
        copies[g][2].wait()


def attention_kernel(
    kv_ref, pack0, pack1, pack2, pack3, cosq_ref, sinq_ref, cosr_ref, sinr_ref, cosc_ref, sinc_ref,
    dkv_ref, dq0, dq2, dq_near,
    pack, kv_acc, turned_sum, counts,
):
    part = pl.program_id(0)
    rows_in = BPC * TOK
    contract = (((1,), (1,)), ((), ()))

    @pl.when(part == 0)
    def _():
        for y in range(RINGS):
            meta = kv_ref[y, TOK:, :].astype(F32)
            counts[0, y] = jnp.max(meta[0:1, :]).astype(jnp.int32)
            counts[1, y] = jnp.max(meta[1:2, :]).astype(jnp.int32)
        turned_sum[...] = jnp.zeros_like(turned_sum)
        kv_acc[...] = jnp.zeros_like(kv_acc)

    for c, source in enumerate((pack0, pack1, pack2, pack3)):

        @pl.when(part == c)
        def _(source=source):
            pack[...] = source[...]

    extra = pack[2 * LANES :, :].astype(F32)
    norms = extra[0:8] + extra[8:16] + extra[16:24]
    deltas = extra[24:32] + extra[32:40] + extra[40:48]
    seg = norms[GROUP : GROUP + 1, :].astype(jnp.int32)
    across = lambda rows, g0, g1: jnp.concatenate([rows[g : g + 1, :] for g in range(g0, g1)], axis=1)
    at = lax.broadcasted_iota(jnp.int32, (TOK, TOK), 0)
    dq = jnp.zeros((HEAD_DIM, LANES), F32)
    for k in range(RINGS // BPC):
        blocks = pl.ds(k * BPC, BPC)
        keys = kv_ref[blocks, :TOK, :HEAD_DIM].reshape(rows_in, HEAD_DIM)
        values = kv_ref[blocks, :TOK, HEAD_DIM:].reshape(rows_in, HEAD_DIM)
        allowed = []
        for b in range(k * BPC, (k + 1) * BPC):
            c0, c1 = counts[0, b], counts[1, b]
            below = jnp.where(seg == 1, c1, c0)
            above = jnp.where(seg == 2, c1, TOK)
            allowed.append((at < below) | (at >= above))
        allowed = jnp.concatenate(allowed, axis=0)
        probs_low = []
        scores_low = []
        for g0, g1 in HEADSETS:
            there = slice(g0 * TOK, g1 * TOK)
            near = slice(LANES + g0 * TOK, LANES + g1 * TOK)
            scores = lax.dot_general(keys, pack[there, :], contract, preferred_element_type=F32)
            probs = jnp.exp2(scores * (SCALE * LOG2E) - across(norms, g0, g1))
            probs = jnp.where(jnp.concatenate([allowed] * (g1 - g0), axis=1), probs, 0.0)
            grad_probs = lax.dot_general(values, pack[near, :], contract, preferred_element_type=F32)
            scores_low.append((probs * (grad_probs - across(deltas, g0, g1))).astype(BF16))
            probs_low.append(probs.astype(BF16))
        scores_low = jnp.concatenate(scores_low, axis=1)
        probs_low = jnp.concatenate(probs_low, axis=1)
        dv = jnp.dot(probs_low, pack[LANES : 2 * LANES, :], preferred_element_type=F32)
        dk = jnp.dot(scores_low, pack[:LANES, :], preferred_element_type=F32)
        kv_acc[k * rows_in : (k + 1) * rows_in, :HEAD_DIM] += dk
        kv_acc[k * rows_in : (k + 1) * rows_in, HEAD_DIM:] += dv
        dq += jnp.dot(keys.T, scores_low, preferred_element_type=F32)

    cosine = jnp.concatenate([cosq_ref[part]] * GROUP, axis=1) * SCALE
    sine = jnp.concatenate([sinq_ref[part]] * GROUP, axis=1) * SCALE
    upper, lower = dq[:HALF], dq[HALF:]
    turned = jnp.concatenate(
        [upper * cosine + lower * sine, lower * cosine - upper * sine], axis=0
    )
    turned_sum[...] += turned
    for c, out in enumerate((dq0, dq_near.at[0], dq2, dq_near.at[1])):

        @pl.when(part == c)
        def _(out=out):
            out[...] = turned.astype(out.dtype)

    @pl.when(part == NEAR - 1)
    def _():
        u_all = jnp.zeros((1, HEAD_DIM), F32)
        w_all = jnp.zeros((1, HEAD_DIM), F32)
        v_all = jnp.zeros((1, HEAD_DIM), F32)
        for b in range(RINGS):
            total = kv_acc[b * TOK : (b + 1) * TOK, :]
            dkv_ref[b, :TOK, :] = total.astype(BF16)
            dk = total[:, :HEAD_DIM]
            u = jnp.sum(dk * cosr_ref[...], axis=0, keepdims=True)
            w = jnp.sum(dk * sinr_ref[...], axis=0, keepdims=True)
            c = cosc_ref[b : b + 1, :]
            s = sinc_ref[b : b + 1, :]
            u_all += u * c - w * s
            w_all += u * s + w * c
            v_all += jnp.sum(total[:, HEAD_DIM:], axis=0, keepdims=True)
        rows = []
        for g in range(GROUP):
            rows.append(jnp.sum(turned_sum[:, g * TOK : (g + 1) * TOK].T, axis=0, keepdims=True))
        u = u_all * SCALE
        w = w_all * SCALE
        rows.append(u + jnp.concatenate([w[:, HALF:], -w[:, :HALF]], axis=1))
        rows.append(v_all)
        spare = jnp.concatenate(rows[META:] + [jnp.zeros((2 * META - BIAS_ROWS, HEAD_DIM), F32)], axis=0)
        both = jnp.concatenate([jnp.concatenate(rows[:META], axis=0), spare], axis=1).astype(BF16)
        for y in range(RINGS):
            dkv_ref[y, TOK:, :] = both


def attend(kv, packs, cosq, sinq, cosr, sinr, cosc, sinc):
    vmem = pl.BlockSpec(memory_space=pltpu.VMEM)
    return pl.pallas_call(
        attention_kernel,
        grid=(NEAR,),
        in_specs=[vmem] * 11,
        out_specs=[vmem] + [pl.BlockSpec((HEAD_DIM, LANES), lambda i: (0, 0))] * 2 + [vmem],
        out_shape=[
            jax.ShapeDtypeStruct((RINGS, TOK + META, 2 * HEAD_DIM), BF16),
            pltpu.HBM((HEAD_DIM, LANES), F32),
            pltpu.HBM((HEAD_DIM, LANES), F32),
            jax.ShapeDtypeStruct((2, HEAD_DIM, LANES), BF16),
        ],
        scratch_shapes=[
            pltpu.VMEM((PACK, TOK), BF16),
            pltpu.VMEM((RINGS * TOK, 2 * HEAD_DIM), F32),
            pltpu.VMEM((HEAD_DIM, LANES), F32),
            pltpu.SMEM((2, RINGS), jnp.int32),
        ],
        compiler_params=pltpu.CompilerParams(vmem_limit_bytes=24 << 20),
    )(kv, *packs, cosq, sinq, cosr, sinr, cosc, sinc)


def bias_kernel(got_ref, unused_ref, out_ref):
    total = jnp.sum(got_ref[...].astype(F32), axis=0)
    total = jnp.concatenate([total[:, :HEAD_DIM], total[:, HEAD_DIM:]], axis=0)
    rows = [total[r : r + 1, :] for r in range(BIAS_ROWS)]
    rows.append(jnp.zeros((1, HEAD_DIM), F32))
    pair = jnp.concatenate(
        [
            jnp.concatenate(rows[:BIAS_COLS], axis=1),
            jnp.concatenate(rows[BIAS_COLS:], axis=1),
        ],
        axis=0,
    )
    out_ref[...] = jnp.broadcast_to(pair.astype(BF16)[None], out_ref.shape)


def bias_sum_kernel(got_ref, out_ref):
    pairs = got_ref.shape[0] // NEAR
    for c in range(KV_HEADS):
        total = None
        for row in range(c, pairs, KV_HEADS):
            part = jnp.sum(got_ref[row * NEAR : (row + 1) * NEAR].astype(F32), axis=0)
            total = part if total is None else total + part
        for r in range(BIAS_ROWS):
            at = c * GROUP + r if r < GROUP else HEADS + (r - GROUP) * KV_HEADS + c
            i, j = r // BIAS_COLS, r % BIAS_COLS
            out_ref[at : at + 1, :] = total[i : i + 1, j * HEAD_DIM : (j + 1) * HEAD_DIM]


def add_kernel(far_ref, near_ref, out_ref):
    out_ref[...] = (far_ref[...] + near_ref[1].astype(F32)).astype(BF16)


def finish_kernel(got_ref, dq_own, dq_near, dq_far, cosk_ref, sink_ref, dq_ref, dk_ref, dv_ref):
    total = jnp.sum(got_ref[:, :TOK, :].astype(F32), axis=0)
    dv_ref[...] = total[:, HEAD_DIM:].astype(BF16)
    a = total[:, :HALF] * SCALE
    b = total[:, HALF:HEAD_DIM] * SCALE
    cosine = cosk_ref[...]
    sine = sink_ref[...]
    dk_ref[...] = jnp.concatenate([a * cosine + b * sine, b * cosine - a * sine], axis=1).astype(BF16)
    for g in range(GROUP):
        there = slice(g * TOK, (g + 1) * TOK)
        value = dq_own[:, there] + (dq_near[0, :, there].astype(F32) + dq_far[:, there].astype(F32))
        dq_ref[:, g * HEAD_DIM : (g + 1) * HEAD_DIM] = value.T.astype(BF16)


def local(query_rot, key_rot, value_rows, attention_out, grad_out, log_norm, segments, block_table):
    near_axes = ("xh", "core")
    y = lax.axis_index("y")
    near = lax.axis_index(near_axes)
    outer = lax.axis_index("outer")
    example = outer // KV_HEADS
    seg = lax.dynamic_index_in_dim(segments, example, 0, keepdims=True)
    params = pltpu.CompilerParams(vmem_limit_bytes=8 << 20)

    vmem = pl.BlockSpec(memory_space=pltpu.VMEM)
    hbm = pl.BlockSpec(memory_space=pltpu.HBM)
    anywhere = pl.BlockSpec(memory_space=pl.ANY)
    kv_copies = pl.pallas_call(
        pack_keys_kernel,
        in_specs=[vmem, hbm, hbm],
        out_specs=hbm,
        out_shape=pltpu.HBM((RINGS, TOK + META, 2 * HEAD_DIM), BF16),
        scratch_shapes=[
            pltpu.VMEM((TOK + META, 2 * HEAD_DIM), BF16),
            pltpu.SemaphoreType.DMA((2 + RINGS,)),
        ],
        compiler_params=params,
    )(
        seg,
        pltpu.with_memory_space_constraint(key_rot[0], pltpu.HBM),
        pltpu.with_memory_space_constraint(value_rows[0], pltpu.HBM),
    )
    kv = lax.all_to_all(kv_copies, "y", split_axis=0, concat_axis=0, tiled=True)
    pack = pl.pallas_call(
        pack_queries_kernel,
        in_specs=[hbm, hbm, hbm, vmem, vmem, anywhere],
        out_shape=jax.ShapeDtypeStruct((PACK, TOK), BF16),
        scratch_shapes=[pltpu.VMEM((LANES, TOK), BF16), pltpu.SemaphoreType.DMA((3, GROUP))],
        compiler_params=params,
    )(query_rot[0], grad_out[0], attention_out[0], log_norm[0], seg, pltpu.with_memory_space_constraint(kv_copies, pltpu.HBM))

    def swap(value, bits):
        return lax.ppermute(value, near_axes, [(i, i ^ bits) for i in range(NEAR)])

    frequency = jnp.exp(
        jnp.arange(HALF, dtype=F32) * (-2.0 * math.log(ROPE_BASE) / HEAD_DIM)
    )
    inside = jnp.arange(TOK, dtype=jnp.int32)
    blocks = y * NEAR + jnp.bitwise_xor(near, jnp.arange(NEAR, dtype=jnp.int32))
    positions = (blocks[:, None] * TOK + inside[None, :]).astype(F32)
    angles = frequency[None, :, None] * positions[:, None, :]
    cosq, sinq = jnp.cos(angles), jnp.sin(angles)
    doubled = jnp.concatenate([frequency, frequency])[None, :]
    within = inside.astype(F32)[:, None] * doubled
    starts = ((jnp.arange(RINGS, dtype=jnp.int32) * NEAR + near) * TOK).astype(F32)
    across = starts[:, None] * doubled
    mine = positions[0][:, None] * frequency[None, :]
    cosk, sink = jnp.cos(mine), jnp.sin(mine)

    far = swap(pack, 2)
    pack_later, cosq = lax.optimization_barrier((pack, cosq))
    packs = [pack, swap(pack_later, 1), far, swap(far, 1)]

    dkv, dq_own, dq_far, dq_near = attend(
        kv, packs, cosq, sinq, jnp.cos(within), jnp.sin(within), jnp.cos(across), jnp.sin(across)
    )

    got = lax.all_to_all(dkv, "y", split_axis=0, concat_axis=0, tiled=True)
    near_back = swap(dq_near, 1)
    far_sum = pl.pallas_call(
        add_kernel,
        out_shape=jax.ShapeDtypeStruct((HEAD_DIM, LANES), BF16),
        compiler_params=params,
    )(dq_far, near_back)
    far_back = swap(far_sum, 2)

    team = lax.axis_size("outer") * NEAR
    bias_copies = pl.pallas_call(
        bias_kernel,
        grid=(1,),
        in_specs=[
            pl.BlockSpec((RINGS, META, 2 * HEAD_DIM), lambda i: (0, TOK // META, 0)),
            anywhere,
        ],
        out_specs=pl.BlockSpec((team, 2, BIAS_COLS * HEAD_DIM), lambda i: (0, 0, 0)),
        out_shape=jax.ShapeDtypeStruct((team, 2, BIAS_COLS * HEAD_DIM), BF16),
        compiler_params=params,
    )(got, far_back)
    biases = lax.all_to_all(
        bias_copies, ("outer",) + near_axes, split_axis=0, concat_axis=0, tiled=True
    )

    dq, dk, dv = pl.pallas_call(
        finish_kernel,
        out_shape=[
            jax.ShapeDtypeStruct((TOK, WIDTH), BF16),
            jax.ShapeDtypeStruct((TOK, HEAD_DIM), BF16),
            jax.ShapeDtypeStruct((TOK, HEAD_DIM), BF16),
        ],
        compiler_params=params,
    )(got, dq_own, near_back, far_back, cosk, sink)

    grad_bias = pl.pallas_call(
        bias_sum_kernel,
        out_shape=jax.ShapeDtypeStruct((HEADS + 2 * KV_HEADS, HEAD_DIM), F32),
        compiler_params=params,
    )(biases).reshape(-1)
    return dq[None], dk[None], dv[None], grad_bias


def solution(mesh):
    fine = Mesh(mesh.devices.reshape(-1, RINGS, 2, 2), ("outer", "y", "xh", "core"))
    inner = ("y", "xh", "core")
    rows = P("outer", inner, None)
    placed = (
        rows,
        rows,
        rows,
        rows,
        rows,
        P("outer", None, inner),
        P(None, inner),
        P(None, inner, None),
    )
    return jax.shard_map(
        local, mesh=fine, in_specs=placed, out_specs=(rows, rows, rows, P()), check_vma=False
    )
```

```python
import math

import jax
import jax.numpy as jnp
from jax import lax
from jax.experimental import pallas as pl
from jax.experimental.pallas import tpu as pltpu
from jax.sharding import Mesh, PartitionSpec as P

HEADS = 28
KV_HEADS = 4
HEAD_DIM = 128
GROUP = HEADS // KV_HEADS
TOK = 128
ROPE_BASE = 1000000.0
HALF = HEAD_DIM // 2
SCALE = HEAD_DIM ** (-0.5)
LOG2E = math.log2(math.e)

RINGS = 8
NEAR = 4
BPC = 8
META = 8
LANES = GROUP * TOK
WIDTH = GROUP * HEAD_DIM
HEADSETS = [(0, 2), (2, 4), (4, 6), (6, 7)]
PACK = 2 * LANES + 48
BIAS_ROWS = GROUP + 2
BIAS_COLS = 5

F32 = jnp.float32
BF16 = jnp.bfloat16


def split(value, terms):
    parts = []
    for _ in range(terms):
        part = value.astype(BF16)
        parts.append(part)
        value = value - part.astype(F32)
    return parts


def pack_keys_kernel(seg_ref, k_ref, v_ref, kv_ref, row_ref, own, segs, sems):
    loads = [
        pltpu.make_async_copy(seg_ref, segs, sems.at[2 + RINGS]),
        pltpu.make_async_copy(k_ref, own.at[pl.ds(0, TOK), pl.ds(0, HEAD_DIM)], sems.at[0]),
        pltpu.make_async_copy(v_ref, own.at[pl.ds(0, TOK), pl.ds(HEAD_DIM, HEAD_DIM)], sems.at[1]),
    ]
    for copy in loads:
        copy.start()
    loads[0].wait()
    seg = segs[pl.ds(lax.axis_index("outer") // KV_HEADS, 1), :]
    row_ref[...] = seg
    row = lax.broadcasted_iota(jnp.int32, (META, 2 * HEAD_DIM), 0)
    prompt = jnp.sum(jnp.where(seg == 0, 1.0, 0.0))
    chosen = jnp.sum(jnp.where(seg <= 1, 1.0, 0.0))
    own[TOK:, :] = jnp.where(row == 0, prompt, jnp.where(row == 1, chosen, 0.0)).astype(BF16)
    for copy in loads[1:]:
        copy.wait()
    stores = [pltpu.make_async_copy(own, kv_ref.at[y], sems.at[2 + y]) for y in range(RINGS)]
    for copy in stores:
        copy.start()
    for copy in stores:
        copy.wait()


def pack_queries_kernel(q_ref, go_ref, ao_ref, norm_ref, seg_ref, unused_ref, pack_ref, ao_own, sems):
    copies = []
    for g in range(GROUP):
        here = slice(g * HEAD_DIM, (g + 1) * HEAD_DIM)
        rows = pl.ds(g * TOK, TOK)
        far_rows = pl.ds(LANES + g * TOK, TOK)
        trio = [
            pltpu.make_async_copy(go_ref.at[:, here], pack_ref.at[far_rows, :], sems.at[0, g]),
            pltpu.make_async_copy(ao_ref.at[:, here], ao_own.at[rows, :], sems.at[1, g]),
            pltpu.make_async_copy(q_ref.at[:, here], pack_ref.at[rows, :], sems.at[2, g]),
        ]
        for copy in trio:
            copy.start()
        copies.append(trio)
    seg = seg_ref[...]
    zero = jnp.zeros((1, TOK), F32)
    eight = lambda rows: jnp.concatenate(rows + [zero] * (8 - len(rows)), axis=0)
    norms = norm_ref[...] * LOG2E
    parts = split(eight([norms[g : g + 1, :] for g in range(GROUP)] + [seg.astype(F32)]), 3)
    deltas = []
    for g in range(GROUP):
        copies[g][0].wait()
        copies[g][1].wait()
        go = pack_ref[LANES + g * TOK : LANES + (g + 1) * TOK, :]
        product = go.astype(F32) * ao_own[g * TOK : (g + 1) * TOK, :].astype(F32)
        deltas.append(jnp.sum(product.T, axis=0, keepdims=True))
    parts += split(eight(deltas), 3)
    rows = jnp.concatenate([part.astype(F32) for part in parts], axis=0)
    pack_ref[2 * LANES :, :] = rows.astype(BF16)
    for g in range(GROUP):
        copies[g][2].wait()


def attention_kernel(
    kv_ref, pack0, pack1, pack2, pack3, cosq_ref, sinq_ref, cosr_ref, sinr_ref, cosc_ref, sinc_ref,
    dkv_ref, dq0, dq2, dq_near,
    pack, kv_acc, turned_sum, counts,
):
    part = pl.program_id(0)
    rows_in = BPC * TOK
    contract = (((1,), (1,)), ((), ()))

    @pl.when(part == 0)
    def _():
        for y in range(RINGS):
            meta = kv_ref[y, TOK:, :].astype(F32)
            counts[0, y] = jnp.max(meta[0:1, :]).astype(jnp.int32)
            counts[1, y] = jnp.max(meta[1:2, :]).astype(jnp.int32)
        turned_sum[...] = jnp.zeros_like(turned_sum)
        kv_acc[...] = jnp.zeros_like(kv_acc)

    for c, source in enumerate((pack0, pack1, pack2, pack3)):

        @pl.when(part == c)
        def _(source=source):
            pack[...] = source[...]

    extra = pack[2 * LANES :, :].astype(F32)
    norms = extra[0:8] + extra[8:16] + extra[16:24]
    deltas = extra[24:32] + extra[32:40] + extra[40:48]
    seg = norms[GROUP : GROUP + 1, :].astype(jnp.int32)
    across = lambda rows, g0, g1: jnp.concatenate([rows[g : g + 1, :] for g in range(g0, g1)], axis=1)
    at = lax.broadcasted_iota(jnp.int32, (TOK, TOK), 0)
    dq = jnp.zeros((HEAD_DIM, LANES), F32)
    for k in range(RINGS // BPC):
        blocks = pl.ds(k * BPC, BPC)
        keys = kv_ref[blocks, :TOK, :HEAD_DIM].reshape(rows_in, HEAD_DIM)
        values = kv_ref[blocks, :TOK, HEAD_DIM:].reshape(rows_in, HEAD_DIM)
        allowed = []
        for b in range(k * BPC, (k + 1) * BPC):
            c0, c1 = counts[0, b], counts[1, b]
            below = jnp.where(seg == 1, c1, c0)
            above = jnp.where(seg == 2, c1, TOK)
            allowed.append((at < below) | (at >= above))
        allowed = jnp.concatenate(allowed, axis=0)
        probs_low = []
        scores_low = []
        for g0, g1 in HEADSETS:
            there = slice(g0 * TOK, g1 * TOK)
            near = slice(LANES + g0 * TOK, LANES + g1 * TOK)
            scores = lax.dot_general(keys, pack[there, :], contract, preferred_element_type=F32)
            probs = jnp.exp2(scores * (SCALE * LOG2E) - across(norms, g0, g1))
            probs = jnp.where(jnp.concatenate([allowed] * (g1 - g0), axis=1), probs, 0.0)
            grad_probs = lax.dot_general(values, pack[near, :], contract, preferred_element_type=F32)
            scores_low.append((probs * (grad_probs - across(deltas, g0, g1))).astype(BF16))
            probs_low.append(probs.astype(BF16))
        scores_low = jnp.concatenate(scores_low, axis=1)
        probs_low = jnp.concatenate(probs_low, axis=1)
        dv = jnp.dot(probs_low, pack[LANES : 2 * LANES, :], preferred_element_type=F32)
        dk = jnp.dot(scores_low, pack[:LANES, :], preferred_element_type=F32)
        kv_acc[k * rows_in : (k + 1) * rows_in, :HEAD_DIM] += dk
        kv_acc[k * rows_in : (k + 1) * rows_in, HEAD_DIM:] += dv
        dq += jnp.dot(keys.T, scores_low, preferred_element_type=F32)

    cosine = jnp.concatenate([cosq_ref[part]] * GROUP, axis=1) * SCALE
    sine = jnp.concatenate([sinq_ref[part]] * GROUP, axis=1) * SCALE
    upper, lower = dq[:HALF], dq[HALF:]
    turned = jnp.concatenate(
        [upper * cosine + lower * sine, lower * cosine - upper * sine], axis=0
    )
    turned_sum[...] += turned
    for c, out in enumerate((dq0, dq_near.at[0], dq2, dq_near.at[1])):

        @pl.when(part == c)
        def _(out=out):
            out[...] = turned.astype(out.dtype)

    @pl.when(part == NEAR - 1)
    def _():
        u_all = jnp.zeros((1, HEAD_DIM), F32)
        w_all = jnp.zeros((1, HEAD_DIM), F32)
        v_all = jnp.zeros((1, HEAD_DIM), F32)
        for b in range(RINGS):
            total = kv_acc[b * TOK : (b + 1) * TOK, :]
            dkv_ref[b, :TOK, :] = total.astype(BF16)
            dk = total[:, :HEAD_DIM]
            u = jnp.sum(dk * cosr_ref[...], axis=0, keepdims=True)
            w = jnp.sum(dk * sinr_ref[...], axis=0, keepdims=True)
            c = cosc_ref[b : b + 1, :]
            s = sinc_ref[b : b + 1, :]
            u_all += u * c - w * s
            w_all += u * s + w * c
            v_all += jnp.sum(total[:, HEAD_DIM:], axis=0, keepdims=True)
        rows = []
        for g in range(GROUP):
            rows.append(jnp.sum(turned_sum[:, g * TOK : (g + 1) * TOK].T, axis=0, keepdims=True))
        u = u_all * SCALE
        w = w_all * SCALE
        rows.append(u + jnp.concatenate([w[:, HALF:], -w[:, :HALF]], axis=1))
        rows.append(v_all)
        spare = jnp.concatenate(rows[META:] + [jnp.zeros((2 * META - BIAS_ROWS, HEAD_DIM), F32)], axis=0)
        both = jnp.concatenate([jnp.concatenate(rows[:META], axis=0), spare], axis=1).astype(BF16)
        for y in range(RINGS):
            dkv_ref[y, TOK:, :] = both


def attend(kv, packs, cosq, sinq, cosr, sinr, cosc, sinc):
    vmem = pl.BlockSpec(memory_space=pltpu.VMEM)
    return pl.pallas_call(
        attention_kernel,
        grid=(NEAR,),
        in_specs=[vmem] * 11,
        out_specs=[vmem] + [pl.BlockSpec((HEAD_DIM, LANES), lambda i: (0, 0))] * 2 + [vmem],
        out_shape=[
            jax.ShapeDtypeStruct((RINGS, TOK + META, 2 * HEAD_DIM), BF16),
            pltpu.HBM((HEAD_DIM, LANES), F32),
            pltpu.HBM((HEAD_DIM, LANES), F32),
            jax.ShapeDtypeStruct((2, HEAD_DIM, LANES), BF16),
        ],
        scratch_shapes=[
            pltpu.VMEM((PACK, TOK), BF16),
            pltpu.VMEM((RINGS * TOK, 2 * HEAD_DIM), F32),
            pltpu.VMEM((HEAD_DIM, LANES), F32),
            pltpu.SMEM((2, RINGS), jnp.int32),
        ],
        compiler_params=pltpu.CompilerParams(vmem_limit_bytes=24 << 20),
    )(kv, *packs, cosq, sinq, cosr, sinr, cosc, sinc)


def bias_kernel(got_ref, unused_ref, out_ref):
    total = jnp.sum(got_ref[...].astype(F32), axis=0)
    total = jnp.concatenate([total[:, :HEAD_DIM], total[:, HEAD_DIM:]], axis=0)
    rows = [total[r : r + 1, :] for r in range(BIAS_ROWS)]
    rows.append(jnp.zeros((1, HEAD_DIM), F32))
    pair = jnp.concatenate(
        [
            jnp.concatenate(rows[:BIAS_COLS], axis=1),
            jnp.concatenate(rows[BIAS_COLS:], axis=1),
        ],
        axis=0,
    )
    out_ref[...] = jnp.broadcast_to(pair.astype(BF16)[None], out_ref.shape)


def bias_sum_kernel(got_ref, out_ref):
    pairs = got_ref.shape[0] // NEAR
    for c in range(KV_HEADS):
        total = None
        for row in range(c, pairs, KV_HEADS):
            part = jnp.sum(got_ref[row * NEAR : (row + 1) * NEAR].astype(F32), axis=0)
            total = part if total is None else total + part
        for r in range(BIAS_ROWS):
            at = c * GROUP + r if r < GROUP else HEADS + (r - GROUP) * KV_HEADS + c
            i, j = r // BIAS_COLS, r % BIAS_COLS
            out_ref[at : at + 1, :] = total[i : i + 1, j * HEAD_DIM : (j + 1) * HEAD_DIM]


def add_kernel(far_ref, near_ref, out_ref):
    out_ref[...] = (far_ref[...] + near_ref[1].astype(F32)).astype(BF16)


def finish_kernel(got_ref, dq_own, dq_near, dq_far, cosk_ref, sink_ref, dq_ref, dk_ref, dv_ref):
    total = jnp.sum(got_ref[:, :TOK, :].astype(F32), axis=0)
    dv_ref[...] = total[:, HEAD_DIM:].astype(BF16)
    a = total[:, :HALF] * SCALE
    b = total[:, HALF:HEAD_DIM] * SCALE
    cosine = cosk_ref[...]
    sine = sink_ref[...]
    dk_ref[...] = jnp.concatenate([a * cosine + b * sine, b * cosine - a * sine], axis=1).astype(BF16)
    for g in range(GROUP):
        there = slice(g * TOK, (g + 1) * TOK)
        value = dq_own[:, there] + (dq_near[0, :, there].astype(F32) + dq_far[:, there].astype(F32))
        dq_ref[:, g * HEAD_DIM : (g + 1) * HEAD_DIM] = value.T.astype(BF16)


def local(query_rot, key_rot, value_rows, attention_out, grad_out, log_norm, segments, block_table):
    near_axes = ("xh", "core")
    y = lax.axis_index("y")
    near = lax.axis_index(near_axes)
    params = pltpu.CompilerParams(vmem_limit_bytes=8 << 20)

    vmem = pl.BlockSpec(memory_space=pltpu.VMEM)
    hbm = pl.BlockSpec(memory_space=pltpu.HBM)
    anywhere = pl.BlockSpec(memory_space=pl.ANY)
    kv_copies, seg = pl.pallas_call(
        pack_keys_kernel,
        in_specs=[hbm, hbm, hbm],
        out_specs=[hbm, vmem],
        out_shape=[
            pltpu.HBM((RINGS, TOK + META, 2 * HEAD_DIM), BF16),
            jax.ShapeDtypeStruct((1, TOK), jnp.int32),
        ],
        scratch_shapes=[
            pltpu.VMEM((TOK + META, 2 * HEAD_DIM), BF16),
            pltpu.VMEM(segments.shape, jnp.int32),
            pltpu.SemaphoreType.DMA((3 + RINGS,)),
        ],
        compiler_params=params,
    )(
        pltpu.with_memory_space_constraint(segments, pltpu.HBM),
        pltpu.with_memory_space_constraint(key_rot[0], pltpu.HBM),
        pltpu.with_memory_space_constraint(value_rows[0], pltpu.HBM),
    )
    kv = lax.all_to_all(kv_copies, "y", split_axis=0, concat_axis=0, tiled=True)
    pack = pl.pallas_call(
        pack_queries_kernel,
        in_specs=[hbm, hbm, hbm, vmem, vmem, anywhere],
        out_shape=jax.ShapeDtypeStruct((PACK, TOK), BF16),
        scratch_shapes=[pltpu.VMEM((LANES, TOK), BF16), pltpu.SemaphoreType.DMA((3, GROUP))],
        compiler_params=params,
    )(query_rot[0], grad_out[0], attention_out[0], log_norm[0], seg, pltpu.with_memory_space_constraint(kv_copies, pltpu.HBM))

    def swap(value, bits):
        return lax.ppermute(value, near_axes, [(i, i ^ bits) for i in range(NEAR)])

    frequency = jnp.exp(
        jnp.arange(HALF, dtype=F32) * (-2.0 * math.log(ROPE_BASE) / HEAD_DIM)
    )
    inside = jnp.arange(TOK, dtype=jnp.int32)
    blocks = y * NEAR + jnp.bitwise_xor(near, jnp.arange(NEAR, dtype=jnp.int32))
    positions = (blocks[:, None] * TOK + inside[None, :]).astype(F32)
    angles = frequency[None, :, None] * positions[:, None, :]
    cosq, sinq = jnp.cos(angles), jnp.sin(angles)
    doubled = jnp.concatenate([frequency, frequency])[None, :]
    within = inside.astype(F32)[:, None] * doubled
    starts = ((jnp.arange(RINGS, dtype=jnp.int32) * NEAR + near) * TOK).astype(F32)
    across = starts[:, None] * doubled
    mine = positions[0][:, None] * frequency[None, :]
    cosk, sink = jnp.cos(mine), jnp.sin(mine)

    far = swap(pack, 2)
    pack_later, cosq = lax.optimization_barrier((pack, cosq))
    packs = [pack, swap(pack_later, 1), far, swap(far, 1)]

    dkv, dq_own, dq_far, dq_near = attend(
        kv, packs, cosq, sinq, jnp.cos(within), jnp.sin(within), jnp.cos(across), jnp.sin(across)
    )

    got = lax.all_to_all(dkv, "y", split_axis=0, concat_axis=0, tiled=True)
    near_back = swap(dq_near, 1)
    far_sum = pl.pallas_call(
        add_kernel,
        out_shape=jax.ShapeDtypeStruct((HEAD_DIM, LANES), BF16),
        compiler_params=params,
    )(dq_far, near_back)
    far_back = swap(far_sum, 2)

    team = lax.axis_size("outer") * NEAR
    bias_copies = pl.pallas_call(
        bias_kernel,
        grid=(1,),
        in_specs=[
            pl.BlockSpec((RINGS, META, 2 * HEAD_DIM), lambda i: (0, TOK // META, 0)),
            anywhere,
        ],
        out_specs=pl.BlockSpec((team, 2, BIAS_COLS * HEAD_DIM), lambda i: (0, 0, 0)),
        out_shape=jax.ShapeDtypeStruct((team, 2, BIAS_COLS * HEAD_DIM), BF16),
        compiler_params=params,
    )(got, far_back)
    biases = lax.all_to_all(
        bias_copies, ("outer",) + near_axes, split_axis=0, concat_axis=0, tiled=True
    )

    dq, dk, dv = pl.pallas_call(
        finish_kernel,
        out_shape=[
            jax.ShapeDtypeStruct((TOK, WIDTH), BF16),
            jax.ShapeDtypeStruct((TOK, HEAD_DIM), BF16),
            jax.ShapeDtypeStruct((TOK, HEAD_DIM), BF16),
        ],
        compiler_params=params,
    )(got, dq_own, near_back, far_back, cosk, sink)

    grad_bias = pl.pallas_call(
        bias_sum_kernel,
        out_shape=jax.ShapeDtypeStruct((HEADS + 2 * KV_HEADS, HEAD_DIM), F32),
        compiler_params=params,
    )(biases).reshape(-1)
    return dq[None], dk[None], dv[None], grad_bias


def solution(mesh):
    fine = Mesh(mesh.devices.reshape(-1, RINGS, 2, 2), ("outer", "y", "xh", "core"))
    inner = ("y", "xh", "core")
    rows = P("outer", inner, None)
    placed = (
        rows,
        rows,
        rows,
        rows,
        rows,
        P("outer", None, inner),
        P(None, inner),
        P(None, inner, None),
    )
    return jax.shard_map(
        local, mesh=fine, in_specs=placed, out_specs=(rows, rows, rows, P()), check_vma=False
    )
```

```python
import math

import jax
import jax.numpy as jnp
from jax import lax
from jax.experimental import pallas as pl
from jax.experimental.pallas import tpu as pltpu
from jax.sharding import Mesh, PartitionSpec as P

HEADS = 28
KV_HEADS = 4
HEAD_DIM = 128
GROUP = HEADS // KV_HEADS
TOK = 128
ROPE_BASE = 1000000.0
HALF = HEAD_DIM // 2
SCALE = HEAD_DIM ** (-0.5)
LOG2E = math.log2(math.e)

RINGS = 8
NEAR = 4
BPC = 8
META = 8
LANES = GROUP * TOK
WIDTH = GROUP * HEAD_DIM
HEADSETS = [(0, 2), (2, 4), (4, 6), (6, 7)]
PACK = 2 * LANES + 48
BIAS_ROWS = GROUP + 2
BIAS_COLS = 5

F32 = jnp.float32
BF16 = jnp.bfloat16


def split(value, terms):
    parts = []
    for _ in range(terms):
        part = value.astype(BF16)
        parts.append(part)
        value = value - part.astype(F32)
    return parts


def pack_keys_kernel(seg_ref, k_ref, v_ref, kv_ref, row_ref, own, meta, segs, sems):
    loads = [
        pltpu.make_async_copy(seg_ref, segs, sems.at[2 + RINGS]),
        pltpu.make_async_copy(k_ref, own.at[pl.ds(0, TOK), pl.ds(0, HEAD_DIM)], sems.at[0]),
        pltpu.make_async_copy(v_ref, own.at[pl.ds(0, TOK), pl.ds(HEAD_DIM, HEAD_DIM)], sems.at[1]),
    ]
    for copy in loads:
        copy.start()
    stores = []
    for copy in loads[1:]:
        copy.wait()
    for y in range(RINGS):
        stores.append(pltpu.make_async_copy(own, kv_ref.at[y, pl.ds(0, TOK), :], sems.at[2 + y]))
        stores[-1].start()
    loads[0].wait()
    seg = segs[pl.ds(lax.axis_index("outer") // KV_HEADS, 1), :]
    row_ref[...] = seg
    row = lax.broadcasted_iota(jnp.int32, (META, 2 * HEAD_DIM), 0)
    prompt = jnp.sum(jnp.where(seg == 0, 1.0, 0.0), axis=1, keepdims=True)
    chosen = jnp.sum(jnp.where(seg <= 1, 1.0, 0.0), axis=1, keepdims=True)
    meta[...] = jnp.where(row == 0, prompt, jnp.where(row == 1, chosen, 0.0)).astype(BF16)
    for y in range(RINGS):
        there = kv_ref.at[y, pl.ds(TOK, META), :]
        stores.append(pltpu.make_async_copy(meta, there, sems.at[3 + RINGS + y]))
        stores[-1].start()
    for copy in stores:
        copy.wait()


def pack_queries_kernel(q_ref, go_ref, ao_ref, norm_ref, seg_ref, unused_ref, pack_ref, ao_own, sems):
    copies = []
    for g in range(GROUP):
        here = slice(g * HEAD_DIM, (g + 1) * HEAD_DIM)
        rows = pl.ds(g * TOK, TOK)
        far_rows = pl.ds(LANES + g * TOK, TOK)
        trio = [
            pltpu.make_async_copy(go_ref.at[:, here], pack_ref.at[far_rows, :], sems.at[0, g]),
            pltpu.make_async_copy(ao_ref.at[:, here], ao_own.at[rows, :], sems.at[1, g]),
            pltpu.make_async_copy(q_ref.at[:, here], pack_ref.at[rows, :], sems.at[2, g]),
        ]
        for copy in trio:
            copy.start()
        copies.append(trio)
    seg = seg_ref[...]
    zero = jnp.zeros((1, TOK), F32)
    eight = lambda rows: jnp.concatenate(rows + [zero] * (8 - len(rows)), axis=0)
    norms = norm_ref[...] * LOG2E
    parts = split(eight([norms[g : g + 1, :] for g in range(GROUP)] + [seg.astype(F32)]), 3)
    deltas = []
    for g in range(GROUP):
        copies[g][0].wait()
        copies[g][1].wait()
        go = pack_ref[LANES + g * TOK : LANES + (g + 1) * TOK, :]
        product = go.astype(F32) * ao_own[g * TOK : (g + 1) * TOK, :].astype(F32)
        deltas.append(jnp.sum(product.T, axis=0, keepdims=True))
    parts += split(eight(deltas), 3)
    rows = jnp.concatenate([part.astype(F32) for part in parts], axis=0)
    pack_ref[2 * LANES :, :] = rows.astype(BF16)
    for g in range(GROUP):
        copies[g][2].wait()


def attention_kernel(
    kv_ref, pack0, pack1, pack2, pack3, cosq_ref, sinq_ref, cosr_ref, sinr_ref, cosc_ref, sinc_ref,
    dkv_ref, dq0, dq2, dq_near,
    pack, kv_acc, turned_sum, counts,
):
    part = pl.program_id(0)
    rows_in = BPC * TOK
    contract = (((1,), (1,)), ((), ()))

    @pl.when(part == 0)
    def _():
        for y in range(RINGS):
            meta = kv_ref[y, TOK:, :].astype(F32)
            counts[0, y] = jnp.max(meta[0:1, :]).astype(jnp.int32)
            counts[1, y] = jnp.max(meta[1:2, :]).astype(jnp.int32)
        turned_sum[...] = jnp.zeros_like(turned_sum)
        kv_acc[...] = jnp.zeros_like(kv_acc)

    for c, source in enumerate((pack0, pack1, pack2, pack3)):

        @pl.when(part == c)
        def _(source=source):
            pack[...] = source[...]

    extra = pack[2 * LANES :, :].astype(F32)
    norms = extra[0:8] + extra[8:16] + extra[16:24]
    deltas = extra[24:32] + extra[32:40] + extra[40:48]
    seg = norms[GROUP : GROUP + 1, :].astype(jnp.int32)
    across = lambda rows, g0, g1: jnp.concatenate([rows[g : g + 1, :] for g in range(g0, g1)], axis=1)
    at = lax.broadcasted_iota(jnp.int32, (TOK, TOK), 0)
    dq = jnp.zeros((HEAD_DIM, LANES), F32)
    for k in range(RINGS // BPC):
        blocks = pl.ds(k * BPC, BPC)
        keys = kv_ref[blocks, :TOK, :HEAD_DIM].reshape(rows_in, HEAD_DIM)
        values = kv_ref[blocks, :TOK, HEAD_DIM:].reshape(rows_in, HEAD_DIM)
        allowed = []
        for b in range(k * BPC, (k + 1) * BPC):
            c0, c1 = counts[0, b], counts[1, b]
            below = jnp.where(seg == 1, c1, c0)
            above = jnp.where(seg == 2, c1, TOK)
            allowed.append((at < below) | (at >= above))
        allowed = jnp.concatenate(allowed, axis=0)
        probs_low = []
        scores_low = []
        for g0, g1 in HEADSETS:
            there = slice(g0 * TOK, g1 * TOK)
            near = slice(LANES + g0 * TOK, LANES + g1 * TOK)
            scores = lax.dot_general(keys, pack[there, :], contract, preferred_element_type=F32)
            probs = jnp.exp2(scores * (SCALE * LOG2E) - across(norms, g0, g1))
            probs = jnp.where(jnp.concatenate([allowed] * (g1 - g0), axis=1), probs, 0.0)
            grad_probs = lax.dot_general(values, pack[near, :], contract, preferred_element_type=F32)
            scores_low.append((probs * (grad_probs - across(deltas, g0, g1))).astype(BF16))
            probs_low.append(probs.astype(BF16))
        scores_low = jnp.concatenate(scores_low, axis=1)
        probs_low = jnp.concatenate(probs_low, axis=1)
        dv = jnp.dot(probs_low, pack[LANES : 2 * LANES, :], preferred_element_type=F32)
        dk = jnp.dot(scores_low, pack[:LANES, :], preferred_element_type=F32)
        kv_acc[k * rows_in : (k + 1) * rows_in, :HEAD_DIM] += dk
        kv_acc[k * rows_in : (k + 1) * rows_in, HEAD_DIM:] += dv
        dq += jnp.dot(keys.T, scores_low, preferred_element_type=F32)

    cosine = jnp.concatenate([cosq_ref[part]] * GROUP, axis=1) * SCALE
    sine = jnp.concatenate([sinq_ref[part]] * GROUP, axis=1) * SCALE
    upper, lower = dq[:HALF], dq[HALF:]
    turned = jnp.concatenate(
        [upper * cosine + lower * sine, lower * cosine - upper * sine], axis=0
    )
    turned_sum[...] += turned
    for c, out in enumerate((dq0, dq_near.at[0], dq2, dq_near.at[1])):

        @pl.when(part == c)
        def _(out=out):
            out[...] = turned.astype(out.dtype)

    @pl.when(part == NEAR - 1)
    def _():
        u_all = jnp.zeros((1, HEAD_DIM), F32)
        w_all = jnp.zeros((1, HEAD_DIM), F32)
        v_all = jnp.zeros((1, HEAD_DIM), F32)
        for b in range(RINGS):
            total = kv_acc[b * TOK : (b + 1) * TOK, :]
            dkv_ref[b, :TOK, :] = total.astype(BF16)
            dk = total[:, :HEAD_DIM]
            u = jnp.sum(dk * cosr_ref[...], axis=0, keepdims=True)
            w = jnp.sum(dk * sinr_ref[...], axis=0, keepdims=True)
            c = cosc_ref[b : b + 1, :]
            s = sinc_ref[b : b + 1, :]
            u_all += u * c - w * s
            w_all += u * s + w * c
            v_all += jnp.sum(total[:, HEAD_DIM:], axis=0, keepdims=True)
        rows = []
        for g in range(GROUP):
            rows.append(jnp.sum(turned_sum[:, g * TOK : (g + 1) * TOK].T, axis=0, keepdims=True))
        u = u_all * SCALE
        w = w_all * SCALE
        rows.append(u + jnp.concatenate([w[:, HALF:], -w[:, :HALF]], axis=1))
        rows.append(v_all)
        spare = jnp.concatenate(rows[META:] + [jnp.zeros((2 * META - BIAS_ROWS, HEAD_DIM), F32)], axis=0)
        both = jnp.concatenate([jnp.concatenate(rows[:META], axis=0), spare], axis=1).astype(BF16)
        for y in range(RINGS):
            dkv_ref[y, TOK:, :] = both


def attend(kv, packs, cosq, sinq, cosr, sinr, cosc, sinc):
    vmem = pl.BlockSpec(memory_space=pltpu.VMEM)
    return pl.pallas_call(
        attention_kernel,
        grid=(NEAR,),
        in_specs=[vmem] * 11,
        out_specs=[vmem] + [pl.BlockSpec((HEAD_DIM, LANES), lambda i: (0, 0))] * 2 + [vmem],
        out_shape=[
            jax.ShapeDtypeStruct((RINGS, TOK + META, 2 * HEAD_DIM), BF16),
            pltpu.HBM((HEAD_DIM, LANES), F32),
            pltpu.HBM((HEAD_DIM, LANES), F32),
            jax.ShapeDtypeStruct((2, HEAD_DIM, LANES), BF16),
        ],
        scratch_shapes=[
            pltpu.VMEM((PACK, TOK), BF16),
            pltpu.VMEM((RINGS * TOK, 2 * HEAD_DIM), F32),
            pltpu.VMEM((HEAD_DIM, LANES), F32),
            pltpu.SMEM((2, RINGS), jnp.int32),
        ],
        compiler_params=pltpu.CompilerParams(vmem_limit_bytes=24 << 20),
    )(kv, *packs, cosq, sinq, cosr, sinr, cosc, sinc)


def bias_kernel(got_ref, unused_ref, out_ref):
    total = jnp.sum(got_ref[...].astype(F32), axis=0)
    total = jnp.concatenate([total[:, :HEAD_DIM], total[:, HEAD_DIM:]], axis=0)
    rows = [total[r : r + 1, :] for r in range(BIAS_ROWS)]
    rows.append(jnp.zeros((1, HEAD_DIM), F32))
    pair = jnp.concatenate(
        [
            jnp.concatenate(rows[:BIAS_COLS], axis=1),
            jnp.concatenate(rows[BIAS_COLS:], axis=1),
        ],
        axis=0,
    )
    out_ref[...] = jnp.broadcast_to(pair.astype(BF16)[None], out_ref.shape)


def bias_sum_kernel(got_ref, out_ref):
    pairs = got_ref.shape[0] // NEAR
    for c in range(KV_HEADS):
        total = None
        for row in range(c, pairs, KV_HEADS):
            part = jnp.sum(got_ref[row * NEAR : (row + 1) * NEAR].astype(F32), axis=0)
            total = part if total is None else total + part
        for r in range(BIAS_ROWS):
            at = c * GROUP + r if r < GROUP else HEADS + (r - GROUP) * KV_HEADS + c
            i, j = r // BIAS_COLS, r % BIAS_COLS
            out_ref[at : at + 1, :] = total[i : i + 1, j * HEAD_DIM : (j + 1) * HEAD_DIM]


def add_kernel(far_ref, near_ref, out_ref):
    out_ref[...] = (far_ref[...] + near_ref[1].astype(F32)).astype(BF16)


def finish_kernel(got_ref, dq_own, dq_near, dq_far, cosk_ref, sink_ref, dq_ref, dk_ref, dv_ref):
    total = jnp.sum(got_ref[:, :TOK, :].astype(F32), axis=0)
    dv_ref[...] = total[:, HEAD_DIM:].astype(BF16)
    a = total[:, :HALF] * SCALE
    b = total[:, HALF:HEAD_DIM] * SCALE
    cosine = cosk_ref[...]
    sine = sink_ref[...]
    dk_ref[...] = jnp.concatenate([a * cosine + b * sine, b * cosine - a * sine], axis=1).astype(BF16)
    for g in range(GROUP):
        there = slice(g * TOK, (g + 1) * TOK)
        value = dq_own[:, there] + (dq_near[0, :, there].astype(F32) + dq_far[:, there].astype(F32))
        dq_ref[:, g * HEAD_DIM : (g + 1) * HEAD_DIM] = value.T.astype(BF16)


def local(query_rot, key_rot, value_rows, attention_out, grad_out, log_norm, segments, block_table):
    near_axes = ("xh", "core")
    y = lax.axis_index("y")
    near = lax.axis_index(near_axes)
    params = pltpu.CompilerParams(vmem_limit_bytes=8 << 20)

    vmem = pl.BlockSpec(memory_space=pltpu.VMEM)
    hbm = pl.BlockSpec(memory_space=pltpu.HBM)
    anywhere = pl.BlockSpec(memory_space=pl.ANY)
    kv_copies, seg = pl.pallas_call(
        pack_keys_kernel,
        in_specs=[hbm, hbm, hbm],
        out_specs=[hbm, vmem],
        out_shape=[
            pltpu.HBM((RINGS, TOK + META, 2 * HEAD_DIM), BF16),
            jax.ShapeDtypeStruct((1, TOK), jnp.int32),
        ],
        scratch_shapes=[
            pltpu.VMEM((TOK, 2 * HEAD_DIM), BF16),
            pltpu.VMEM((META, 2 * HEAD_DIM), BF16),
            pltpu.VMEM(segments.shape, jnp.int32),
            pltpu.SemaphoreType.DMA((3 + 2 * RINGS,)),
        ],
        compiler_params=params,
    )(
        pltpu.with_memory_space_constraint(segments, pltpu.HBM),
        pltpu.with_memory_space_constraint(key_rot[0], pltpu.HBM),
        pltpu.with_memory_space_constraint(value_rows[0], pltpu.HBM),
    )
    kv = lax.all_to_all(kv_copies, "y", split_axis=0, concat_axis=0, tiled=True)
    pack = pl.pallas_call(
        pack_queries_kernel,
        in_specs=[hbm, hbm, hbm, vmem, vmem, anywhere],
        out_shape=jax.ShapeDtypeStruct((PACK, TOK), BF16),
        scratch_shapes=[pltpu.VMEM((LANES, TOK), BF16), pltpu.SemaphoreType.DMA((3, GROUP))],
        compiler_params=params,
    )(query_rot[0], grad_out[0], attention_out[0], log_norm[0], seg, pltpu.with_memory_space_constraint(kv_copies, pltpu.HBM))

    def swap(value, bits):
        return lax.ppermute(value, near_axes, [(i, i ^ bits) for i in range(NEAR)])

    frequency = jnp.exp(
        jnp.arange(HALF, dtype=F32) * (-2.0 * math.log(ROPE_BASE) / HEAD_DIM)
    )
    inside = jnp.arange(TOK, dtype=jnp.int32)
    blocks = y * NEAR + jnp.bitwise_xor(near, jnp.arange(NEAR, dtype=jnp.int32))
    positions = (blocks[:, None] * TOK + inside[None, :]).astype(F32)
    angles = frequency[None, :, None] * positions[:, None, :]
    cosq, sinq = jnp.cos(angles), jnp.sin(angles)
    doubled = jnp.concatenate([frequency, frequency])[None, :]
    within = inside.astype(F32)[:, None] * doubled
    starts = ((jnp.arange(RINGS, dtype=jnp.int32) * NEAR + near) * TOK).astype(F32)
    across = starts[:, None] * doubled
    mine = positions[0][:, None] * frequency[None, :]
    cosk, sink = jnp.cos(mine), jnp.sin(mine)

    far = swap(pack, 2)
    pack_later, cosq = lax.optimization_barrier((pack, cosq))
    packs = [pack, swap(pack_later, 1), far, swap(far, 1)]

    dkv, dq_own, dq_far, dq_near = attend(
        kv, packs, cosq, sinq, jnp.cos(within), jnp.sin(within), jnp.cos(across), jnp.sin(across)
    )

    got = lax.all_to_all(dkv, "y", split_axis=0, concat_axis=0, tiled=True)
    near_back = swap(dq_near, 1)
    far_sum = pl.pallas_call(
        add_kernel,
        out_shape=jax.ShapeDtypeStruct((HEAD_DIM, LANES), BF16),
        compiler_params=params,
    )(dq_far, near_back)
    far_back = swap(far_sum, 2)

    team = lax.axis_size("outer") * NEAR
    bias_copies = pl.pallas_call(
        bias_kernel,
        grid=(1,),
        in_specs=[
            pl.BlockSpec((RINGS, META, 2 * HEAD_DIM), lambda i: (0, TOK // META, 0)),
            anywhere,
        ],
        out_specs=pl.BlockSpec((team, 2, BIAS_COLS * HEAD_DIM), lambda i: (0, 0, 0)),
        out_shape=jax.ShapeDtypeStruct((team, 2, BIAS_COLS * HEAD_DIM), BF16),
        compiler_params=params,
    )(got, far_back)
    biases = lax.all_to_all(
        bias_copies, ("outer",) + near_axes, split_axis=0, concat_axis=0, tiled=True
    )

    dq, dk, dv = pl.pallas_call(
        finish_kernel,
        out_shape=[
            jax.ShapeDtypeStruct((TOK, WIDTH), BF16),
            jax.ShapeDtypeStruct((TOK, HEAD_DIM), BF16),
            jax.ShapeDtypeStruct((TOK, HEAD_DIM), BF16),
        ],
        compiler_params=params,
    )(got, dq_own, near_back, far_back, cosk, sink)

    grad_bias = pl.pallas_call(
        bias_sum_kernel,
        out_shape=jax.ShapeDtypeStruct((HEADS + 2 * KV_HEADS, HEAD_DIM), F32),
        compiler_params=params,
    )(biases).reshape(-1)
    return dq[None], dk[None], dv[None], grad_bias


def solution(mesh):
    fine = Mesh(mesh.devices.reshape(-1, RINGS, 2, 2), ("outer", "y", "xh", "core"))
    inner = ("y", "xh", "core")
    rows = P("outer", inner, None)
    placed = (
        rows,
        rows,
        rows,
        rows,
        rows,
        P("outer", None, inner),
        P(None, inner),
        P(None, inner, None),
    )
    return jax.shard_map(
        local, mesh=fine, in_specs=placed, out_specs=(rows, rows, rows, P()), check_vma=False
    )
```
